256 devices in a mesh: req: 16 (over z, y_lo), blk: 16 (over x, y_hi, core).
Axes of the slice: x: 4, y: 4 (y_hi: 2, y_lo: 2; y = y_hi * 2 + y_lo), z: 8, core: 2. Of those that a mesh axis runs over, the one named last changes fastest.
Arguments:
- step_inputs: bfloat16 [2, 1024, 2560], P(None, 'req', 'blk'), may hold values from -6 to 6
- attention_gain: float32 [2560], replicated, may hold values from 0.25 to 1.75
- query_weight: bfloat16 [2560, 2560], P(None, 'blk'), may hold values from -0.3125 to 0.3125
- key_value_weight: bfloat16 [2560, 1024], P(None, 'blk'), may hold values from -0.125 to 0.125
- output_weight: bfloat16 [2560, 2560], P(None, 'blk'), may hold values from -0.125 to 0.125
- prompt_cache: bfloat16 [16, 48, 128, 1024], P('req', 'blk'), may hold values from -102 to 102
- page_table: int32 [16, 16, 3], P(None, 'blk'), may hold values from 0 to 2, each once within a row
- cache_lengths: int32 [16], replicated, may hold values from 1 to 6144, 49152 in all
- migration: int32 [16], replicated, may hold values from 0 to 15, each once
- parents: int32 [1, 1024], P(None, 'req'), may hold values from 0 to 7
- routes: int32 [2, 1024, 6], P(None, 'req'), may hold values from 0 to 63, all different within a row; in each aligned block of 64 rows (0 to 63, 64 to 127, ..., all dimensions but the last counted through in order) at most 16 rows name the same one
- feedforward_gain: float32 [2560], replicated, may hold values from 0.25 to 1.75
- router_weight: bfloat16 [2560, 64], replicated, may hold values from -0.125 to 0.125
- expert_gate: bfloat16 [256, 2560, 384], P(('req', 'blk')), may hold values from -0.125 to 0.125
- expert_up: bfloat16 [256, 2560, 384], P(('req', 'blk')), may hold values from -0.125 to 0.125
- expert_down: bfloat16 [256, 384, 2560], P(('req', 'blk')), may hold values from -0.15625 to 0.15625
- shared_gate: bfloat16 [2560, 3072], P(None, 'blk'), may hold values from -0.125 to 0.125
- shared_up: bfloat16 [2560, 3072], P(None, 'blk'), may hold values from -0.125 to 0.125
- shared_down: bfloat16 [3072, 2560], P('blk'), may hold values from -0.15625 to 0.15625
Outputs:
- layer_outputs: bfloat16 [2, 1024, 2560], P(None, 'req', 'blk')
The draws below stay inside these ranges and needn't reach their ends.
Inputs may be any that keep to these rules, and one draw needn't show every extreme that they name: `routes`: in each step the 64 rows of one device along req name any one expert at most 16 times. `migration`: A permutation of the slots. Each page_table[g, c] is a permutation.
All inputs are finite; a program needn't handle non-finite values.
Results may differ from the reference program's by a relative error of at most 0.018.
The reference program's roundings to bfloat16 on the way count: a program that leaves them out, or rounds other values in their place, can miss the bound.
Values may be sent and summed in bfloat16 or wider, within the bound.
No kernel may reach another device: no remote copies, remote signals or barrier semaphores. Data moves between devices by JAX's collectives and lax.ppermute only.
A program may use at most 128 MiB of HBM per device.

```python
import math
import jax
import jax.numpy as jnp
import numpy as np
from jax import lax

D = 2560
QUERY_HEADS = 20
KEY_VALUE_HEADS = 4
HEAD_WIDTH = 128
E = 64
FFE = 1536
TOPK = 6
SH = 3072
BEAMS = 8
STEPS = 2
PAGE = 128
CAP = 16
GR = 8
PROMPT_LIMIT = 6144
G = 16
ROWS_DEV = 64
BEAM_ROWS = 1024
KEY_VALUE_WIDTH = 1024
PAGES = 48
PAGE_COLS = 16
PAGES_LOC = 3
SPLIT = 4
FQ = 384
N_REQ = 16


def draw_prompt_cache(key, part):
    cache_shape = (G, PAGE_COLS * PAGES_LOC, PAGE, KEY_VALUE_WIDTH)
    normal_key = jax.random.fold_in(key, 0)
    values = jnp.clip(jax.random.normal(normal_key, cache_shape, jnp.float32), -6.0, 6.0)
    return values.astype(jnp.bfloat16)


def with_ends(drawn, key, smallest, top_value):
    extent = drawn.shape
    place = [jax.random.randint(jax.random.fold_in(key, axis), (), 0, extent[axis]) for axis in range(len(extent))]
    drawn = drawn.at[tuple(place)].set(smallest)
    longest = extent.index(max(extent))
    place[longest] = (place[longest] + 1) % extent[longest]
    return drawn.at[tuple(place)].set(top_value)


def with_spikes(entries, key, source, target, parts, factor):
    owner, partner = [(jnp.arange(entries.shape[axis_at]) // (entries.shape[axis_at] // parts)).reshape([-1 if axis == axis_at else 1 for axis in range(entries.ndim)]) for axis_at in (source, target)]
    chosen = jax.random.permutation(key, parts)[partner]
    strong = (owner == chosen) | (owner == (partner + parts // 2) % parts)
    return jnp.where(strong, factor * entries, entries)


def steps_of(key, dims, cuts, smallest, high):
    factor_of, own = 1.0, jax.random.fold_in(key, 6)
    for dim, parts in cuts:
        draws = jnp.exp(jax.random.uniform(jax.random.fold_in(own, dim), (parts,), jnp.float32, smallest / len(cuts), high / len(cuts)))
        factor_of = factor_of * jnp.repeat(draws, dims[dim] // parts).reshape([-1 if axis == dim else 1 for axis in range(len(dims))])
    return factor_of


def profile(amount, total, limit, skew):
    weights = [(1 << 20) // math.isqrt(grade ** skew) + 1 for grade in range(2, amount + 1)]
    spare, given = total - limit - (amount - 1), [1] * (amount - 1)
    while spare > 0:
        free = [i for i in range(amount - 1) if given[i] < limit]
        mass, left = sum([weights[i] for i in free]), spare
        for i in free:
            extra = min(limit - given[i], max(1, left * weights[i] // mass), spare)
            given[i] = given[i] + extra
            spare = spare - extra
    return np.array([limit] + given)


def uneven(own_key, number_of, total, most, skew):
    if number_of == 2:
        one = jax.random.randint(own_key, (), max(1, total - most), min(most, total - 1) + 1)
        return jnp.stack([one, total - one])
    sizes = jnp.asarray(profile(number_of, total, most, skew), jnp.int32)
    couples = (number_of - 1) // 2
    giver, receiver = sizes[1:1 + 2 * couples:2], sizes[2:2 + 2 * couples:2]
    slack = jnp.minimum(giver - 1, most - receiver)
    moved = jax.random.randint(jax.random.fold_in(own_key, 1), (couples,), 0, 1 << 20) % (slack + 1)
    sizes = sizes.at[1:1 + 2 * couples:2].set(giver - moved).at[2:2 + 2 * couples:2].set(receiver + moved)
    return sizes[jax.random.permutation(jax.random.fold_in(own_key, 2), number_of)]


def routed_block(own_key, own, number, rows, number_of, top, reach, slope):
    ranking = jax.random.permutation(own_key, number_of)
    heavy_load, usual = shares(number_of, rows * top, reach, slope, True), shares(number_of, rows * top, reach, slope, False)
    places = jnp.arange(number_of)

    def named(tallies, offset_by):
        used = int((tallies > 0).sum())
        fixed = max(1, used // 4)
        shifted = fixed + (places - fixed + offset_by * (used - fixed)) % max(1, number_of - fixed)
        return jnp.zeros((number_of,), jnp.int32).at[ranking[jnp.where(places < fixed, places, shifted)]].set(jnp.asarray(tallies, jnp.int32))

    tallies = jnp.where(number % 4 == 0, named(heavy_load, number // 4), named(usual, number - number // 4 - 1))
    mixed = jax.random.permutation(jax.random.fold_in(own, 3), number_of)
    giver, receiver = mixed[0:number_of // 2 * 2:2], mixed[1:number_of // 2 * 2:2]
    slack = jnp.minimum(tallies[giver] - 1, reach - tallies[receiver]) // 2
    slack = jnp.where((giver == ranking[0]) | (receiver == ranking[0]) | (tallies[receiver] == 0), 0, jnp.maximum(slack, 0))
    shifted = jax.random.randint(jax.random.fold_in(own, 4), (number_of // 2,), 0, 1 << 20) % (slack + 1)
    tallies = tallies.at[giver].add(-shifted).at[receiver].add(shifted)
    labels = jnp.searchsorted(jnp.cumsum(tallies), jnp.arange(rows * top), side="right").astype(jnp.int32)
    listing = labels.reshape(top, rows).T
    listing = listing[jax.random.permutation(jax.random.fold_in(own, 1), rows)]
    offset_by = jax.random.randint(jax.random.fold_in(own, 2), (rows, 1), 0, top)
    return jnp.take_along_axis(listing, (jnp.arange(top)[None, :] + offset_by) % top, axis=1)


def shares(number_of, total, most, lean, full):
    weights = [(1 << 20) // math.isqrt(grade ** lean) + 1 for grade in range(1, number_of + 1)]
    largest = most if full else min(most, max(-(-total // number_of), total * weights[0] // sum(weights)))
    least = 1 if total - largest >= number_of - 1 else 0
    counts, surplus = [largest] + [least] * (number_of - 1), total - largest - least * (number_of - 1)
    while surplus > 0:
        free = [i for i in range(1, number_of) if counts[i] < largest] or [i for i in range(1, number_of) if counts[i] < most]
        mass, remaining = sum([weights[i] for i in free]), surplus
        for i in free:
            more = min(most - counts[i], max(1, remaining * weights[i] // mass), surplus)
            counts[i] = counts[i] + more
            surplus = surplus - more
    return np.array(counts)


def scatter_about(key, extent, scale, limit, cuts=(), kind=jnp.bfloat16):
    entries = jax.random.normal(key, extent, jnp.float32) * scale
    if len(cuts) > 0:
        entries = steps_of(key, extent, cuts, -0.22, 0.18) * entries
    return jnp.clip(entries, min=-limit, max=limit).astype(kind)


def noise_with(stream_key, dims, scale, most, cuts, heavy, held_as=jnp.bfloat16):
    result = scale * jax.random.normal(stream_key, dims, jnp.float32)
    if cuts:
        result = result * steps_of(stream_key, dims, cuts, -0.22, 0.18)
    return jnp.clip(with_spikes(result, jax.random.fold_in(stream_key, 3), *heavy), -most, most).astype(held_as)


def setup_inputs(seed: int = 0) -> dict:
    seeds = jax.random.split(jax.random.key(seed), 20)
    step_inputs = scatter_about(seeds[0], (STEPS, BEAM_ROWS, D), 1.0, 6.0, ((1, 16), (2, 16)))
    attention_gain = jnp.clip(1.0 + 0.15 * jax.random.normal(seeds[1], (D,), jnp.float32), 0.25, 1.75)
    query_weight = scatter_about(seeds[2], (D, QUERY_HEADS * HEAD_WIDTH), (D // 6) ** -0.5, 0.3125, ((1, 16),))
    key_value_weight = scatter_about(seeds[3], (D, KEY_VALUE_WIDTH), D ** -0.5, 0.125, ((1, 16),))
    output_weight = scatter_about(seeds[4], (QUERY_HEADS * HEAD_WIDTH, D), (QUERY_HEADS * HEAD_WIDTH) ** -0.5, 0.125, ((1, 16),))
    prompt_cache = draw_prompt_cache(jax.random.fold_in(seeds[19], 71), 0)
    page_table = jax.vmap(lambda own: jax.random.permutation(own, PAGES_LOC))(jax.random.split(seeds[6], G * PAGE_COLS)).reshape((G, PAGE_COLS, PAGES_LOC)).astype(jnp.int32)
    cache_lengths = uneven(seeds[7], G, G * PROMPT_LIMIT // 2, PROMPT_LIMIT, 2).astype(jnp.int32)
    migration = jax.random.permutation(seeds[8], G).astype(jnp.int32)
    parents = with_ends(jax.random.randint(seeds[9], (STEPS - 1, BEAM_ROWS), 0, BEAMS), jax.random.fold_in(seeds[9], 1), 0, BEAMS - 1).astype(jnp.int32)
    routes_keys = jax.random.split(jax.random.fold_in(seeds[10], 1), STEPS * BEAM_ROWS // ROWS_DEV)
    routes_turns = jax.random.permutation(jax.random.fold_in(seeds[10], 3), STEPS * BEAM_ROWS // ROWS_DEV)
    routes = jax.vmap(lambda own, number: routed_block(jax.random.fold_in(seeds[10], 2), own, number, ROWS_DEV, E, TOPK, CAP, 2))(routes_keys, routes_turns).reshape((STEPS, BEAM_ROWS, TOPK))
    feedforward_gain = jnp.clip(1.0 + 0.15 * jax.random.normal(seeds[11], (D,), jnp.float32), 0.25, 1.75)
    router_weight = scatter_about(seeds[12], (D, E), D ** -0.5, 0.125)
    expert_gate = scatter_about(seeds[13], (E * SPLIT, D, FQ), D ** -0.5, 0.125, ((0, 256),))
    expert_up = scatter_about(seeds[14], (E * SPLIT, D, FQ), D ** -0.5, 0.125, ((0, 256),))
    expert_down = scatter_about(seeds[15], (E * SPLIT, FQ, D), FFE ** -0.5, 0.15625, ((0, 256),))
    shared_gate = scatter_about(seeds[16], (D, SH), D ** -0.5, 0.125, ((1, 16),))
    shared_up = scatter_about(seeds[17], (D, SH), D ** -0.5, 0.125, ((1, 16),))
    shared_down = noise_with(seeds[18], (SH, D), SH ** -0.5, 0.15625, ((0, 16),), (0, 1, 16, 2.0))
    return dict(step_inputs=step_inputs, attention_gain=attention_gain, query_weight=query_weight, key_value_weight=key_value_weight, output_weight=output_weight, prompt_cache=prompt_cache, page_table=page_table, cache_lengths=cache_lengths, migration=migration, parents=parents, routes=routes, feedforward_gain=feedforward_gain, router_weight=router_weight, expert_gate=expert_gate, expert_up=expert_up, expert_down=expert_down, shared_gate=shared_gate, shared_up=shared_up, shared_down=shared_down)


epsilon = 1e-05
rope_base = 500000.0
masked_floor = -1e+30

def norm_rows(values, gain):
    as_float = values.astype(jnp.float32)
    inverse = lax.rsqrt(lax.optimization_barrier(jnp.mean(as_float * as_float, axis=-1, keepdims=True)) + epsilon)
    return (as_float * inverse * gain).astype(jnp.bfloat16)

def apply_rotary(vectors, position_list):
    half_width = vectors.shape[-1] // 2
    frequency = rope_base ** (-2.0 * jnp.arange(half_width, dtype=jnp.float32) / vectors.shape[-1])
    angles = position_list.astype(jnp.float32)[:, None, None] * frequency
    cosine_part = jnp.cos(angles)
    sine_part = jnp.sin(angles)
    leading = vectors[..., :half_width]
    trailing = vectors[..., half_width:]
    return jnp.concatenate([leading * cosine_part - trailing * sine_part, trailing * cosine_part + leading * sine_part], axis=-1)

def reference(step_inputs, attention_gain, query_weight, key_value_weight, output_weight, prompt_cache, page_table, cache_lengths, migration, parents, routes, feedforward_gain, router_weight, expert_gate, expert_up, expert_down, shared_gate, shared_up, shared_down):
    group_of_rows = GR * BEAMS
    heads_per_group = QUERY_HEADS // KEY_VALUE_HEADS
    scaling = HEAD_WIDTH ** (-0.5)
    logical = jnp.arange(PAGES, dtype=jnp.int32)
    column_of = logical % PAGE_COLS
    local_of = logical // PAGE_COLS
    physical = column_of[None, :] * PAGES_LOC + page_table[:, column_of, local_of]
    ordered = jax.vmap(lambda pages, ordering: pages[ordering])(prompt_cache, physical)
    ordered = ordered.reshape(G, PROMPT_LIMIT, KEY_VALUE_WIDTH)
    inverse = jnp.zeros((G,), jnp.int32).at[migration].set(jnp.arange(G, dtype=jnp.int32))
    slot_lengths = cache_lengths[inverse]
    row_ids = jnp.arange(BEAM_ROWS, dtype=jnp.int32)
    slot_of_row = row_ids // group_of_rows
    tail_entries = []
    results = []
    for step_index in range(STEPS):
        current = step_inputs[step_index]
        if step_index > 0:
            parent_rows = row_ids // BEAMS * BEAMS + parents[step_index - 1]
            tail_entries = [(entry_pair[0][parent_rows], entry_pair[1][parent_rows]) for entry_pair in tail_entries]
        normed_x = norm_rows(current, attention_gain)
        projected_q = jnp.dot(normed_x, query_weight, preferred_element_type=jnp.float32).astype(jnp.bfloat16)
        key_value_projected = jnp.dot(normed_x, key_value_weight, preferred_element_type=jnp.float32).astype(jnp.bfloat16)
        position_list = slot_lengths[slot_of_row] + step_index
        query_vectors = apply_rotary(projected_q.astype(jnp.float32).reshape(BEAM_ROWS, QUERY_HEADS, HEAD_WIDTH), position_list).astype(jnp.bfloat16)
        step_keys = apply_rotary(key_value_projected[:, :KEY_VALUE_HEADS * HEAD_WIDTH].astype(jnp.float32).reshape(BEAM_ROWS, KEY_VALUE_HEADS, HEAD_WIDTH), position_list).astype(jnp.bfloat16).reshape(BEAM_ROWS, KEY_VALUE_HEADS * HEAD_WIDTH)
        step_values = key_value_projected[:, KEY_VALUE_HEADS * HEAD_WIDTH:]
        tail_entries = tail_entries + [(step_keys, step_values)]
        recent_keys = jnp.stack([entry_pair[0] for entry_pair in tail_entries], axis=1)
        recent_values = jnp.stack([entry_pair[1] for entry_pair in tail_entries], axis=1)
        tail_length = len(tail_entries)

        def one_group(slot):
            owner = inverse[slot]
            cache_entries = lax.dynamic_index_in_dim(ordered, owner, 0, keepdims=False)
            heads_of_keys = cache_entries[:, :KEY_VALUE_HEADS * HEAD_WIDTH].reshape(PROMPT_LIMIT, KEY_VALUE_HEADS, HEAD_WIDTH).astype(jnp.float32)
            heads_of_values = cache_entries[:, KEY_VALUE_HEADS * HEAD_WIDTH:].reshape(PROMPT_LIMIT, KEY_VALUE_HEADS, HEAD_WIDTH).astype(jnp.float32)
            beginning_row = slot * group_of_rows
            grouped_rows = lax.dynamic_slice_in_dim(query_vectors, beginning_row, group_of_rows, 0).astype(jnp.float32).reshape(group_of_rows, KEY_VALUE_HEADS, heads_per_group, HEAD_WIDTH)
            beam_keys = lax.dynamic_slice_in_dim(recent_keys, beginning_row, group_of_rows, 0).astype(jnp.float32).reshape(group_of_rows, tail_length, KEY_VALUE_HEADS, HEAD_WIDTH)
            beam_values = lax.dynamic_slice_in_dim(recent_values, beginning_row, group_of_rows, 0).astype(jnp.float32).reshape(group_of_rows, tail_length, KEY_VALUE_HEADS, HEAD_WIDTH)
            cache_scores = jnp.einsum('rkqd,skd->rkqs', grouped_rows, heads_of_keys) * scaling
            tail_scores = jnp.einsum('rkqd,rtkd->rkqt', grouped_rows, beam_keys) * scaling
            valid = jnp.arange(PROMPT_LIMIT, dtype=jnp.int32) < slot_lengths[slot]
            largest = jnp.maximum(lax.optimization_barrier(jnp.max(jnp.where(valid, cache_scores, masked_floor), axis=-1)), lax.optimization_barrier(jnp.max(tail_scores, axis=-1)))
            cache_probs = jnp.where(valid, jnp.exp(cache_scores - largest[..., None]), 0.0)
            tail_probs = jnp.exp(tail_scores - largest[..., None])
            denominators = lax.optimization_barrier(jnp.sum(cache_probs, axis=-1)) + lax.optimization_barrier(jnp.sum(tail_probs, axis=-1))
            rounded_cache = lax.optimization_barrier(cache_probs.astype(jnp.bfloat16)).astype(jnp.float32)
            rounded_tail = lax.optimization_barrier(tail_probs.astype(jnp.bfloat16)).astype(jnp.float32)
            weighted_values = jnp.einsum('rkqs,skd->rkqd', rounded_cache, heads_of_values) + jnp.einsum('rkqt,rtkd->rkqd', rounded_tail, beam_values)
            return (weighted_values / denominators[..., None]).astype(jnp.bfloat16).reshape(group_of_rows, QUERY_HEADS * HEAD_WIDTH)
        heads = lax.map(one_group, jnp.arange(G, dtype=jnp.int32)).reshape(BEAM_ROWS, QUERY_HEADS * HEAD_WIDTH)
        attended = (current.astype(jnp.float32) + jnp.dot(heads, output_weight, preferred_element_type=jnp.float32)).astype(jnp.bfloat16)
        normed_h = norm_rows(attended, feedforward_gain)
        logits = jnp.dot(normed_h, router_weight, preferred_element_type=jnp.float32)
        chosen = routes[step_index]
        raised = jnp.exp(jnp.take_along_axis(logits, chosen, axis=1))
        gate_weights = raised / lax.optimization_barrier(jnp.sum(raised, axis=1, keepdims=True))
        flat_routes = chosen.reshape(N_REQ, ROWS_DEV * TOPK)
        one_hot = (flat_routes[:, :, None] == jnp.arange(E, dtype=jnp.int32)[None, None, :]).astype(jnp.int32)
        ranks = lax.optimization_barrier(jnp.sum((jnp.cumsum(one_hot, axis=1) - 1) * one_hot, axis=2))
        slot_index = (jnp.arange(N_REQ, dtype=jnp.int32)[:, None] * CAP + ranks).reshape(BEAM_ROWS, TOPK)
        row_numbers = jnp.repeat(row_ids, TOPK)
        table = jnp.zeros((E, N_REQ * CAP), jnp.int32).at[chosen.reshape(-1), slot_index.reshape(-1)].set(row_numbers)
        filled = jnp.zeros((E, N_REQ * CAP), jnp.bool_).at[chosen.reshape(-1), slot_index.reshape(-1)].set(True)

        def one_expert(expert):
            members = jnp.where(filled[expert][:, None], normed_h[table[expert]], jnp.zeros((), jnp.bfloat16))
            summed = jnp.zeros((N_REQ * CAP, D), jnp.float32)
            for block_index in range(SPLIT):
                weight_index = expert * SPLIT + block_index
                gate_part = jnp.dot(members, expert_gate[weight_index], preferred_element_type=jnp.float32)
                up_part = jnp.dot(members, expert_up[weight_index], preferred_element_type=jnp.float32)
                hidden = (jax.nn.silu(gate_part) * up_part).astype(jnp.bfloat16)
                partial_value = jnp.dot(hidden, expert_down[weight_index], preferred_element_type=jnp.float32).astype(jnp.bfloat16)
                summed = summed + lax.optimization_barrier(partial_value).astype(jnp.float32)
            return summed
        expert_out = lax.map(one_expert, jnp.arange(E, dtype=jnp.int32))
        gathered = expert_out[chosen, slot_index]
        routed = lax.optimization_barrier(jnp.sum(gate_weights[..., None] * gathered, axis=1))
        shared_act = (jax.nn.silu(jnp.dot(normed_h, shared_gate, preferred_element_type=jnp.float32)) * jnp.dot(normed_h, shared_up, preferred_element_type=jnp.float32)).astype(jnp.bfloat16)
        shared = jnp.dot(shared_act, shared_down, preferred_element_type=jnp.float32)
        results.append((attended.astype(jnp.float32) + routed + shared).astype(jnp.bfloat16))
    return jnp.stack(results, axis=0)
```

```python
import jax
import jax.numpy as jnp
from jax import lax
from jax.experimental import pallas as pl
from jax.experimental.pallas import tpu as pltpu
from jax.sharding import PartitionSpec as P

QUERY_HEADS = 20
KEY_VALUE_HEADS = 4
HEAD_WIDTH = 128
E = 64
TOPK = 6
BEAMS = 8
CAP = 16
PAGE = 128

epsilon = 1e-05
rope_base = 500000.0
masked_floor = -1e30

bf16 = jnp.bfloat16
f32 = jnp.float32

SIDE = 4
QUAD = [[SIDE * i + k for k in range(SIDE)] for i in range(SIDE)]


def dot(a, b):
    return jnp.dot(a, b, preferred_element_type=f32)


def to_all(piece, axis):
    count = lax.axis_size(axis)
    copies = jnp.broadcast_to(piece[None], (count,) + piece.shape)
    return lax.all_to_all(copies, axis, 0, 0, tiled=True)


def partners(distance):
    return [(d, d ^ distance) for d in range(SIDE * SIDE)]


def group_parts(piece_for, stride):
    return [piece_for(0)] + [
        lax.ppermute(piece_for(d), "blk", partners(d * stride)) for d in range(1, SIDE)
    ]


def in_order(parts, index):
    odd = index % 2 == 1
    upper = index // 2 == 1
    a, b, c, d = parts
    a, b = jnp.where(odd, b, a), jnp.where(odd, a, b)
    c, d = jnp.where(odd, d, c), jnp.where(odd, c, d)
    return [
        jnp.where(upper, c, a),
        jnp.where(upper, d, b),
        jnp.where(upper, a, c),
        jnp.where(upper, b, d),
    ]


def norm_rows(rows, gain, axis):
    wide = rows.astype(f32)
    inverse = lax.rsqrt(jnp.mean(wide * wide, axis=axis, keepdims=True) + epsilon)
    return (wide * inverse * gain).astype(bf16)


def three_parts(value):
    high = value.astype(bf16)
    rest = value - high.astype(f32)
    middle = rest.astype(bf16)
    low = (rest - middle.astype(f32)).astype(bf16)
    return high, middle, low


def rotated(vectors, cosine, sine):
    half = vectors.shape[0] // 2
    a = vectors[:half].astype(f32)
    b = vectors[half:].astype(f32)
    return jnp.concatenate([a * cosine - b * sine, b * cosine + a * sine], axis=0)


def across(a, b):
    return lax.dot_general(a, b, (((0,), (0,)), ((), ())), preferred_element_type=f32)


def attention_kernel(
    scalars, parent, cosine, sine, p0, p1, p2, p3, c0, c1, c2, c3,
    o0, o1, o2, o3, query_rows, key_rows, value_rows, bias, scores, stats, joined,
):
    length = scalars[0]
    q_index = scalars[1]
    x_index = scalars[2]
    features, total = p0.shape
    span = query_rows.shape[0]
    share = span // SIDE
    half = HEAD_WIDTH // SIDE
    for d, piece in enumerate((p0, p1, p2, p3)):
        source = q_index ^ d
        query_rows[pl.ds(pl.multiple_of(source * share, half), share), :] = piece[:share, :]
        key_rows[pl.ds(pl.multiple_of(source * half, half), half), :] = piece[
            share : share + half, :
        ]
        value_rows[pl.ds(pl.multiple_of(source * half, half), half), :] = piece[
            share + half :, :
        ]
    cos = cosine[...]
    sin = sine[...]
    new_keys = rotated(key_rows[...], cos, sin).T.astype(bf16)
    new_values = value_rows[...]
    caches = (c0, c1, c2, c3)
    held = c0.shape[0]
    line = lax.broadcasted_iota(jnp.int32, (held, total), 0)
    spread = line + (line // PAGE) * (SIDE * SIDE - 1) * PAGE
    for d in range(SIDE):
        column = (x_index ^ d) * SIDE + q_index
        bias[d * held : (d + 1) * held, :] = jnp.where(
            spread + column * PAGE < length, 0.0, masked_floor
        )
    key_id = lax.broadcasted_iota(jnp.int32, (total, total), 0)
    row_id = lax.broadcasted_iota(jnp.int32, (total, total), 1)
    near = ((key_id == row_id) | (key_id == parent[...])) & (
        key_id // (total // SIDE) == q_index
    )
    bias[SIDE * held :, :] = jnp.where(near, 0.0, masked_floor)
    stats[...] = jnp.zeros(stats.shape, f32)
    scale = HEAD_WIDTH ** (-0.5)
    heads_here = span // HEAD_WIDTH
    for h in range(heads_here):
        query = rotated(
            query_rows[h * HEAD_WIDTH : (h + 1) * HEAD_WIDTH, :], cos, sin
        ).astype(bf16)
        for d, cache in enumerate(caches):
            scores[d * held : (d + 1) * held, :] = (
                dot(cache[:, :HEAD_WIDTH], query) * scale
                + bias[d * held : (d + 1) * held, :]
            )
        scores[SIDE * held :, :] = dot(new_keys, query) * scale + bias[SIDE * held :, :]
        peak = jnp.max(scores[...], axis=0, keepdims=True)
        mass = jnp.zeros((1, total), f32)
        weighted = jnp.zeros((HEAD_WIDTH, total), f32)
        for d, cache in enumerate(caches):
            raised = jnp.exp(scores[d * held : (d + 1) * held, :] - peak)
            mass = mass + jnp.sum(raised, axis=0, keepdims=True)
            weighted = weighted + across(cache[:, HEAD_WIDTH:], raised.astype(bf16))
        raised = jnp.exp(scores[SIDE * held :, :] - peak)
        mass = mass + jnp.sum(raised, axis=0, keepdims=True)
        weighted = weighted + dot(new_values, raised.astype(bf16))
        joined[:, h * HEAD_WIDTH : (h + 1) * HEAD_WIDTH] = (weighted / mass).T.astype(bf16)
        level = jnp.where(peak > 0.5 * masked_floor, peak + jnp.log(mass), masked_floor)
        for i, part in enumerate(three_parts(level)):
            place = i * heads_here + h
            stats[place : place + 1, :] = part.astype(f32)
    joined[:, span:] = stats[...].T.astype(bf16)
    subset = total // SIDE
    for d, out in enumerate((o0, o1, o2, o3)):
        out[...] = joined[pl.ds(pl.multiple_of((q_index ^ d) * subset, subset), subset), :]


def attend(scalars, parent, cosine, sine, pieces, caches):
    total = pieces[0].shape[1]
    subset = total // SIDE
    span = QUERY_HEADS // KEY_VALUE_HEADS * HEAD_WIDTH
    keys = SIDE * caches[0].shape[0] + total
    vmem = pl.BlockSpec(memory_space=pltpu.VMEM)
    return pl.pallas_call(
        attention_kernel,
        out_shape=[jax.ShapeDtypeStruct((subset, span + HEAD_WIDTH), bf16)] * SIDE,
        in_specs=[pl.BlockSpec(memory_space=pltpu.SMEM)] + [vmem] * (3 + 2 * SIDE),
        out_specs=[vmem] * SIDE,
        scratch_shapes=[
            pltpu.VMEM((span, total), bf16),
            pltpu.VMEM((HEAD_WIDTH, total), bf16),
            pltpu.VMEM((HEAD_WIDTH, total), bf16),
            pltpu.VMEM((keys, total), f32),
            pltpu.VMEM((keys, total), f32),
            pltpu.VMEM((HEAD_WIDTH, total), f32),
            pltpu.VMEM((total, span + HEAD_WIDTH), bf16),
        ],
        compiler_params=pltpu.CompilerParams(vmem_limit_bytes=24 << 20),
        name="attention",
    )(scalars, parent, cosine, sine, *pieces, *caches)


def expert_kernel(rows, g0, u0, d0, g1, u1, d1, out, gate_w, up_w, down_w, sems):
    copies = []
    for i, (g, u, d) in enumerate(((g0, u0, d0), (g1, u1, d1))):
        copies.append(
            [
                pltpu.make_async_copy(src, dst.at[i], sems.at[3 * i + k])
                for k, (src, dst) in enumerate(((g, gate_w), (u, up_w), (d, down_w)))
            ]
        )
    order = [(0, 0), (0, 1), (1, 0), (1, 1), (0, 2), (1, 2)]
    for i, k in order:
        copies[i][k].start()
    width = down_w.shape[2]
    hidden = []
    for i in (0, 1):
        copies[i][0].wait()
        gated = dot(rows[:, :width], gate_w[i])
        copies[i][1].wait()
        lifted = dot(rows[:, :width], up_w[i])
        hidden.append((gated / (1.0 + jnp.exp(-gated)) * lifted).astype(bf16))
    weight = (
        rows[:, width : width + 1].astype(f32)
        + rows[:, width + 1 : width + 2].astype(f32)
        + rows[:, width + 2 : width + 3].astype(f32)
    )
    copies[0][2].wait()
    copies[1][2].wait()
    step = 512
    for n in range(width // step):
        part = dot(hidden[0], down_w[0, :, n * step : (n + 1) * step]) + dot(
            hidden[1], down_w[1, :, n * step : (n + 1) * step]
        )
        out[n * step : (n + 1) * step, :] = (part * weight).T.astype(bf16)


def expert_rows(rows, blocks):
    count, wide = rows.shape
    width, units = blocks[0].shape
    vmem = pl.BlockSpec(memory_space=pltpu.VMEM)
    return pl.pallas_call(
        expert_kernel,
        out_shape=jax.ShapeDtypeStruct((width, count), bf16),
        in_specs=[vmem] + [pl.BlockSpec(memory_space=pl.ANY)] * 6,
        out_specs=vmem,
        scratch_shapes=[
            pltpu.VMEM((2, width, units), bf16),
            pltpu.VMEM((2, width, units), bf16),
            pltpu.VMEM((2, units, width), bf16),
            pltpu.SemaphoreType.DMA((6,)),
        ],
        compiler_params=pltpu.CompilerParams(vmem_limit_bytes=40 << 20),
        name="experts",
    )(rows, *blocks)


def collect_kernel(slot, returned, codes, shared, own, out, sums):
    groups, width, count = returned.shape
    slots, _, total = out.shape
    rows = total // 2
    lines = lax.broadcasted_iota(jnp.int32, (count, slots * rows), 0)
    by_step = []
    for c in (0, 1):
        acc = jnp.zeros((2 * width, slots * rows), f32)
        for x in range(SIDE):
            pick = jnp.where(
                lines == codes[2 * x + c : 2 * x + c + 1, :], 1.0, 0.0
            ).astype(bf16)
            pair = jnp.concatenate(
                [returned[SIDE * x + c], returned[SIDE * x + 2 + c]], axis=0
            )
            acc = acc + dot(pair, pick)
        by_step.append(acc[:width] + acc[width:])
    lane = lax.broadcasted_iota(jnp.int32, (width, total), 1)
    for pair in range(slots // 2):
        a = by_step[0][:, pair * total : (pair + 1) * total]
        b = by_step[1][:, pair * total : (pair + 1) * total]
        sums[2 * pair] = jnp.where(lane < rows, a, pltpu.roll(b, rows, 1))
        sums[2 * pair + 1] = jnp.where(lane < rows, pltpu.roll(a, rows, 1), b)
    mine = own[...].astype(f32)
    for g in range(groups):
        mine = mine + shared[g].astype(f32)
    sums[slot[0]] = sums[slot[0]] + mine
    out[...] = sums[...].astype(bf16)


def collect(slot, returned, codes, shared, own):
    vmem = pl.BlockSpec(memory_space=pltpu.VMEM)
    return pl.pallas_call(
        collect_kernel,
        out_shape=jax.ShapeDtypeStruct(shared.shape, bf16),
        in_specs=[pl.BlockSpec(memory_space=pltpu.SMEM)] + [vmem] * 4,
        out_specs=vmem,
        scratch_shapes=[pltpu.VMEM(shared.shape, f32)],
        compiler_params=pltpu.CompilerParams(vmem_limit_bytes=32 << 20),
        name="collect",
    )(slot, returned, codes, shared, own)


def ranks_of(named):
    rows = named.shape[-2]
    lower = (
        jnp.arange(rows, dtype=jnp.int32)[:, None] > jnp.arange(rows, dtype=jnp.int32)[None, :]
    ).astype(bf16)
    return jnp.einsum("ij,...je->...ie", lower, named.astype(bf16), preferred_element_type=f32)


def per_device(
    step_inputs,
    attention_gain,
    query_weight,
    key_value_weight,
    output_weight,
    prompt_cache,
    page_table,
    cache_lengths,
    migration,
    parents,
    routes,
    feedforward_gain,
    router_weight,
    expert_gate,
    expert_up,
    expert_down,
    shared_gate,
    shared_up,
    shared_down,
):
    req_count = lax.axis_size("req")
    blk_count = lax.axis_size("blk")
    req_index = lax.axis_index("req")
    blk_index = lax.axis_index("blk")
    x_index = blk_index // SIDE
    q_index = blk_index % SIDE
    core = blk_index % 2
    steps, rows, width_local = step_inputs.shape
    total = steps * rows
    width = width_local * blk_count
    heads_here = QUERY_HEADS // KEY_VALUE_HEADS
    span = heads_here * HEAD_WIDTH
    subset = total // SIDE

    beam = jnp.concatenate([jnp.zeros((rows,), jnp.int32), parents.reshape(-1)])
    payload = jnp.concatenate(
        [
            step_inputs.reshape(total, width_local).T,
            routes.reshape(total, TOPK).T.astype(bf16),
            beam.astype(bf16)[None],
            jnp.zeros((1, total), bf16),
        ],
        axis=0,
    )
    key_value_weight, payload = lax.optimization_barrier((key_value_weight, payload))
    by_slot = to_all(payload, "req")
    slot = migration[req_index]
    mine = lax.dynamic_index_in_dim(by_slot, slot, 0, False)
    routes_all = by_slot[:, width_local : width_local + TOPK].astype(jnp.int32)
    routes_mine = mine[width_local : width_local + TOPK].astype(jnp.int32).T
    beam_mine = mine[width_local + TOPK, rows:].astype(jnp.int32)
    inputs = to_all(mine[:width_local], "blk").reshape(width, total)

    half = key_value_weight.shape[1] // 2
    left, right = key_value_weight[:, :half], key_value_weight[:, half:]
    prompt, _ = lax.optimization_barrier((prompt_cache[0], by_slot))
    low_side = blk_index < blk_count // 2
    groups = blk_count // 2
    straight = [(d, 2 * d) for d in range(groups)] + [
        (groups + d, 2 * d + 1) for d in range(groups)
    ]
    crossed = [(d, 2 * d + 1) for d in range(groups)] + [
        (groups + d, 2 * d) for d in range(groups)
    ]
    first = lax.ppermute(jnp.where(low_side, left, right), "blk", straight)
    second = lax.ppermute(jnp.where(low_side, right, left), "blk", crossed)
    key_columns = jnp.where(core == 0, first, second)
    value_columns = jnp.where(core == 0, second, first)
    projection = jnp.concatenate([query_weight, key_columns, value_columns], axis=1)

    output_columns = lax.all_gather(
        output_weight, "blk", axis=1, tiled=True, axis_index_groups=QUAD
    )

    order = lax.dynamic_index_in_dim(page_table, req_index, 0, False)[0]
    pages = prompt[order]
    pages_local = pages.shape[0]
    by_head = (
        pages.reshape(pages_local * PAGE, 2, KEY_VALUE_HEADS, HEAD_WIDTH)
        .transpose(2, 0, 1, 3)
        .reshape(KEY_VALUE_HEADS, pages_local * PAGE, 2 * HEAD_WIDTH)
    )
    caches = group_parts(
        lambda d: lax.dynamic_index_in_dim(by_head, x_index ^ d, 0, False), SIDE
    )

    normed = norm_rows(inputs, attention_gain[:, None], 0)
    projected = across(projection, normed).astype(bf16)
    length = cache_lengths[req_index]
    frequency = rope_base ** (
        -2.0 * jnp.arange(HEAD_WIDTH // 2, dtype=f32) / HEAD_WIDTH
    )
    position = length + jnp.arange(steps, dtype=jnp.int32)
    angles = position.astype(f32)[:, None] * frequency
    cosine = jnp.repeat(jnp.cos(angles).T, rows, axis=1)
    sine = jnp.repeat(jnp.sin(angles).T, rows, axis=1)

    parent = jnp.concatenate(
        [
            jnp.full((rows,), -1, jnp.int32),
            jnp.arange(rows, dtype=jnp.int32) // BEAMS * BEAMS + beam_mine,
        ]
    )[None]
    parts = attend(
        jnp.stack([length, q_index, x_index]).astype(jnp.int32),
        parent,
        cosine,
        sine,
        group_parts(lambda d: projected, 1),
        caches,
    )
    met = jnp.stack(group_parts(lambda d: parts[d], 1))
    levels = sum(
        met[:, :, span + i * heads_here : span + (i + 1) * heads_here].astype(f32)
        for i in range(3)
    )
    shares = jnp.exp(levels - jnp.max(levels, axis=0, keepdims=True))
    shares = shares / jnp.sum(shares, axis=0, keepdims=True)
    heads = (
        jnp.sum(
            shares[..., None]
            * met[:, :, :span].reshape(SIDE, subset, heads_here, HEAD_WIDTH).astype(f32),
            axis=0,
        )
        .astype(bf16)
        .reshape(subset, span)
    )

    all_heads = jnp.concatenate(
        in_order(group_parts(lambda d: heads, SIDE), x_index), axis=1
    )
    residual = lax.dynamic_slice(
        inputs, (x_index * span, q_index * subset), (span, subset)
    ).T
    attended_part = (residual.astype(f32) + dot(all_heads, output_columns)).astype(bf16)
    gate_here, up_here, down_here, attended_part = lax.optimization_barrier(
        (expert_gate[0], expert_up[0], expert_down[0], attended_part)
    )
    blocks = [gate_here, up_here, down_here]
    expert_blocks = blocks + [lax.ppermute(b, "blk", partners(1)) for b in blocks]
    attended = (
        to_all(attended_part, "blk")
        .reshape(SIDE, SIDE, subset, span)
        .transpose(1, 2, 0, 3)
        .reshape(total, width)
    )
    normed_h = norm_rows(attended, feedforward_gain, 1)

    experts = jnp.arange(E, dtype=jnp.int32)
    named = jnp.any(routes_mine[:, :, None] == experts, axis=1)
    raised_gate = jnp.where(named, jnp.exp(dot(normed_h, router_weight)), 0.0)
    gates = raised_gate / jnp.sum(raised_gate, axis=1, keepdims=True)
    per_req = E // req_count

    def of_step(a):
        return lax.dynamic_slice_in_dim(a, core * rows, rows, 0)

    def of_expert(a):
        return lax.dynamic_index_in_dim(a.reshape(rows, req_count, per_req), x_index, 2, False).T

    named_step = of_step(named)
    rank_step = of_expert(ranks_of(named_step))
    named_here = of_expert(named_step.astype(f32)) > 0.0
    slots = jnp.arange(CAP, dtype=f32)
    dispatch = (
        named_here[:, None, :] & (rank_step[:, None, :] == slots[None, :, None])
    ).reshape(req_count * CAP, rows)
    gate_here = jnp.broadcast_to(
        of_expert(of_step(gates))[:, None, :], (req_count, CAP, rows)
    ).reshape(req_count * CAP, rows)
    slot_gate = jnp.sum(jnp.where(dispatch, gate_here, 0.0), axis=1, keepdims=True)
    sent = jnp.concatenate(
        [
            dot(dispatch.astype(bf16), of_step(normed_h)).astype(bf16),
            *three_parts(slot_gate),
            jnp.zeros((req_count * CAP, HEAD_WIDTH - 3), bf16),
        ],
        axis=1,
    ).reshape(req_count, CAP, width + HEAD_WIDTH)
    arrived = lax.all_to_all(sent, "req", 0, 0, tiled=True).reshape(
        req_count * CAP, width + HEAD_WIDTH
    )

    returned = lax.all_to_all(
        expert_rows(arrived, expert_blocks).reshape(blk_count, width_local, req_count * CAP),
        "blk",
        0,
        0,
        tiled=True,
    )

    act = (jax.nn.silu(dot(normed_h, shared_gate)) * dot(normed_h, shared_up)).astype(bf16)
    shared_part = lax.dot_general(
        shared_down, act, (((0,), (1,)), ((), ())), preferred_element_type=f32
    ).astype(bf16)
    shared = lax.all_to_all(
        shared_part.reshape(blk_count, width_local, total), "blk", 0, 0, tiled=True
    )

    slot_ids = jnp.arange(req_count, dtype=jnp.int32)
    holder = jnp.sum(
        jnp.where(migration[None, :] == slot_ids[:, None], slot_ids[None, :], 0), axis=1
    )
    owned = jnp.arange(per_req, dtype=jnp.int32) + req_index * per_req
    named_all = jnp.any(
        routes_all.reshape(1, req_count, TOPK, steps, rows) == owned[:, None, None, None, None],
        axis=2,
    )
    before = (
        jnp.arange(rows, dtype=jnp.int32)[:, None] < jnp.arange(rows, dtype=jnp.int32)[None, :]
    ).astype(bf16)
    rank_all = dot(named_all.astype(bf16).reshape(-1, rows), before).reshape(named_all.shape)
    codes = (
        jnp.where(
            named_all,
            holder[None, :, None, None] * CAP + rank_all.astype(jnp.int32),
            -1,
        )
        .transpose(0, 2, 1, 3)
        .reshape(per_req * steps, req_count * rows)
    )
    own = lax.dynamic_slice_in_dim(attended, blk_index * width_local, width_local, 1).T
    outgoing = collect(slot[None], returned, codes, shared, own)
    final = lax.all_to_all(outgoing, "req", 0, 0, tiled=True)
    return (
        jnp.sum(final.astype(f32), axis=0).T.astype(bf16).reshape(steps, rows, width_local)
    )


def solution(mesh):
    in_specs = (
        P(None, "req", "blk"),
        P(),
        P(None, "blk"),
        P(None, "blk"),
        P(None, "blk"),
        P("req", "blk", None, None),
        P(None, "blk", None),
        P(),
        P(),
        P(None, "req"),
        P(None, "req", None),
        P(),
        P(),
        P(("req", "blk"), None, None),
        P(("req", "blk"), None, None),
        P(("req", "blk"), None, None),
        P(None, "blk"),
        P(None, "blk"),
        P("blk", None),
    )
    out_specs = P(None, "req", "blk")
    return jax.shard_map(
        per_device, mesh=mesh, in_specs=in_specs, out_specs=out_specs, check_vma=False
    )
```

```python
import jax
import jax.numpy as jnp
from jax import lax
from jax.experimental import pallas as pl
from jax.experimental.pallas import tpu as pltpu
from jax.sharding import PartitionSpec as P

QUERY_HEADS = 20
KEY_VALUE_HEADS = 4
HEAD_WIDTH = 128
E = 64
TOPK = 6
BEAMS = 8
CAP = 16
PAGE = 128

epsilon = 1e-05
rope_base = 500000.0
masked_floor = -1e30

bf16 = jnp.bfloat16
f32 = jnp.float32

SIDE = 4
QUAD = [[SIDE * i + k for k in range(SIDE)] for i in range(SIDE)]


def dot(a, b):
    return jnp.dot(a, b, preferred_element_type=f32)


def to_all(piece, axis):
    count = lax.axis_size(axis)
    copies = jnp.broadcast_to(piece[None], (count,) + piece.shape)
    return lax.all_to_all(copies, axis, 0, 0, tiled=True)


def partners(distance):
    return [(d, d ^ distance) for d in range(SIDE * SIDE)]


def group_parts(piece_for, stride):
    return [piece_for(0)] + [
        lax.ppermute(piece_for(d), "blk", partners(d * stride)) for d in range(1, SIDE)
    ]


def in_order(parts, index):
    odd = index % 2 == 1
    upper = index // 2 == 1
    a, b, c, d = parts
    a, b = jnp.where(odd, b, a), jnp.where(odd, a, b)
    c, d = jnp.where(odd, d, c), jnp.where(odd, c, d)
    return [
        jnp.where(upper, c, a),
        jnp.where(upper, d, b),
        jnp.where(upper, a, c),
        jnp.where(upper, b, d),
    ]


def norm_rows(rows, gain, axis):
    wide = rows.astype(f32)
    inverse = lax.rsqrt(jnp.mean(wide * wide, axis=axis, keepdims=True) + epsilon)
    return (wide * inverse * gain).astype(bf16)


def three_parts(value):
    high = value.astype(bf16)
    rest = value - high.astype(f32)
    middle = rest.astype(bf16)
    low = (rest - middle.astype(f32)).astype(bf16)
    return high, middle, low


def rotated(vectors, cosine, sine):
    half = vectors.shape[0] // 2
    a = vectors[:half].astype(f32)
    b = vectors[half:].astype(f32)
    return jnp.concatenate([a * cosine - b * sine, b * cosine + a * sine], axis=0)


def across(a, b):
    return lax.dot_general(a, b, (((0,), (0,)), ((), ())), preferred_element_type=f32)


def attention_kernel(
    scalars, parent, cosine, sine, p0, p1, p2, p3, c0, c1, c2, c3,
    o0, o1, o2, o3, query_rows, key_rows, value_rows, bias, scores, stats, joined,
):
    length = scalars[0]
    q_index = scalars[1]
    x_index = scalars[2]
    features, total = p0.shape
    span = query_rows.shape[0]
    share = span // SIDE
    half = HEAD_WIDTH // SIDE
    for d, piece in enumerate((p0, p1, p2, p3)):
        source = q_index ^ d
        query_rows[pl.ds(pl.multiple_of(source * share, half), share), :] = piece[:share, :]
        key_rows[pl.ds(pl.multiple_of(source * half, half), half), :] = piece[
            share : share + half, :
        ]
        value_rows[pl.ds(pl.multiple_of(source * half, half), half), :] = piece[
            share + half :, :
        ]
    cos = cosine[...]
    sin = sine[...]
    new_keys = rotated(key_rows[...], cos, sin).T.astype(bf16)
    new_values = value_rows[...]
    caches = (c0, c1, c2, c3)
    held = c0.shape[0]
    line = lax.broadcasted_iota(jnp.int32, (held, total), 0)
    spread = line + (line // PAGE) * (SIDE * SIDE - 1) * PAGE
    for d in range(SIDE):
        column = (x_index ^ d) * SIDE + q_index
        bias[d * held : (d + 1) * held, :] = jnp.where(
            spread + column * PAGE < length, 0.0, masked_floor
        )
    key_id = lax.broadcasted_iota(jnp.int32, (total, total), 0)
    row_id = lax.broadcasted_iota(jnp.int32, (total, total), 1)
    near = ((key_id == row_id) | (key_id == parent[...])) & (
        key_id // (total // SIDE) == q_index
    )
    bias[SIDE * held :, :] = jnp.where(near, 0.0, masked_floor)
    stats[...] = jnp.zeros(stats.shape, f32)
    scale = HEAD_WIDTH ** (-0.5)
    heads_here = span // HEAD_WIDTH
    for h in range(heads_here):
        query = rotated(
            query_rows[h * HEAD_WIDTH : (h + 1) * HEAD_WIDTH, :], cos, sin
        ).astype(bf16)
        for d, cache in enumerate(caches):
            scores[d * held : (d + 1) * held, :] = (
                dot(cache[:, :HEAD_WIDTH], query) * scale
                + bias[d * held : (d + 1) * held, :]
            )
        scores[SIDE * held :, :] = dot(new_keys, query) * scale + bias[SIDE * held :, :]
        peak = jnp.max(scores[...], axis=0, keepdims=True)
        mass = jnp.zeros((1, total), f32)
        weighted = jnp.zeros((HEAD_WIDTH, total), f32)
        for d, cache in enumerate(caches):
            raised = jnp.exp(scores[d * held : (d + 1) * held, :] - peak)
            mass = mass + jnp.sum(raised, axis=0, keepdims=True)
            weighted = weighted + across(cache[:, HEAD_WIDTH:], raised.astype(bf16))
        raised = jnp.exp(scores[SIDE * held :, :] - peak)
        mass = mass + jnp.sum(raised, axis=0, keepdims=True)
        weighted = weighted + dot(new_values, raised.astype(bf16))
        joined[:, h * HEAD_WIDTH : (h + 1) * HEAD_WIDTH] = (weighted / mass).T.astype(bf16)
        level = jnp.where(peak > 0.5 * masked_floor, peak + jnp.log(mass), masked_floor)
        for i, part in enumerate(three_parts(level)):
            place = i * heads_here + h
            stats[place : place + 1, :] = part.astype(f32)
    joined[:, span:] = stats[...].T.astype(bf16)
    subset = total // SIDE
    for d, out in enumerate((o0, o1, o2, o3)):
        out[...] = joined[pl.ds(pl.multiple_of((q_index ^ d) * subset, subset), subset), :]


def attend(scalars, parent, cosine, sine, pieces, caches):
    total = pieces[0].shape[1]
    subset = total // SIDE
    span = QUERY_HEADS // KEY_VALUE_HEADS * HEAD_WIDTH
    keys = SIDE * caches[0].shape[0] + total
    vmem = pl.BlockSpec(memory_space=pltpu.VMEM)
    return pl.pallas_call(
        attention_kernel,
        out_shape=[jax.ShapeDtypeStruct((subset, span + HEAD_WIDTH), bf16)] * SIDE,
        in_specs=[pl.BlockSpec(memory_space=pltpu.SMEM)] + [vmem] * (3 + 2 * SIDE),
        out_specs=[vmem] * SIDE,
        scratch_shapes=[
            pltpu.VMEM((span, total), bf16),
            pltpu.VMEM((HEAD_WIDTH, total), bf16),
            pltpu.VMEM((HEAD_WIDTH, total), bf16),
            pltpu.VMEM((keys, total), f32),
            pltpu.VMEM((keys, total), f32),
            pltpu.VMEM((HEAD_WIDTH, total), f32),
            pltpu.VMEM((total, span + HEAD_WIDTH), bf16),
        ],
        compiler_params=pltpu.CompilerParams(vmem_limit_bytes=24 << 20),
        name="attention",
    )(scalars, parent, cosine, sine, *pieces, *caches)


def expert_kernel(
    expert, rows, router, named, g0, u0, d0, g1, u1, d1, out,
    gate_w, up_w, down_w, result, sems, out_sems,
):
    copies = []
    for i, (g, u, d) in enumerate(((g0, u0, d0), (g1, u1, d1))):
        copies.append(
            [
                pltpu.make_async_copy(src, dst.at[i], sems.at[3 * i + k])
                for k, (src, dst) in enumerate(((g, gate_w), (u, up_w), (d, down_w)))
            ]
        )
    order = [(0, 0), (0, 1), (1, 0), (1, 1), (0, 2), (1, 2)]
    for i, k in order:
        copies[i][k].start()
    width = down_w.shape[2]
    hidden = []
    for i in (0, 1):
        copies[i][0].wait()
        gated = dot(rows[...], gate_w[i])
        copies[i][1].wait()
        lifted = dot(rows[...], up_w[i])
        hidden.append((gated / (1.0 + jnp.exp(-gated)) * lifted).astype(bf16))
    logits = lax.dot_general(
        rows[...], router[...], (((1,), (1,)), ((), ())), preferred_element_type=f32
    )
    raised = jnp.where(named[...] > 0.0, jnp.exp(logits), 0.0)
    column = lax.broadcasted_iota(jnp.int32, raised.shape, 1)
    total = jnp.sum(raised, axis=1, keepdims=True)
    picked = jnp.sum(jnp.where(column == expert[0], raised, 0.0), axis=1, keepdims=True)
    weight = picked / jnp.where(total > 0.0, total, 1.0)
    copies[0][2].wait()
    copies[1][2].wait()
    step = width // out_sems.shape[0]
    stores = []
    for n in range(width // step):
        part = dot(hidden[0], down_w[0, :, n * step : (n + 1) * step]) + dot(
            hidden[1], down_w[1, :, n * step : (n + 1) * step]
        )
        span = slice(n * step, (n + 1) * step)
        result[span, :] = (part * weight).T.astype(bf16)
        stores.append(
            pltpu.make_async_copy(result.at[span, :], out.at[span, :], out_sems.at[n])
        )
        stores[-1].start()
    for store in stores:
        store.wait()


def expert_rows(expert, rows, router, named, blocks):
    count, width = rows.shape
    units = blocks[0].shape[1]
    vmem = pl.BlockSpec(memory_space=pltpu.VMEM)
    hbm = pl.BlockSpec(memory_space=pltpu.HBM)
    return pl.pallas_call(
        expert_kernel,
        out_shape=jax.ShapeDtypeStruct((width, count), bf16),
        in_specs=[pl.BlockSpec(memory_space=pltpu.SMEM)] + [vmem] * 3 + [hbm] * 6,
        out_specs=hbm,
        scratch_shapes=[
            pltpu.VMEM((2, width, units), bf16),
            pltpu.VMEM((2, width, units), bf16),
            pltpu.VMEM((2, units, width), bf16),
            pltpu.VMEM((width, count), bf16),
            pltpu.SemaphoreType.DMA((6,)),
            pltpu.SemaphoreType.DMA((5,)),
        ],
        compiler_params=pltpu.CompilerParams(vmem_limit_bytes=40 << 20),
        name="experts",
    )(expert, rows, router, named, *blocks)


def collect_kernel(slot, returned, codes, own, out, sums):
    groups, width, count = returned.shape
    slots, _, total = out.shape
    rows = total // 2
    lines = lax.broadcasted_iota(jnp.int32, (count, slots * rows), 0)
    by_step = []
    for c in (0, 1):
        acc = jnp.zeros((2 * width, slots * rows), f32)
        for x in range(SIDE):
            pick = jnp.where(
                lines == codes[2 * x + c : 2 * x + c + 1, :], 1.0, 0.0
            ).astype(bf16)
            pair = jnp.concatenate(
                [returned[SIDE * x + c], returned[SIDE * x + 2 + c]], axis=0
            )
            acc = acc + dot(pair, pick)
        by_step.append(acc[:width] + acc[width:])
    lane = lax.broadcasted_iota(jnp.int32, (width, total), 1)
    for pair in range(slots // 2):
        a = by_step[0][:, pair * total : (pair + 1) * total]
        b = by_step[1][:, pair * total : (pair + 1) * total]
        sums[2 * pair] = jnp.where(lane < rows, a, pltpu.roll(b, rows, 1))
        sums[2 * pair + 1] = jnp.where(lane < rows, pltpu.roll(a, rows, 1), b)
    sums[slot[0]] = sums[slot[0]] + own[...]
    out[...] = sums[...].astype(bf16)


def collect(slot, returned, codes, own):
    groups, width, _ = returned.shape
    shape = (groups, width, own.shape[1])
    vmem = pl.BlockSpec(memory_space=pltpu.VMEM)
    return pl.pallas_call(
        collect_kernel,
        out_shape=jax.ShapeDtypeStruct(shape, bf16),
        in_specs=[pl.BlockSpec(memory_space=pltpu.SMEM)] + [vmem] * 3,
        out_specs=vmem,
        scratch_shapes=[pltpu.VMEM(shape, f32)],
        compiler_params=pltpu.CompilerParams(vmem_limit_bytes=32 << 20),
        name="collect",
    )(slot, returned, codes, own)


def ranks_of(named):
    rows = named.shape[-2]
    lower = (
        jnp.arange(rows, dtype=jnp.int32)[:, None] > jnp.arange(rows, dtype=jnp.int32)[None, :]
    ).astype(bf16)
    return jnp.einsum("ij,...je->...ie", lower, named.astype(bf16), preferred_element_type=f32)


def per_device(
    step_inputs,
    attention_gain,
    query_weight,
    key_value_weight,
    output_weight,
    prompt_cache,
    page_table,
    cache_lengths,
    migration,
    parents,
    routes,
    feedforward_gain,
    router_weight,
    expert_gate,
    expert_up,
    expert_down,
    shared_gate,
    shared_up,
    shared_down,
):
    req_count = lax.axis_size("req")
    blk_count = lax.axis_size("blk")
    req_index = lax.axis_index("req")
    blk_index = lax.axis_index("blk")
    x_index = blk_index // SIDE
    q_index = blk_index % SIDE
    core = blk_index % 2
    steps, rows, width_local = step_inputs.shape
    total = steps * rows
    width = width_local * blk_count
    heads_here = QUERY_HEADS // KEY_VALUE_HEADS
    span = heads_here * HEAD_WIDTH
    subset = total // SIDE

    beam = jnp.concatenate([jnp.zeros((rows,), jnp.int32), parents.reshape(-1)])
    payload = jnp.concatenate(
        [
            step_inputs.reshape(total, width_local).T,
            routes.reshape(total, TOPK).T.astype(bf16),
            beam.astype(bf16)[None],
            jnp.zeros((1, total), bf16),
        ],
        axis=0,
    )
    key_value_weight, prompt, payload = lax.optimization_barrier(
        (key_value_weight, prompt_cache[0], payload)
    )
    by_slot = to_all(payload, "req")
    slot = migration[req_index]
    mine = lax.dynamic_index_in_dim(by_slot, slot, 0, False)
    routes_all = by_slot[:, width_local : width_local + TOPK].astype(jnp.int32)
    routes_mine = mine[width_local : width_local + TOPK].astype(jnp.int32).T
    beam_mine = mine[width_local + TOPK, rows:].astype(jnp.int32)
    inputs = to_all(mine[:width_local], "blk").reshape(width, total)

    half = key_value_weight.shape[1] // 2
    left, right = key_value_weight[:, :half], key_value_weight[:, half:]
    low_side = blk_index < blk_count // 2
    groups = blk_count // 2
    straight = [(d, 2 * d) for d in range(groups)] + [
        (groups + d, 2 * d + 1) for d in range(groups)
    ]
    crossed = [(d, 2 * d + 1) for d in range(groups)] + [
        (groups + d, 2 * d) for d in range(groups)
    ]
    first = lax.ppermute(jnp.where(low_side, left, right), "blk", straight)
    second = lax.ppermute(jnp.where(low_side, right, left), "blk", crossed)
    key_columns = jnp.where(core == 0, first, second)
    value_columns = jnp.where(core == 0, second, first)
    projection = jnp.concatenate([query_weight, key_columns, value_columns], axis=1)

    output_columns = lax.all_gather(
        output_weight, "blk", axis=1, tiled=True, axis_index_groups=QUAD
    )

    order = lax.dynamic_index_in_dim(page_table, req_index, 0, False)[0]
    pages = prompt[order]
    pages_local = pages.shape[0]
    by_head = (
        pages.reshape(pages_local * PAGE, 2, KEY_VALUE_HEADS, HEAD_WIDTH)
        .transpose(2, 0, 1, 3)
        .reshape(KEY_VALUE_HEADS, pages_local * PAGE, 2 * HEAD_WIDTH)
    )
    by_head, by_slot = lax.optimization_barrier((by_head, by_slot))
    caches = group_parts(
        lambda d: lax.dynamic_index_in_dim(by_head, x_index ^ d, 0, False), SIDE
    )

    normed = norm_rows(inputs, attention_gain[:, None], 0)
    projected = across(projection, normed).astype(bf16)
    length = cache_lengths[req_index]
    frequency = rope_base ** (
        -2.0 * jnp.arange(HEAD_WIDTH // 2, dtype=f32) / HEAD_WIDTH
    )
    position = length + jnp.arange(steps, dtype=jnp.int32)
    angles = position.astype(f32)[:, None] * frequency
    cosine = jnp.repeat(jnp.cos(angles).T, rows, axis=1)
    sine = jnp.repeat(jnp.sin(angles).T, rows, axis=1)

    parent = jnp.concatenate(
        [
            jnp.full((rows,), -1, jnp.int32),
            jnp.arange(rows, dtype=jnp.int32) // BEAMS * BEAMS + beam_mine,
        ]
    )[None]
    parts = attend(
        jnp.stack([length, q_index, x_index]).astype(jnp.int32),
        parent,
        cosine,
        sine,
        group_parts(lambda d: projected, 1),
        caches,
    )
    met = jnp.stack(group_parts(lambda d: parts[d], 1))
    levels = sum(
        met[:, :, span + i * heads_here : span + (i + 1) * heads_here].astype(f32)
        for i in range(3)
    )
    shares = jnp.exp(levels - jnp.max(levels, axis=0, keepdims=True))
    shares = shares / jnp.sum(shares, axis=0, keepdims=True)
    heads = (
        jnp.sum(
            shares[..., None]
            * met[:, :, :span].reshape(SIDE, subset, heads_here, HEAD_WIDTH).astype(f32),
            axis=0,
        )
        .astype(bf16)
        .reshape(subset, span)
    )

    all_heads = jnp.concatenate(
        in_order(group_parts(lambda d: heads, SIDE), x_index), axis=1
    )
    residual = lax.dynamic_slice(
        inputs, (x_index * span, q_index * subset), (span, subset)
    ).T
    attended_part = (residual.astype(f32) + dot(all_heads, output_columns)).astype(bf16)
    gate_here, up_here, down_here, attended_part = lax.optimization_barrier(
        (expert_gate[0], expert_up[0], expert_down[0], attended_part)
    )
    blocks = [gate_here, up_here, down_here]
    expert_blocks = blocks + [lax.ppermute(b, "blk", partners(1)) for b in blocks]
    attended = (
        to_all(attended_part, "blk")
        .reshape(SIDE, SIDE, subset, span)
        .transpose(1, 2, 0, 3)
        .reshape(total, width)
    )
    normed_h = norm_rows(attended, feedforward_gain, 1)

    per_req = E // req_count
    slot_ids = jnp.arange(req_count, dtype=jnp.int32)
    holder = jnp.sum(
        jnp.where(migration[None, :] == slot_ids[:, None], slot_ids[None, :], 0), axis=1
    )
    owned = jnp.arange(per_req, dtype=jnp.int32) + req_index * per_req
    named_all = jnp.any(
        routes_all.reshape(1, req_count, TOPK, steps, rows) == owned[:, None, None, None, None],
        axis=2,
    )
    before = (
        jnp.arange(rows, dtype=jnp.int32)[:, None] < jnp.arange(rows, dtype=jnp.int32)[None, :]
    ).astype(bf16)
    rank_all = dot(named_all.astype(bf16).reshape(-1, rows), before).reshape(named_all.shape)
    codes = (
        jnp.where(
            named_all,
            holder[None, :, None, None] * CAP + rank_all.astype(jnp.int32),
            -1,
        )
        .transpose(0, 2, 1, 3)
        .reshape(per_req * steps, req_count * rows)
    )

    experts = jnp.arange(E, dtype=jnp.int32)
    code = lax.dynamic_index_in_dim(codes, x_index * steps + core, 0, False)
    slot_of = (
        code[None, :] == jnp.arange(req_count * CAP, dtype=jnp.int32)[:, None]
    ).astype(bf16)
    routes_step = lax.dynamic_slice_in_dim(routes_all, core * rows, rows, 2)
    named_rows = (
        jnp.any(routes_step.transpose(0, 2, 1)[..., None] == experts, axis=2)
        .astype(bf16)
        .reshape(req_count * rows, E)
    )
    named_slots = dot(slot_of, named_rows)

    def of_step(a):
        return lax.dynamic_slice_in_dim(a, core * rows, rows, 0)

    def of_expert(a):
        return lax.dynamic_index_in_dim(a.reshape(rows, req_count, per_req), x_index, 2, False).T

    named_step = jnp.any(of_step(routes_mine)[:, :, None] == experts, axis=1)
    rank_step = of_expert(ranks_of(named_step))
    named_here = of_expert(named_step.astype(f32)) > 0.0
    slots = jnp.arange(CAP, dtype=f32)
    dispatch = (
        (named_here[:, None, :] & (rank_step[:, None, :] == slots[None, :, None]))
        .reshape(req_count * CAP, rows)
        .astype(bf16)
    )
    sent = dot(dispatch, of_step(normed_h)).astype(bf16).reshape(req_count, CAP, width)
    arrived = lax.all_to_all(sent, "req", 0, 0, tiled=True).reshape(req_count * CAP, width)

    returned = lax.all_to_all(
        expert_rows(
            (req_index * per_req + x_index)[None].astype(jnp.int32),
            arrived,
            router_weight.T,
            named_slots,
            expert_blocks,
        ).reshape(blk_count, width_local, req_count * CAP),
        "blk",
        0,
        0,
        tiled=True,
    )

    act = (jax.nn.silu(dot(normed_h, shared_gate)) * dot(normed_h, shared_up)).astype(bf16)
    shared_part = lax.dot_general(
        shared_down, act, (((0,), (1,)), ((), ())), preferred_element_type=f32
    ).astype(bf16)
    shared_pieces = shared_part.reshape(SIDE, SIDE, width_local, total)
    over_q = sum(
        p.astype(f32)
        for p in group_parts(
            lambda d: lax.dynamic_index_in_dim(shared_pieces, q_index ^ d, 1, False), 1
        )
    ).astype(bf16)
    shared = sum(
        p.astype(f32)
        for p in group_parts(
            lambda d: lax.dynamic_index_in_dim(over_q, x_index ^ d, 0, False), SIDE
        )
    )
    own = (
        lax.dynamic_slice_in_dim(attended, blk_index * width_local, width_local, 1)
        .T.astype(f32)
        + shared
    )
    outgoing = collect(slot[None], returned, codes, own)
    final = lax.all_to_all(outgoing, "req", 0, 0, tiled=True)
    return (
        jnp.sum(final.astype(f32), axis=0).T.astype(bf16).reshape(steps, rows, width_local)
    )


def solution(mesh):
    in_specs = (
        P(None, "req", "blk"),
        P(),
        P(None, "blk"),
        P(None, "blk"),
        P(None, "blk"),
        P("req", "blk", None, None),
        P(None, "blk", None),
        P(),
        P(),
        P(None, "req"),
        P(None, "req", None),
        P(),
        P(),
        P(("req", "blk"), None, None),
        P(("req", "blk"), None, None),
        P(("req", "blk"), None, None),
        P(None, "blk"),
        P(None, "blk"),
        P("blk", None),
    )
    out_specs = P(None, "req", "blk")
    return jax.shard_map(
        per_device, mesh=mesh, in_specs=in_specs, out_specs=out_specs, check_vma=False
    )
```

```python
import jax
import jax.numpy as jnp
from jax import lax
from jax.experimental import pallas as pl
from jax.experimental.pallas import tpu as pltpu
from jax.sharding import PartitionSpec as P

QUERY_HEADS = 20
KEY_VALUE_HEADS = 4
HEAD_WIDTH = 128
E = 64
TOPK = 6
BEAMS = 8
CAP = 16
PAGE = 128

epsilon = 1e-05
rope_base = 500000.0
masked_floor = -1e30

bf16 = jnp.bfloat16
f32 = jnp.float32

SIDE = 4
QUAD = [[SIDE * i + k for k in range(SIDE)] for i in range(SIDE)]


def dot(a, b):
    return jnp.dot(a, b, preferred_element_type=f32)


def to_all(piece, axis):
    count = lax.axis_size(axis)
    copies = jnp.broadcast_to(piece[None], (count,) + piece.shape)
    return lax.all_to_all(copies, axis, 0, 0, tiled=True)


def partners(distance):
    return [(d, d ^ distance) for d in range(SIDE * SIDE)]


def group_parts(piece_for, stride):
    return [piece_for(0)] + [
        lax.ppermute(piece_for(d), "blk", partners(d * stride)) for d in range(1, SIDE)
    ]


def in_order(parts, index):
    odd = index % 2 == 1
    upper = index // 2 == 1
    a, b, c, d = parts
    a, b = jnp.where(odd, b, a), jnp.where(odd, a, b)
    c, d = jnp.where(odd, d, c), jnp.where(odd, c, d)
    return [
        jnp.where(upper, c, a),
        jnp.where(upper, d, b),
        jnp.where(upper, a, c),
        jnp.where(upper, b, d),
    ]


def norm_rows(rows, gain, axis):
    wide = rows.astype(f32)
    inverse = lax.rsqrt(jnp.mean(wide * wide, axis=axis, keepdims=True) + epsilon)
    return (wide * inverse * gain).astype(bf16)


def three_parts(value):
    high = value.astype(bf16)
    rest = value - high.astype(f32)
    middle = rest.astype(bf16)
    low = (rest - middle.astype(f32)).astype(bf16)
    return high, middle, low


def rotated(vectors, cosine, sine):
    half = vectors.shape[0] // 2
    a = vectors[:half].astype(f32)
    b = vectors[half:].astype(f32)
    return jnp.concatenate([a * cosine - b * sine, b * cosine + a * sine], axis=0)


def across(a, b):
    return lax.dot_general(a, b, (((0,), (0,)), ((), ())), preferred_element_type=f32)


def attention_kernel(
    scalars, parent, cosine, sine, p0, p1, p2, p3, c0, c1, c2, c3,
    o0, o1, o2, o3, query_rows, key_rows, value_rows, bias, scores, stats, joined,
):
    length = scalars[0]
    q_index = scalars[1]
    x_index = scalars[2]
    features, total = p0.shape
    span = query_rows.shape[0]
    share = span // SIDE
    half = HEAD_WIDTH // SIDE
    for d, piece in enumerate((p0, p1, p2, p3)):
        source = q_index ^ d
        query_rows[pl.ds(pl.multiple_of(source * share, half), share), :] = piece[:share, :]
        key_rows[pl.ds(pl.multiple_of(source * half, half), half), :] = piece[
            share : share + half, :
        ]
        value_rows[pl.ds(pl.multiple_of(source * half, half), half), :] = piece[
            share + half :, :
        ]
    cos = cosine[...]
    sin = sine[...]
    new_keys = rotated(key_rows[...], cos, sin).T.astype(bf16)
    new_values = value_rows[...]
    caches = (c0, c1, c2, c3)
    held = c0.shape[0]
    line = lax.broadcasted_iota(jnp.int32, (held, total), 0)
    spread = line + (line // PAGE) * (SIDE * SIDE - 1) * PAGE
    for d in range(SIDE):
        column = (x_index ^ d) * SIDE + q_index
        bias[d * held : (d + 1) * held, :] = jnp.where(
            spread + column * PAGE < length, 0.0, masked_floor
        )
    key_id = lax.broadcasted_iota(jnp.int32, (total, total), 0)
    row_id = lax.broadcasted_iota(jnp.int32, (total, total), 1)
    near = ((key_id == row_id) | (key_id == parent[...])) & (
        key_id // (total // SIDE) == q_index
    )
    bias[SIDE * held :, :] = jnp.where(near, 0.0, masked_floor)
    stats[...] = jnp.zeros(stats.shape, f32)
    scale = HEAD_WIDTH ** (-0.5)
    heads_here = span // HEAD_WIDTH
    for h in range(heads_here):
        query = rotated(
            query_rows[h * HEAD_WIDTH : (h + 1) * HEAD_WIDTH, :], cos, sin
        ).astype(bf16)
        for d, cache in enumerate(caches):
            scores[d * held : (d + 1) * held, :] = (
                dot(cache[:, :HEAD_WIDTH], query) * scale
                + bias[d * held : (d + 1) * held, :]
            )
        scores[SIDE * held :, :] = dot(new_keys, query) * scale + bias[SIDE * held :, :]
        peak = jnp.max(scores[...], axis=0, keepdims=True)
        mass = jnp.zeros((1, total), f32)
        weighted = jnp.zeros((HEAD_WIDTH, total), f32)
        for d, cache in enumerate(caches):
            raised = jnp.exp(scores[d * held : (d + 1) * held, :] - peak)
            mass = mass + jnp.sum(raised, axis=0, keepdims=True)
            weighted = weighted + across(cache[:, HEAD_WIDTH:], raised.astype(bf16))
        raised = jnp.exp(scores[SIDE * held :, :] - peak)
        mass = mass + jnp.sum(raised, axis=0, keepdims=True)
        weighted = weighted + dot(new_values, raised.astype(bf16))
        joined[:, h * HEAD_WIDTH : (h + 1) * HEAD_WIDTH] = (weighted / mass).T.astype(bf16)
        level = jnp.where(peak > 0.5 * masked_floor, peak + jnp.log(mass), masked_floor)
        for i, part in enumerate(three_parts(level)):
            place = i * heads_here + h
            stats[place : place + 1, :] = part.astype(f32)
    joined[:, span:] = stats[...].T.astype(bf16)
    subset = total // SIDE
    for d, out in enumerate((o0, o1, o2, o3)):
        out[...] = joined[pl.ds(pl.multiple_of((q_index ^ d) * subset, subset), subset), :]


def attend(scalars, parent, cosine, sine, pieces, caches):
    total = pieces[0].shape[1]
    subset = total // SIDE
    span = QUERY_HEADS // KEY_VALUE_HEADS * HEAD_WIDTH
    keys = SIDE * caches[0].shape[0] + total
    vmem = pl.BlockSpec(memory_space=pltpu.VMEM)
    return pl.pallas_call(
        attention_kernel,
        out_shape=[jax.ShapeDtypeStruct((subset, span + HEAD_WIDTH), bf16)] * SIDE,
        in_specs=[pl.BlockSpec(memory_space=pltpu.SMEM)] + [vmem] * (3 + 2 * SIDE),
        out_specs=[vmem] * SIDE,
        scratch_shapes=[
            pltpu.VMEM((span, total), bf16),
            pltpu.VMEM((HEAD_WIDTH, total), bf16),
            pltpu.VMEM((HEAD_WIDTH, total), bf16),
            pltpu.VMEM((keys, total), f32),
            pltpu.VMEM((keys, total), f32),
            pltpu.VMEM((HEAD_WIDTH, total), f32),
            pltpu.VMEM((total, span + HEAD_WIDTH), bf16),
        ],
        compiler_params=pltpu.CompilerParams(vmem_limit_bytes=24 << 20),
        name="attention",
    )(scalars, parent, cosine, sine, *pieces, *caches)


def expert_kernel(
    expert, rows, router, named, g0, u0, d0, g1, u1, d1, out,
    gate_w, up_w, down_w, result, sems, out_sems,
):
    copies = []
    for i, (g, u, d) in enumerate(((g0, u0, d0), (g1, u1, d1))):
        copies.append(
            [
                pltpu.make_async_copy(src, dst.at[i], sems.at[3 * i + k])
                for k, (src, dst) in enumerate(((g, gate_w), (u, up_w), (d, down_w)))
            ]
        )
    order = [(0, 0), (0, 1), (1, 0), (1, 1), (0, 2), (1, 2)]
    for i, k in order:
        copies[i][k].start()
    width = down_w.shape[2]
    hidden = []
    for i in (0, 1):
        copies[i][0].wait()
        gated = dot(rows[...], gate_w[i])
        copies[i][1].wait()
        lifted = dot(rows[...], up_w[i])
        hidden.append((gated / (1.0 + jnp.exp(-gated)) * lifted).astype(bf16))
    logits = lax.dot_general(
        rows[...], router[...], (((1,), (1,)), ((), ())), preferred_element_type=f32
    )
    raised = jnp.where(named[...] > 0.0, jnp.exp(logits), 0.0)
    column = lax.broadcasted_iota(jnp.int32, raised.shape, 1)
    total = jnp.sum(raised, axis=1, keepdims=True)
    picked = jnp.sum(jnp.where(column == expert[0], raised, 0.0), axis=1, keepdims=True)
    weight = picked / jnp.where(total > 0.0, total, 1.0)
    copies[0][2].wait()
    copies[1][2].wait()
    step = width // out_sems.shape[0]
    stores = []
    for n in range(width // step):
        part = dot(hidden[0], down_w[0, :, n * step : (n + 1) * step]) + dot(
            hidden[1], down_w[1, :, n * step : (n + 1) * step]
        )
        span = slice(n * step, (n + 1) * step)
        result[span, :] = (part * weight).T.astype(bf16)
        stores.append(
            pltpu.make_async_copy(result.at[span, :], out.at[span, :], out_sems.at[n])
        )
        stores[-1].start()
    for store in stores:
        store.wait()


def expert_rows(expert, rows, router, named, blocks):
    count, width = rows.shape
    units = blocks[0].shape[1]
    vmem = pl.BlockSpec(memory_space=pltpu.VMEM)
    hbm = pl.BlockSpec(memory_space=pltpu.HBM)
    return pl.pallas_call(
        expert_kernel,
        out_shape=jax.ShapeDtypeStruct((width, count), bf16),
        in_specs=[pl.BlockSpec(memory_space=pltpu.SMEM)] + [vmem] * 3 + [hbm] * 6,
        out_specs=hbm,
        scratch_shapes=[
            pltpu.VMEM((2, width, units), bf16),
            pltpu.VMEM((2, width, units), bf16),
            pltpu.VMEM((2, units, width), bf16),
            pltpu.VMEM((width, count), bf16),
            pltpu.SemaphoreType.DMA((6,)),
            pltpu.SemaphoreType.DMA((5,)),
        ],
        compiler_params=pltpu.CompilerParams(vmem_limit_bytes=40 << 20),
        name="experts",
    )(
        expert,
        rows,
        router,
        named,
        *[pltpu.with_memory_space_constraint(b, pltpu.HBM) for b in blocks],
    )


def collect_kernel(slot, returned, codes, own, out, sums):
    groups, width, count = returned.shape
    slots, _, total = out.shape
    rows = total // 2
    lines = lax.broadcasted_iota(jnp.int32, (count, slots * rows), 0)
    by_step = []
    for c in (0, 1):
        acc = jnp.zeros((2 * width, slots * rows), f32)
        for x in range(SIDE):
            pick = jnp.where(
                lines == codes[2 * x + c : 2 * x + c + 1, :], 1.0, 0.0
            ).astype(bf16)
            pair = jnp.concatenate(
                [returned[SIDE * x + c], returned[SIDE * x + 2 + c]], axis=0
            )
            acc = acc + dot(pair, pick)
        by_step.append(acc[:width] + acc[width:])
    lane = lax.broadcasted_iota(jnp.int32, (width, total), 1)
    for pair in range(slots // 2):
        a = by_step[0][:, pair * total : (pair + 1) * total]
        b = by_step[1][:, pair * total : (pair + 1) * total]
        sums[2 * pair] = jnp.where(lane < rows, a, pltpu.roll(b, rows, 1))
        sums[2 * pair + 1] = jnp.where(lane < rows, pltpu.roll(a, rows, 1), b)
    sums[slot[0]] = sums[slot[0]] + own[...]
    out[...] = sums[...].astype(bf16)


def collect(slot, returned, codes, own):
    groups, width, _ = returned.shape
    shape = (groups, width, own.shape[1])
    vmem = pl.BlockSpec(memory_space=pltpu.VMEM)
    return pl.pallas_call(
        collect_kernel,
        out_shape=jax.ShapeDtypeStruct(shape, bf16),
        in_specs=[pl.BlockSpec(memory_space=pltpu.SMEM)] + [vmem] * 3,
        out_specs=vmem,
        scratch_shapes=[pltpu.VMEM(shape, f32)],
        compiler_params=pltpu.CompilerParams(vmem_limit_bytes=32 << 20),
        name="collect",
    )(slot, returned, codes, own)


def ranks_of(named):
    rows = named.shape[-2]
    lower = (
        jnp.arange(rows, dtype=jnp.int32)[:, None] > jnp.arange(rows, dtype=jnp.int32)[None, :]
    ).astype(bf16)
    return jnp.einsum("ij,...je->...ie", lower, named.astype(bf16), preferred_element_type=f32)


def per_device(
    step_inputs,
    attention_gain,
    query_weight,
    key_value_weight,
    output_weight,
    prompt_cache,
    page_table,
    cache_lengths,
    migration,
    parents,
    routes,
    feedforward_gain,
    router_weight,
    expert_gate,
    expert_up,
    expert_down,
    shared_gate,
    shared_up,
    shared_down,
):
    req_count = lax.axis_size("req")
    blk_count = lax.axis_size("blk")
    req_index = lax.axis_index("req")
    blk_index = lax.axis_index("blk")
    x_index = blk_index // SIDE
    q_index = blk_index % SIDE
    core = blk_index % 2
    steps, rows, width_local = step_inputs.shape
    total = steps * rows
    width = width_local * blk_count
    heads_here = QUERY_HEADS // KEY_VALUE_HEADS
    span = heads_here * HEAD_WIDTH
    subset = total // SIDE

    beam = jnp.concatenate([jnp.zeros((rows,), jnp.int32), parents.reshape(-1)])
    payload = jnp.concatenate(
        [
            step_inputs.reshape(total, width_local).T,
            routes.reshape(total, TOPK).T.astype(bf16),
            beam.astype(bf16)[None],
            jnp.zeros((1, total), bf16),
        ],
        axis=0,
    )
    prompt, payload = lax.optimization_barrier((prompt_cache[0], payload))
    by_slot = to_all(payload, "req")
    slot = migration[req_index]
    mine = lax.dynamic_index_in_dim(by_slot, slot, 0, False)
    routes_all = by_slot[:, width_local : width_local + TOPK].astype(jnp.int32)
    routes_mine = mine[width_local : width_local + TOPK].astype(jnp.int32).T
    beam_mine = mine[width_local + TOPK, rows:].astype(jnp.int32)
    inputs = to_all(mine[:width_local], "blk").reshape(width, total)

    output_columns = lax.all_gather(
        output_weight, "blk", axis=1, tiled=True, axis_index_groups=QUAD
    )

    order = lax.dynamic_index_in_dim(page_table, req_index, 0, False)[0]
    pages = prompt[order]
    pages_local = pages.shape[0]
    by_head = (
        pages.reshape(pages_local * PAGE, 2, KEY_VALUE_HEADS, HEAD_WIDTH)
        .transpose(2, 0, 1, 3)
        .reshape(KEY_VALUE_HEADS, pages_local * PAGE, 2 * HEAD_WIDTH)
    )
    key_value_weight, by_head = lax.optimization_barrier((key_value_weight, by_head))
    caches = group_parts(
        lambda d: lax.dynamic_index_in_dim(by_head, x_index ^ d, 0, False), SIDE
    )

    half = key_value_weight.shape[1] // 2
    left, right = key_value_weight[:, :half], key_value_weight[:, half:]
    low_side = blk_index < blk_count // 2
    groups = blk_count // 2
    straight = [(d, 2 * d) for d in range(groups)] + [
        (groups + d, 2 * d + 1) for d in range(groups)
    ]
    crossed = [(d, 2 * d + 1) for d in range(groups)] + [
        (groups + d, 2 * d) for d in range(groups)
    ]
    first = lax.ppermute(jnp.where(low_side, left, right), "blk", straight)
    second = lax.ppermute(jnp.where(low_side, right, left), "blk", crossed)
    key_columns = jnp.where(core == 0, first, second)
    value_columns = jnp.where(core == 0, second, first)
    projection = jnp.concatenate([query_weight, key_columns, value_columns], axis=1)

    normed = norm_rows(inputs, attention_gain[:, None], 0)
    projected = across(projection, normed).astype(bf16)
    length = cache_lengths[req_index]
    frequency = rope_base ** (
        -2.0 * jnp.arange(HEAD_WIDTH // 2, dtype=f32) / HEAD_WIDTH
    )
    position = length + jnp.arange(steps, dtype=jnp.int32)
    angles = position.astype(f32)[:, None] * frequency
    cosine = jnp.repeat(jnp.cos(angles).T, rows, axis=1)
    sine = jnp.repeat(jnp.sin(angles).T, rows, axis=1)

    parent = jnp.concatenate(
        [
            jnp.full((rows,), -1, jnp.int32),
            jnp.arange(rows, dtype=jnp.int32) // BEAMS * BEAMS + beam_mine,
        ]
    )[None]
    parts = attend(
        jnp.stack([length, q_index, x_index]).astype(jnp.int32),
        parent,
        cosine,
        sine,
        group_parts(lambda d: projected, 1),
        caches,
    )
    met = jnp.stack(group_parts(lambda d: parts[d], 1))
    levels = sum(
        met[:, :, span + i * heads_here : span + (i + 1) * heads_here].astype(f32)
        for i in range(3)
    )
    shares = jnp.exp(levels - jnp.max(levels, axis=0, keepdims=True))
    shares = shares / jnp.sum(shares, axis=0, keepdims=True)
    heads = (
        jnp.sum(
            shares[..., None]
            * met[:, :, :span].reshape(SIDE, subset, heads_here, HEAD_WIDTH).astype(f32),
            axis=0,
        )
        .astype(bf16)
        .reshape(subset, span)
    )

    all_heads = jnp.concatenate(
        in_order(group_parts(lambda d: heads, SIDE), x_index), axis=1
    )
    residual = lax.dynamic_slice(
        inputs, (x_index * span, q_index * subset), (span, subset)
    ).T
    attended_part = (residual.astype(f32) + dot(all_heads, output_columns)).astype(bf16)
    gate_here, up_here, down_here, attended_part = lax.optimization_barrier(
        (expert_gate[0], expert_up[0], expert_down[0], attended_part)
    )
    blocks = [gate_here, up_here, down_here]
    expert_blocks = blocks + [lax.ppermute(b, "blk", partners(1)) for b in blocks]
    attended = (
        to_all(attended_part, "blk")
        .reshape(SIDE, SIDE, subset, span)
        .transpose(1, 2, 0, 3)
        .reshape(total, width)
    )
    normed_h = norm_rows(attended, feedforward_gain, 1)

    per_req = E // req_count
    slot_ids = jnp.arange(req_count, dtype=jnp.int32)
    holder = jnp.sum(
        jnp.where(migration[None, :] == slot_ids[:, None], slot_ids[None, :], 0), axis=1
    )
    owned = jnp.arange(per_req, dtype=jnp.int32) + req_index * per_req
    named_all = jnp.any(
        routes_all.reshape(1, req_count, TOPK, steps, rows) == owned[:, None, None, None, None],
        axis=2,
    )
    before = (
        jnp.arange(rows, dtype=jnp.int32)[:, None] < jnp.arange(rows, dtype=jnp.int32)[None, :]
    ).astype(bf16)
    rank_all = dot(named_all.astype(bf16).reshape(-1, rows), before).reshape(named_all.shape)
    codes = (
        jnp.where(
            named_all,
            holder[None, :, None, None] * CAP + rank_all.astype(jnp.int32),
            -1,
        )
        .transpose(0, 2, 1, 3)
        .reshape(per_req * steps, req_count * rows)
    )

    experts = jnp.arange(E, dtype=jnp.int32)
    code = lax.dynamic_index_in_dim(codes, x_index * steps + core, 0, False)
    slot_of = (
        code[None, :] == jnp.arange(req_count * CAP, dtype=jnp.int32)[:, None]
    ).astype(bf16)
    routes_step = lax.dynamic_slice_in_dim(routes_all, core * rows, rows, 2)
    named_rows = (
        jnp.any(routes_step.transpose(0, 2, 1)[..., None] == experts, axis=2)
        .astype(bf16)
        .reshape(req_count * rows, E)
    )
    named_slots = dot(slot_of, named_rows)

    def of_step(a):
        return lax.dynamic_slice_in_dim(a, core * rows, rows, 0)

    def of_expert(a):
        return lax.dynamic_index_in_dim(a.reshape(rows, req_count, per_req), x_index, 2, False).T

    named_step = jnp.any(of_step(routes_mine)[:, :, None] == experts, axis=1)
    rank_step = of_expert(ranks_of(named_step))
    named_here = of_expert(named_step.astype(f32)) > 0.0
    slots = jnp.arange(CAP, dtype=f32)
    dispatch = (
        (named_here[:, None, :] & (rank_step[:, None, :] == slots[None, :, None]))
        .reshape(req_count * CAP, rows)
        .astype(bf16)
    )
    sent = dot(dispatch, of_step(normed_h)).astype(bf16).reshape(req_count, CAP, width)
    arrived = lax.all_to_all(sent, "req", 0, 0, tiled=True).reshape(req_count * CAP, width)

    act = (jax.nn.silu(dot(normed_h, shared_gate)) * dot(normed_h, shared_up)).astype(bf16)
    shared_part = lax.dot_general(
        shared_down, act, (((0,), (1,)), ((), ())), preferred_element_type=f32
    ).astype(bf16)
    shared_pieces = shared_part.reshape(SIDE, SIDE, width_local, total)
    over_q = sum(
        p.astype(f32)
        for p in group_parts(
            lambda d: lax.dynamic_index_in_dim(shared_pieces, q_index ^ d, 1, False), 1
        )
    ).astype(bf16)
    shared = sum(
        p.astype(f32)
        for p in group_parts(
            lambda d: lax.dynamic_index_in_dim(over_q, x_index ^ d, 0, False), SIDE
        )
    )
    own = (
        lax.dynamic_slice_in_dim(attended, blk_index * width_local, width_local, 1)
        .T.astype(f32)
        + shared
    )
    arrived, own = lax.optimization_barrier((arrived, own))

    returned = lax.all_to_all(
        expert_rows(
            (req_index * per_req + x_index)[None].astype(jnp.int32),
            arrived,
            router_weight.T,
            named_slots,
            expert_blocks,
        ).reshape(blk_count, width_local, req_count * CAP),
        "blk",
        0,
        0,
        tiled=True,
    )

    outgoing = collect(slot[None], returned, codes, own)
    final = lax.all_to_all(outgoing, "req", 0, 0, tiled=True)
    return (
        jnp.sum(final.astype(f32), axis=0).T.astype(bf16).reshape(steps, rows, width_local)
    )


def solution(mesh):
    in_specs = (
        P(None, "req", "blk"),
        P(),
        P(None, "blk"),
        P(None, "blk"),
        P(None, "blk"),
        P("req", "blk", None, None),
        P(None, "blk", None),
        P(),
        P(),
        P(None, "req"),
        P(None, "req", None),
        P(),
        P(),
        P(("req", "blk"), None, None),
        P(("req", "blk"), None, None),
        P(("req", "blk"), None, None),
        P(None, "blk"),
        P(None, "blk"),
        P("blk", None),
    )
    out_specs = P(None, "req", "blk")
    return jax.shard_map(
        per_device, mesh=mesh, in_specs=in_specs, out_specs=out_specs, check_vma=False
    )
```

```python
import jax
import jax.numpy as jnp
from jax import lax
from jax.experimental import pallas as pl
from jax.experimental.pallas import tpu as pltpu
from jax.sharding import PartitionSpec as P

QUERY_HEADS = 20
KEY_VALUE_HEADS = 4
HEAD_WIDTH = 128
E = 64
TOPK = 6
BEAMS = 8
CAP = 16
PAGE = 128

epsilon = 1e-05
rope_base = 500000.0
masked_floor = -1e30

bf16 = jnp.bfloat16
f32 = jnp.float32

SIDE = 4
QUAD = [[SIDE * i + k for k in range(SIDE)] for i in range(SIDE)]


def dot(a, b):
    return jnp.dot(a, b, preferred_element_type=f32)


def to_all(piece, axis):
    count = lax.axis_size(axis)
    copies = jnp.broadcast_to(piece[None], (count,) + piece.shape)
    return lax.all_to_all(copies, axis, 0, 0, tiled=True)


def partners(distance):
    return [(d, d ^ distance) for d in range(SIDE * SIDE)]


def group_parts(piece_for, stride):
    return [piece_for(0)] + [
        lax.ppermute(piece_for(d), "blk", partners(d * stride)) for d in range(1, SIDE)
    ]


def in_order(parts, index):
    odd = index % 2 == 1
    upper = index // 2 == 1
    a, b, c, d = parts
    a, b = jnp.where(odd, b, a), jnp.where(odd, a, b)
    c, d = jnp.where(odd, d, c), jnp.where(odd, c, d)
    return [
        jnp.where(upper, c, a),
        jnp.where(upper, d, b),
        jnp.where(upper, a, c),
        jnp.where(upper, b, d),
    ]


def norm_rows(rows, gain, axis):
    wide = rows.astype(f32)
    inverse = lax.rsqrt(jnp.mean(wide * wide, axis=axis, keepdims=True) + epsilon)
    return (wide * inverse * gain).astype(bf16)


def three_parts(value):
    high = value.astype(bf16)
    rest = value - high.astype(f32)
    middle = rest.astype(bf16)
    low = (rest - middle.astype(f32)).astype(bf16)
    return high, middle, low


def rotated(vectors, cosine, sine):
    half = vectors.shape[0] // 2
    a = vectors[:half].astype(f32)
    b = vectors[half:].astype(f32)
    return jnp.concatenate([a * cosine - b * sine, b * cosine + a * sine], axis=0)


def across(a, b):
    return lax.dot_general(a, b, (((0,), (0,)), ((), ())), preferred_element_type=f32)


def payload_kernel(x, routes, beams, out, lines):
    total, width = x.shape
    rows = total // 2
    main = width // 128 * 128
    lines[:main, :] = x[:, :main].astype(f32).T.astype(bf16)
    rest = jnp.concatenate(
        [x[:, main:].astype(f32), jnp.zeros((total, 128 - width + main), f32)], axis=1
    )
    lines[main:width, :] = rest.T[: width - main].astype(bf16)
    named = [
        jnp.concatenate([routes[k, 0:1, :], routes[k, 1:2, :]], axis=1) for k in range(TOPK)
    ]
    beam = jnp.concatenate([jnp.zeros((1, rows), jnp.int32), beams[...]], axis=1)
    extra = jnp.concatenate(named + [beam, jnp.zeros((1, total), jnp.int32)], axis=0)
    lines[width:, :] = extra.astype(f32).astype(bf16)
    for i in range(out.shape[0]):
        out[i] = lines[...]


def payloads(count, x, routes, beams):
    total, width = x.shape
    vmem = pl.BlockSpec(memory_space=pltpu.VMEM)
    return pl.pallas_call(
        payload_kernel,
        out_shape=jax.ShapeDtypeStruct((count, width + TOPK + 2, total), bf16),
        in_specs=[vmem] * 3,
        out_specs=vmem,
        scratch_shapes=[pltpu.VMEM((width + TOPK + 2, total), bf16)],
        name="payload",
    )(x, routes, beams)


def attention_kernel(
    scalars, parent, cosine, sine, p0, p1, p2, p3, c0, c1, c2, c3,
    o0, o1, o2, o3, query_rows, key_rows, value_rows, bias, scores, stats, joined,
):
    length = scalars[0]
    q_index = scalars[1]
    x_index = scalars[2]
    features, total = p0.shape
    span = query_rows.shape[0]
    share = span // SIDE
    half = HEAD_WIDTH // SIDE
    for d, piece in enumerate((p0, p1, p2, p3)):
        source = q_index ^ d
        query_rows[pl.ds(pl.multiple_of(source * share, half), share), :] = piece[:share, :]
        key_rows[pl.ds(pl.multiple_of(source * half, half), half), :] = piece[
            share : share + half, :
        ]
        value_rows[pl.ds(pl.multiple_of(source * half, half), half), :] = piece[
            share + half :, :
        ]
    cos = cosine[...]
    sin = sine[...]
    new_keys = rotated(key_rows[...], cos, sin).T.astype(bf16)
    new_values = value_rows[...]
    caches = (c0, c1, c2, c3)
    held = c0.shape[0]
    line = lax.broadcasted_iota(jnp.int32, (held, total), 0)
    spread = line + (line // PAGE) * (SIDE * SIDE - 1) * PAGE
    for d in range(SIDE):
        column = (x_index ^ d) * SIDE + q_index
        bias[d * held : (d + 1) * held, :] = jnp.where(
            spread + column * PAGE < length, 0.0, masked_floor
        )
    key_id = lax.broadcasted_iota(jnp.int32, (total, total), 0)
    row_id = lax.broadcasted_iota(jnp.int32, (total, total), 1)
    near = ((key_id == row_id) | (key_id == parent[...])) & (
        key_id // (total // SIDE) == q_index
    )
    bias[SIDE * held :, :] = jnp.where(near, 0.0, masked_floor)
    stats[...] = jnp.zeros(stats.shape, f32)
    scale = HEAD_WIDTH ** (-0.5)
    heads_here = span // HEAD_WIDTH
    for h in range(heads_here):
        query = rotated(
            query_rows[h * HEAD_WIDTH : (h + 1) * HEAD_WIDTH, :], cos, sin
        ).astype(bf16)
        for d, cache in enumerate(caches):
            scores[d * held : (d + 1) * held, :] = (
                dot(cache[:, :HEAD_WIDTH], query) * scale
                + bias[d * held : (d + 1) * held, :]
            )
        scores[SIDE * held :, :] = dot(new_keys, query) * scale + bias[SIDE * held :, :]
        peak = jnp.max(scores[...], axis=0, keepdims=True)
        mass = jnp.zeros((1, total), f32)
        weighted = jnp.zeros((HEAD_WIDTH, total), f32)
        for d, cache in enumerate(caches):
            raised = jnp.exp(scores[d * held : (d + 1) * held, :] - peak)
            mass = mass + jnp.sum(raised, axis=0, keepdims=True)
            weighted = weighted + across(cache[:, HEAD_WIDTH:], raised.astype(bf16))
        raised = jnp.exp(scores[SIDE * held :, :] - peak)
        mass = mass + jnp.sum(raised, axis=0, keepdims=True)
        weighted = weighted + dot(new_values, raised.astype(bf16))
        joined[:, h * HEAD_WIDTH : (h + 1) * HEAD_WIDTH] = (weighted / mass).T.astype(bf16)
        level = jnp.where(peak > 0.5 * masked_floor, peak + jnp.log(mass), masked_floor)
        for i, part in enumerate(three_parts(level)):
            place = i * heads_here + h
            stats[place : place + 1, :] = part.astype(f32)
    joined[:, span:] = stats[...].T.astype(bf16)
    subset = total // SIDE
    for d, out in enumerate((o0, o1, o2, o3)):
        out[...] = joined[pl.ds(pl.multiple_of((q_index ^ d) * subset, subset), subset), :]


def attend(scalars, parent, cosine, sine, pieces, caches):
    total = pieces[0].shape[1]
    subset = total // SIDE
    span = QUERY_HEADS // KEY_VALUE_HEADS * HEAD_WIDTH
    keys = SIDE * caches[0].shape[0] + total
    vmem = pl.BlockSpec(memory_space=pltpu.VMEM)
    return pl.pallas_call(
        attention_kernel,
        out_shape=[jax.ShapeDtypeStruct((subset, span + HEAD_WIDTH), bf16)] * SIDE,
        in_specs=[pl.BlockSpec(memory_space=pltpu.SMEM)] + [vmem] * (3 + 2 * SIDE),
        out_specs=[vmem] * SIDE,
        scratch_shapes=[
            pltpu.VMEM((span, total), bf16),
            pltpu.VMEM((HEAD_WIDTH, total), bf16),
            pltpu.VMEM((HEAD_WIDTH, total), bf16),
            pltpu.VMEM((keys, total), f32),
            pltpu.VMEM((keys, total), f32),
            pltpu.VMEM((HEAD_WIDTH, total), f32),
            pltpu.VMEM((total, span + HEAD_WIDTH), bf16),
        ],
        compiler_params=pltpu.CompilerParams(vmem_limit_bytes=24 << 20),
        name="attention",
    )(scalars, parent, cosine, sine, *pieces, *caches)


def expert_kernel(
    expert, rows, router, named, g0, u0, d0, g1, u1, d1, out,
    gate_w, up_w, down_w, result, sems, out_sems,
):
    copies = []
    for i, (g, u, d) in enumerate(((g0, u0, d0), (g1, u1, d1))):
        copies.append(
            [
                pltpu.make_async_copy(src, dst.at[i], sems.at[3 * i + k])
                for k, (src, dst) in enumerate(((g, gate_w), (u, up_w), (d, down_w)))
            ]
        )
    order = [(0, 0), (0, 1), (1, 0), (1, 1), (0, 2), (1, 2)]
    for i, k in order:
        copies[i][k].start()
    width = down_w.shape[2]
    logits = lax.dot_general(
        rows[...], router[...], (((1,), (1,)), ((), ())), preferred_element_type=f32
    )
    raised = jnp.where(named[...] > 0.0, jnp.exp(logits), 0.0)
    column = lax.broadcasted_iota(jnp.int32, raised.shape, 1)
    total = jnp.sum(raised, axis=1, keepdims=True)
    picked = jnp.sum(jnp.where(column == expert[0], raised, 0.0), axis=1, keepdims=True)
    weight = picked / jnp.where(total > 0.0, total, 1.0)
    hidden = []
    for i in (0, 1):
        copies[i][0].wait()
        gated = dot(rows[...], gate_w[i])
        copies[i][1].wait()
        lifted = dot(rows[...], up_w[i])
        hidden.append((gated / (1.0 + jnp.exp(-gated)) * lifted).astype(bf16))
    copies[0][2].wait()
    copies[1][2].wait()
    step = width // out_sems.shape[0]
    stores = []
    for n in range(width // step):
        part = dot(hidden[0], down_w[0, :, n * step : (n + 1) * step]) + dot(
            hidden[1], down_w[1, :, n * step : (n + 1) * step]
        )
        span = slice(n * step, (n + 1) * step)
        result[span, :] = (part * weight).T.astype(bf16)
        stores.append(
            pltpu.make_async_copy(result.at[span, :], out.at[span, :], out_sems.at[n])
        )
        stores[-1].start()
    for store in stores:
        store.wait()


def expert_rows(expert, rows, router, named, blocks):
    count, width = rows.shape
    units = blocks[0].shape[1]
    vmem = pl.BlockSpec(memory_space=pltpu.VMEM)
    hbm = pl.BlockSpec(memory_space=pltpu.HBM)
    return pl.pallas_call(
        expert_kernel,
        out_shape=jax.ShapeDtypeStruct((width, count), bf16),
        in_specs=[pl.BlockSpec(memory_space=pltpu.SMEM)] + [vmem] * 3 + [hbm] * 6,
        out_specs=hbm,
        scratch_shapes=[
            pltpu.VMEM((2, width, units), bf16),
            pltpu.VMEM((2, width, units), bf16),
            pltpu.VMEM((2, units, width), bf16),
            pltpu.VMEM((width, count), bf16),
            pltpu.SemaphoreType.DMA((6,)),
            pltpu.SemaphoreType.DMA((5,)),
        ],
        compiler_params=pltpu.CompilerParams(vmem_limit_bytes=40 << 20),
        name="experts",
    )(
        expert,
        rows,
        router,
        named,
        *[pltpu.with_memory_space_constraint(b, pltpu.HBM) for b in blocks],
    )


def collect_kernel(slot, returned, codes, own, out, sums):
    groups, width, count = returned.shape
    slots, _, total = out.shape
    rows = total // 2
    lines = lax.broadcasted_iota(jnp.int32, (count, slots * rows), 0)
    by_step = []
    for c in (0, 1):
        acc = jnp.zeros((2 * width, slots * rows), f32)
        for x in range(SIDE):
            pick = jnp.where(
                lines == codes[2 * x + c : 2 * x + c + 1, :], 1.0, 0.0
            ).astype(bf16)
            pair = jnp.concatenate(
                [returned[SIDE * x + c], returned[SIDE * x + 2 + c]], axis=0
            )
            acc = acc + dot(pair, pick)
        by_step.append(acc[:width] + acc[width:])
    lane = lax.broadcasted_iota(jnp.int32, (width, total), 1)
    for pair in range(slots // 2):
        a = by_step[0][:, pair * total : (pair + 1) * total]
        b = by_step[1][:, pair * total : (pair + 1) * total]
        sums[2 * pair] = jnp.where(lane < rows, a, pltpu.roll(b, rows, 1))
        sums[2 * pair + 1] = jnp.where(lane < rows, pltpu.roll(a, rows, 1), b)
    sums[slot[0]] = sums[slot[0]] + own[...]
    out[...] = sums[...].astype(bf16)


def collect(slot, returned, codes, own):
    groups, width, _ = returned.shape
    shape = (groups, width, own.shape[1])
    vmem = pl.BlockSpec(memory_space=pltpu.VMEM)
    return pl.pallas_call(
        collect_kernel,
        out_shape=jax.ShapeDtypeStruct(shape, bf16),
        in_specs=[pl.BlockSpec(memory_space=pltpu.SMEM)] + [vmem] * 3,
        out_specs=vmem,
        scratch_shapes=[pltpu.VMEM(shape, f32)],
        compiler_params=pltpu.CompilerParams(vmem_limit_bytes=32 << 20),
        name="collect",
    )(slot, returned, codes, own)


def ranks_of(named):
    rows = named.shape[-2]
    lower = (
        jnp.arange(rows, dtype=jnp.int32)[:, None] > jnp.arange(rows, dtype=jnp.int32)[None, :]
    ).astype(bf16)
    return jnp.einsum("ij,...je->...ie", lower, named.astype(bf16), preferred_element_type=f32)


def per_device(
    step_inputs,
    attention_gain,
    query_weight,
    key_value_weight,
    output_weight,
    prompt_cache,
    page_table,
    cache_lengths,
    migration,
    parents,
    routes,
    feedforward_gain,
    router_weight,
    expert_gate,
    expert_up,
    expert_down,
    shared_gate,
    shared_up,
    shared_down,
):
    req_count = lax.axis_size("req")
    blk_count = lax.axis_size("blk")
    req_index = lax.axis_index("req")
    blk_index = lax.axis_index("blk")
    x_index = blk_index // SIDE
    q_index = blk_index % SIDE
    core = blk_index % 2
    steps, rows, width_local = step_inputs.shape
    total = steps * rows
    width = width_local * blk_count
    heads_here = QUERY_HEADS // KEY_VALUE_HEADS
    span = heads_here * HEAD_WIDTH
    subset = total // SIDE

    payload = payloads(
        req_count,
        step_inputs.reshape(total, width_local),
        routes.transpose(2, 0, 1),
        parents,
    )
    prompt, payload = lax.optimization_barrier((prompt_cache[0], payload))
    by_slot = lax.all_to_all(payload, "req", 0, 0, tiled=True)
    slot = migration[req_index]
    mine = lax.dynamic_index_in_dim(by_slot, slot, 0, False)
    routes_all = by_slot[:, width_local : width_local + TOPK].astype(jnp.int32)
    routes_mine = mine[width_local : width_local + TOPK].astype(jnp.int32).T
    beam_mine = mine[width_local + TOPK, rows:].astype(jnp.int32)
    inputs = to_all(mine[:width_local], "blk").reshape(width, total)

    output_columns = lax.all_gather(
        output_weight, "blk", axis=1, tiled=True, axis_index_groups=QUAD
    )

    order = lax.dynamic_index_in_dim(page_table, req_index, 0, False)[0]
    pages = prompt[order]
    pages_local = pages.shape[0]
    by_head = (
        pages.reshape(pages_local * PAGE, 2, KEY_VALUE_HEADS, HEAD_WIDTH)
        .transpose(2, 0, 1, 3)
        .reshape(KEY_VALUE_HEADS, pages_local * PAGE, 2 * HEAD_WIDTH)
    )
    key_value_weight, by_head = lax.optimization_barrier((key_value_weight, by_head))
    caches = group_parts(
        lambda d: lax.dynamic_index_in_dim(by_head, x_index ^ d, 0, False), SIDE
    )

    half = key_value_weight.shape[1] // 2
    left, right = key_value_weight[:, :half], key_value_weight[:, half:]
    low_side = blk_index < blk_count // 2
    groups = blk_count // 2
    straight = [(d, 2 * d) for d in range(groups)] + [
        (groups + d, 2 * d + 1) for d in range(groups)
    ]
    crossed = [(d, 2 * d + 1) for d in range(groups)] + [
        (groups + d, 2 * d) for d in range(groups)
    ]
    first = lax.ppermute(jnp.where(low_side, left, right), "blk", straight)
    second = lax.ppermute(jnp.where(low_side, right, left), "blk", crossed)
    key_columns = jnp.where(core == 0, first, second)
    value_columns = jnp.where(core == 0, second, first)
    projection = jnp.concatenate([query_weight, key_columns, value_columns], axis=1)

    normed = norm_rows(inputs, attention_gain[:, None], 0)
    projected = across(projection, normed).astype(bf16)
    length = cache_lengths[req_index]
    frequency = rope_base ** (
        -2.0 * jnp.arange(HEAD_WIDTH // 2, dtype=f32) / HEAD_WIDTH
    )
    position = length + jnp.arange(steps, dtype=jnp.int32)
    angles = position.astype(f32)[:, None] * frequency
    cosine = jnp.repeat(jnp.cos(angles).T, rows, axis=1)
    sine = jnp.repeat(jnp.sin(angles).T, rows, axis=1)

    parent = jnp.concatenate(
        [
            jnp.full((rows,), -1, jnp.int32),
            jnp.arange(rows, dtype=jnp.int32) // BEAMS * BEAMS + beam_mine,
        ]
    )[None]
    parts = attend(
        jnp.stack([length, q_index, x_index]).astype(jnp.int32),
        parent,
        cosine,
        sine,
        group_parts(lambda d: projected, 1),
        caches,
    )
    met = jnp.stack(group_parts(lambda d: parts[d], 1))
    levels = sum(
        met[:, :, span + i * heads_here : span + (i + 1) * heads_here].astype(f32)
        for i in range(3)
    )
    shares = jnp.exp(levels - jnp.max(levels, axis=0, keepdims=True))
    shares = shares / jnp.sum(shares, axis=0, keepdims=True)
    heads = (
        jnp.sum(
            shares[..., None]
            * met[:, :, :span].reshape(SIDE, subset, heads_here, HEAD_WIDTH).astype(f32),
            axis=0,
        )
        .astype(bf16)
        .reshape(subset, span)
    )

    all_heads = jnp.concatenate(
        in_order(group_parts(lambda d: heads, SIDE), x_index), axis=1
    )
    residual = lax.dynamic_slice(
        inputs, (x_index * span, q_index * subset), (span, subset)
    ).T
    attended_part = (residual.astype(f32) + dot(all_heads, output_columns)).astype(bf16)
    gate_here, up_here, down_here, attended_part = lax.optimization_barrier(
        (expert_gate[0], expert_up[0], expert_down[0], attended_part)
    )
    blocks = [gate_here, up_here, down_here]
    expert_blocks = blocks + [lax.ppermute(b, "blk", partners(1)) for b in blocks]
    attended = (
        to_all(attended_part, "blk")
        .reshape(SIDE, SIDE, subset, span)
        .transpose(1, 2, 0, 3)
        .reshape(total, width)
    )
    normed_h = norm_rows(attended, feedforward_gain, 1)

    per_req = E // req_count
    slot_ids = jnp.arange(req_count, dtype=jnp.int32)
    holder = jnp.sum(
        jnp.where(migration[None, :] == slot_ids[:, None], slot_ids[None, :], 0), axis=1
    )
    owned = jnp.arange(per_req, dtype=jnp.int32) + req_index * per_req
    named_all = jnp.any(
        routes_all.reshape(1, req_count, TOPK, steps, rows) == owned[:, None, None, None, None],
        axis=2,
    )
    before = (
        jnp.arange(rows, dtype=jnp.int32)[:, None] < jnp.arange(rows, dtype=jnp.int32)[None, :]
    ).astype(bf16)
    rank_all = dot(named_all.astype(bf16).reshape(-1, rows), before).reshape(named_all.shape)
    codes = (
        jnp.where(
            named_all,
            holder[None, :, None, None] * CAP + rank_all.astype(jnp.int32),
            -1,
        )
        .transpose(0, 2, 1, 3)
        .reshape(per_req * steps, req_count * rows)
    )

    experts = jnp.arange(E, dtype=jnp.int32)
    code = lax.dynamic_index_in_dim(codes, x_index * steps + core, 0, False)
    slot_of = (
        code[None, :] == jnp.arange(req_count * CAP, dtype=jnp.int32)[:, None]
    ).astype(bf16)
    routes_step = lax.dynamic_slice_in_dim(routes_all, core * rows, rows, 2)
    named_rows = (
        jnp.any(routes_step.transpose(0, 2, 1)[..., None] == experts, axis=2)
        .astype(bf16)
        .reshape(req_count * rows, E)
    )
    named_slots = dot(slot_of, named_rows)

    def of_step(a):
        return lax.dynamic_slice_in_dim(a, core * rows, rows, 0)

    def of_expert(a):
        return lax.dynamic_index_in_dim(a.reshape(rows, req_count, per_req), x_index, 2, False).T

    named_step = jnp.any(of_step(routes_mine)[:, :, None] == experts, axis=1)
    rank_step = of_expert(ranks_of(named_step))
    named_here = of_expert(named_step.astype(f32)) > 0.0
    slots = jnp.arange(CAP, dtype=f32)
    dispatch = (
        (named_here[:, None, :] & (rank_step[:, None, :] == slots[None, :, None]))
        .reshape(req_count * CAP, rows)
        .astype(bf16)
    )
    sent = dot(dispatch, of_step(normed_h)).astype(bf16).reshape(req_count, CAP, width)
    arrived = lax.all_to_all(sent, "req", 0, 0, tiled=True).reshape(req_count * CAP, width)

    act = (jax.nn.silu(dot(normed_h, shared_gate)) * dot(normed_h, shared_up)).astype(bf16)
    shared_part = lax.dot_general(
        shared_down, act, (((0,), (1,)), ((), ())), preferred_element_type=f32
    ).astype(bf16)
    q_high = q_index // 2
    halves = shared_part.reshape(SIDE, 2, 2, width_local, total)
    pair = lax.dynamic_index_in_dim(halves, core, 2, False).astype(f32) + lax.ppermute(
        lax.dynamic_index_in_dim(halves, 1 - core, 2, False), "blk", partners(1)
    ).astype(f32)
    quads = pair.astype(bf16)
    over_q = (
        lax.dynamic_index_in_dim(pair, q_high, 1, False)
        + lax.ppermute(
            lax.dynamic_index_in_dim(quads, 1 - q_high, 1, False), "blk", partners(2)
        ).astype(f32)
    ).astype(bf16)
    shared = sum(
        p.astype(f32)
        for p in group_parts(
            lambda d: lax.dynamic_index_in_dim(over_q, x_index ^ d, 0, False), SIDE
        )
    )
    own = (
        lax.dynamic_slice_in_dim(attended, blk_index * width_local, width_local, 1)
        .T.astype(f32)
        + shared
    )
    arrived, own = lax.optimization_barrier((arrived, own))

    returned = lax.all_to_all(
        expert_rows(
            (req_index * per_req + x_index)[None].astype(jnp.int32),
            arrived,
            router_weight.T,
            named_slots,
            expert_blocks,
        ).reshape(blk_count, width_local, req_count * CAP),
        "blk",
        0,
        0,
        tiled=True,
    )

    outgoing = collect(slot[None], returned, codes, own)
    final = lax.all_to_all(outgoing, "req", 0, 0, tiled=True)
    return (
        jnp.sum(final.astype(f32), axis=0).T.astype(bf16).reshape(steps, rows, width_local)
    )


def solution(mesh):
    in_specs = (
        P(None, "req", "blk"),
        P(),
        P(None, "blk"),
        P(None, "blk"),
        P(None, "blk"),
        P("req", "blk", None, None),
        P(None, "blk", None),
        P(),
        P(),
        P(None, "req"),
        P(None, "req", None),
        P(),
        P(),
        P(("req", "blk"), None, None),
        P(("req", "blk"), None, None),
        P(("req", "blk"), None, None),
        P(None, "blk"),
        P(None, "blk"),
        P("blk", None),
    )
    out_specs = P(None, "req", "blk")
    return jax.shard_map(
        per_device, mesh=mesh, in_specs=in_specs, out_specs=out_specs, check_vma=False
    )
```

```python
import jax
import jax.numpy as jnp
from jax import lax
from jax.experimental import pallas as pl
from jax.experimental.pallas import tpu as pltpu
from jax.sharding import PartitionSpec as P

QUERY_HEADS = 20
KEY_VALUE_HEADS = 4
HEAD_WIDTH = 128
E = 64
TOPK = 6
BEAMS = 8
CAP = 16
PAGE = 128

epsilon = 1e-05
rope_base = 500000.0
masked_floor = -1e30

bf16 = jnp.bfloat16
f32 = jnp.float32

SIDE = 4
QUAD = [[SIDE * i + k for k in range(SIDE)] for i in range(SIDE)]


def dot(a, b):
    return jnp.dot(a, b, preferred_element_type=f32)


def to_all(piece, axis):
    count = lax.axis_size(axis)
    copies = jnp.broadcast_to(piece[None], (count,) + piece.shape)
    return lax.all_to_all(copies, axis, 0, 0, tiled=True)


def partners(distance):
    return [(d, d ^ distance) for d in range(SIDE * SIDE)]


def group_parts(piece_for, stride):
    return [piece_for(0)] + [
        lax.ppermute(piece_for(d), "blk", partners(d * stride)) for d in range(1, SIDE)
    ]


def in_order(parts, index):
    odd = index % 2 == 1
    upper = index // 2 == 1
    a, b, c, d = parts
    a, b = jnp.where(odd, b, a), jnp.where(odd, a, b)
    c, d = jnp.where(odd, d, c), jnp.where(odd, c, d)
    return [
        jnp.where(upper, c, a),
        jnp.where(upper, d, b),
        jnp.where(upper, a, c),
        jnp.where(upper, b, d),
    ]


def norm_rows(rows, gain, axis):
    wide = rows.astype(f32)
    inverse = lax.rsqrt(jnp.mean(wide * wide, axis=axis, keepdims=True) + epsilon)
    return (wide * inverse * gain).astype(bf16)


def three_parts(value):
    high = value.astype(bf16)
    rest = value - high.astype(f32)
    middle = rest.astype(bf16)
    low = (rest - middle.astype(f32)).astype(bf16)
    return high, middle, low


def rotated(vectors, cosine, sine):
    half = vectors.shape[0] // 2
    a = vectors[:half].astype(f32)
    b = vectors[half:].astype(f32)
    return jnp.concatenate([a * cosine - b * sine, b * cosine + a * sine], axis=0)


def across(a, b):
    return lax.dot_general(a, b, (((0,), (0,)), ((), ())), preferred_element_type=f32)


def payload_kernel(x, routes, beams, out, lines):
    total, width = x.shape
    rows = total // 2
    part = rows // SIDE
    main = width // 128 * 128
    ordered = jnp.concatenate(
        [
            x[t * rows + q * part : t * rows + (q + 1) * part, :]
            for q in range(SIDE)
            for t in (0, 1)
        ],
        axis=0,
    ).astype(f32)
    lines[:main, :] = ordered[:, :main].T.astype(bf16)
    rest = jnp.concatenate(
        [ordered[:, main:], jnp.zeros((total, 128 - width + main), f32)], axis=1
    )
    lines[main:width, :] = rest.T[: width - main].astype(bf16)
    none = jnp.zeros((1, rows), jnp.int32)
    by_step = [
        jnp.concatenate([routes[k, t : t + 1, :] for k in range(TOPK)] + [last, none], axis=0)
        for t, last in ((0, none), (1, beams[...]))
    ]
    extra = jnp.concatenate(
        [
            by_step[t][:, q * part : (q + 1) * part]
            for q in range(SIDE)
            for t in (0, 1)
        ],
        axis=1,
    )
    lines[width:, :] = extra.astype(f32).astype(bf16)
    for i in range(out.shape[0]):
        out[i] = lines[...]


def payloads(count, x, routes, beams):
    total, width = x.shape
    vmem = pl.BlockSpec(memory_space=pltpu.VMEM)
    return pl.pallas_call(
        payload_kernel,
        out_shape=jax.ShapeDtypeStruct((count, width + TOPK + 2, total), bf16),
        in_specs=[vmem] * 3,
        out_specs=vmem,
        scratch_shapes=[pltpu.VMEM((width + TOPK + 2, total), bf16)],
        name="payload",
    )(x, routes, beams)


def attention_kernel(
    scalars, parent, cosine, sine, p0, p1, p2, p3, c0, c1, c2, c3,
    o0, o1, o2, o3, query_rows, key_rows, value_rows, bias, scores, stats, joined,
):
    length = scalars[0]
    q_index = scalars[1]
    x_index = scalars[2]
    features, total = p0.shape
    span = query_rows.shape[0]
    share = span // SIDE
    half = HEAD_WIDTH // SIDE
    for d, piece in enumerate((p0, p1, p2, p3)):
        source = q_index ^ d
        query_rows[pl.ds(pl.multiple_of(source * share, half), share), :] = piece[:share, :]
        key_rows[pl.ds(pl.multiple_of(source * half, half), half), :] = piece[
            share : share + half, :
        ]
        value_rows[pl.ds(pl.multiple_of(source * half, half), half), :] = piece[
            share + half :, :
        ]
    cos = cosine[...]
    sin = sine[...]
    new_keys = rotated(key_rows[...], cos, sin).T.astype(bf16)
    new_values = value_rows[...]
    caches = (c0, c1, c2, c3)
    held = c0.shape[0]
    line = lax.broadcasted_iota(jnp.int32, (held, total), 0)
    spread = line + (line // PAGE) * (SIDE * SIDE - 1) * PAGE
    for d in range(SIDE):
        column = (x_index ^ d) * SIDE + q_index
        bias[d * held : (d + 1) * held, :] = jnp.where(
            spread + column * PAGE < length, 0.0, masked_floor
        )
    key_id = lax.broadcasted_iota(jnp.int32, (total, total), 0)
    row_id = lax.broadcasted_iota(jnp.int32, (total, total), 1)
    near = ((key_id == row_id) | (key_id == parent[...])) & (
        key_id // (total // SIDE) == q_index
    )
    bias[SIDE * held :, :] = jnp.where(near, 0.0, masked_floor)
    stats[...] = jnp.zeros(stats.shape, f32)
    scale = HEAD_WIDTH ** (-0.5)
    heads_here = span // HEAD_WIDTH
    for h in range(heads_here):
        query = rotated(
            query_rows[h * HEAD_WIDTH : (h + 1) * HEAD_WIDTH, :], cos, sin
        ).astype(bf16)
        for d, cache in enumerate(caches):
            scores[d * held : (d + 1) * held, :] = (
                dot(cache[:, :HEAD_WIDTH], query) * scale
                + bias[d * held : (d + 1) * held, :]
            )
        scores[SIDE * held :, :] = dot(new_keys, query) * scale + bias[SIDE * held :, :]
        peak = jnp.max(scores[...], axis=0, keepdims=True)
        mass = jnp.zeros((1, total), f32)
        weighted = jnp.zeros((HEAD_WIDTH, total), f32)
        for d, cache in enumerate(caches):
            raised = jnp.exp(scores[d * held : (d + 1) * held, :] - peak)
            mass = mass + jnp.sum(raised, axis=0, keepdims=True)
            weighted = weighted + across(cache[:, HEAD_WIDTH:], raised.astype(bf16))
        raised = jnp.exp(scores[SIDE * held :, :] - peak)
        mass = mass + jnp.sum(raised, axis=0, keepdims=True)
        weighted = weighted + dot(new_values, raised.astype(bf16))
        joined[:, h * HEAD_WIDTH : (h + 1) * HEAD_WIDTH] = (weighted / mass).T.astype(bf16)
        level = jnp.where(peak > 0.5 * masked_floor, peak + jnp.log(mass), masked_floor)
        for i, part in enumerate(three_parts(level)):
            place = i * heads_here + h
            stats[place : place + 1, :] = part.astype(f32)
    joined[:, span:] = stats[...].T.astype(bf16)
    subset = total // SIDE
    for d, out in enumerate((o0, o1, o2, o3)):
        out[...] = joined[pl.ds(pl.multiple_of((q_index ^ d) * subset, subset), subset), :]


def attend(scalars, parent, cosine, sine, pieces, caches):
    total = pieces[0].shape[1]
    subset = total // SIDE
    span = QUERY_HEADS // KEY_VALUE_HEADS * HEAD_WIDTH
    keys = SIDE * caches[0].shape[0] + total
    vmem = pl.BlockSpec(memory_space=pltpu.VMEM)
    return pl.pallas_call(
        attention_kernel,
        out_shape=[jax.ShapeDtypeStruct((subset, span + HEAD_WIDTH), bf16)] * SIDE,
        in_specs=[pl.BlockSpec(memory_space=pltpu.SMEM)] + [vmem] * (3 + 2 * SIDE),
        out_specs=[vmem] * SIDE,
        scratch_shapes=[
            pltpu.VMEM((span, total), bf16),
            pltpu.VMEM((HEAD_WIDTH, total), bf16),
            pltpu.VMEM((HEAD_WIDTH, total), bf16),
            pltpu.VMEM((keys, total), f32),
            pltpu.VMEM((keys, total), f32),
            pltpu.VMEM((HEAD_WIDTH, total), f32),
            pltpu.VMEM((total, span + HEAD_WIDTH), bf16),
        ],
        compiler_params=pltpu.CompilerParams(vmem_limit_bytes=24 << 20),
        name="attention",
    )(scalars, parent, cosine, sine, *pieces, *caches)


def spread_kernel(pieces, gain, dispatch, attended, normed, sent):
    count, part, span = pieces.shape
    for x in range(count // SIDE):
        for q in range(SIDE):
            attended[q * part : (q + 1) * part, x * span : (x + 1) * span] = pieces[
                SIDE * x + q
            ]
    normed[...] = norm_rows(attended[...], gain[...], 1)
    sent[...] = dot(dispatch[...], normed[...]).astype(bf16)


def spread(pieces, gain, dispatch):
    count, part, span = pieces.shape
    width = count // SIDE * span
    vmem = pl.BlockSpec(memory_space=pltpu.VMEM)
    return pl.pallas_call(
        spread_kernel,
        out_shape=[
            jax.ShapeDtypeStruct((SIDE * part, width), bf16),
            jax.ShapeDtypeStruct((SIDE * part, width), bf16),
            jax.ShapeDtypeStruct((dispatch.shape[0], width), bf16),
        ],
        in_specs=[vmem] * 3,
        out_specs=[vmem] * 3,
        name="spread",
    )(pieces, gain, dispatch)


def expert_kernel(
    expert, rows, router, named, g0, u0, d0, g1, u1, d1, out,
    gate_w, up_w, down_w, result, sems, out_sems,
):
    copies = []
    for i, (g, u, d) in enumerate(((g0, u0, d0), (g1, u1, d1))):
        copies.append(
            [
                pltpu.make_async_copy(src, dst.at[i], sems.at[3 * i + k])
                for k, (src, dst) in enumerate(((g, gate_w), (u, up_w), (d, down_w)))
            ]
        )
    order = [(0, 0), (0, 1), (1, 0), (1, 1), (0, 2), (1, 2)]
    for i, k in order:
        copies[i][k].start()
    width = down_w.shape[2]
    logits = lax.dot_general(
        rows[...], router[...], (((1,), (1,)), ((), ())), preferred_element_type=f32
    )
    raised = jnp.where(named[...] > 0.0, jnp.exp(logits), 0.0)
    column = lax.broadcasted_iota(jnp.int32, raised.shape, 1)
    total = jnp.sum(raised, axis=1, keepdims=True)
    picked = jnp.sum(jnp.where(column == expert[0], raised, 0.0), axis=1, keepdims=True)
    weight = picked / jnp.where(total > 0.0, total, 1.0)
    hidden = []
    for i in (0, 1):
        copies[i][0].wait()
        gated = dot(rows[...], gate_w[i])
        copies[i][1].wait()
        lifted = dot(rows[...], up_w[i])
        hidden.append((gated / (1.0 + jnp.exp(-gated)) * lifted).astype(bf16))
    copies[0][2].wait()
    copies[1][2].wait()
    step = width // out_sems.shape[0]
    stores = []
    for n in range(width // step):
        part = dot(hidden[0], down_w[0, :, n * step : (n + 1) * step]) + dot(
            hidden[1], down_w[1, :, n * step : (n + 1) * step]
        )
        span = slice(n * step, (n + 1) * step)
        result[span, :] = (part * weight).T.astype(bf16)
        stores.append(
            pltpu.make_async_copy(result.at[span, :], out.at[span, :], out_sems.at[n])
        )
        stores[-1].start()
    for store in stores:
        store.wait()


def expert_rows(expert, rows, router, named, blocks):
    count, width = rows.shape
    units = blocks[0].shape[1]
    vmem = pl.BlockSpec(memory_space=pltpu.VMEM)
    hbm = pl.BlockSpec(memory_space=pltpu.HBM)
    return pl.pallas_call(
        expert_kernel,
        out_shape=jax.ShapeDtypeStruct((width, count), bf16),
        in_specs=[pl.BlockSpec(memory_space=pltpu.SMEM)] + [vmem] * 3 + [hbm] * 6,
        out_specs=hbm,
        scratch_shapes=[
            pltpu.VMEM((2, width, units), bf16),
            pltpu.VMEM((2, width, units), bf16),
            pltpu.VMEM((2, units, width), bf16),
            pltpu.VMEM((width, count), bf16),
            pltpu.SemaphoreType.DMA((6,)),
            pltpu.SemaphoreType.DMA((5,)),
        ],
        compiler_params=pltpu.CompilerParams(vmem_limit_bytes=40 << 20),
        name="experts",
    )(
        expert,
        rows,
        router,
        named,
        *[pltpu.with_memory_space_constraint(b, pltpu.HBM) for b in blocks],
    )


def collect_kernel(slot, returned, codes, own, out, sums):
    groups, width, count = returned.shape
    slots, _, total = out.shape
    rows = total // 2
    lines = lax.broadcasted_iota(jnp.int32, (count, slots * rows), 0)
    by_step = []
    for c in (0, 1):
        acc = jnp.zeros((2 * width, slots * rows), f32)
        for x in range(SIDE):
            pick = jnp.where(
                lines == codes[2 * x + c : 2 * x + c + 1, :], 1.0, 0.0
            ).astype(bf16)
            pair = jnp.concatenate(
                [returned[SIDE * x + c], returned[SIDE * x + 2 + c]], axis=0
            )
            acc = acc + dot(pair, pick)
        by_step.append(acc[:width] + acc[width:])
    lane = lax.broadcasted_iota(jnp.int32, (width, total), 1)
    for pair in range(slots // 2):
        a = by_step[0][:, pair * total : (pair + 1) * total]
        b = by_step[1][:, pair * total : (pair + 1) * total]
        sums[2 * pair] = jnp.where(lane < rows, a, pltpu.roll(b, rows, 1))
        sums[2 * pair + 1] = jnp.where(lane < rows, pltpu.roll(a, rows, 1), b)
    sums[slot[0]] = sums[slot[0]] + own[...]
    out[...] = sums[...].astype(bf16)


def collect(slot, returned, codes, own):
    groups, width, _ = returned.shape
    shape = (groups, width, own.shape[1])
    vmem = pl.BlockSpec(memory_space=pltpu.VMEM)
    return pl.pallas_call(
        collect_kernel,
        out_shape=jax.ShapeDtypeStruct(shape, bf16),
        in_specs=[pl.BlockSpec(memory_space=pltpu.SMEM)] + [vmem] * 3,
        out_specs=vmem,
        scratch_shapes=[pltpu.VMEM(shape, f32)],
        compiler_params=pltpu.CompilerParams(vmem_limit_bytes=32 << 20),
        name="collect",
    )(slot, returned, codes, own)


def ranks_of(named):
    rows = named.shape[-2]
    lower = (
        jnp.arange(rows, dtype=jnp.int32)[:, None] > jnp.arange(rows, dtype=jnp.int32)[None, :]
    ).astype(bf16)
    return jnp.einsum("ij,...je->...ie", lower, named.astype(bf16), preferred_element_type=f32)


def per_device(
    step_inputs,
    attention_gain,
    query_weight,
    key_value_weight,
    output_weight,
    prompt_cache,
    page_table,
    cache_lengths,
    migration,
    parents,
    routes,
    feedforward_gain,
    router_weight,
    expert_gate,
    expert_up,
    expert_down,
    shared_gate,
    shared_up,
    shared_down,
):
    req_count = lax.axis_size("req")
    blk_count = lax.axis_size("blk")
    req_index = lax.axis_index("req")
    blk_index = lax.axis_index("blk")
    x_index = blk_index // SIDE
    q_index = blk_index % SIDE
    core = blk_index % 2
    steps, rows, width_local = step_inputs.shape
    total = steps * rows
    width = width_local * blk_count
    heads_here = QUERY_HEADS // KEY_VALUE_HEADS
    span = heads_here * HEAD_WIDTH
    subset = total // SIDE

    payload = payloads(
        req_count,
        step_inputs.reshape(total, width_local),
        routes.transpose(2, 0, 1),
        parents,
    )
    prompt, payload = lax.optimization_barrier((prompt_cache[0], payload))
    by_slot = lax.all_to_all(payload, "req", 0, 0, tiled=True)
    slot = migration[req_index]
    mine = lax.dynamic_index_in_dim(by_slot, slot, 0, False)
    part = rows // SIDE
    routes_all = (
        by_slot[:, width_local : width_local + TOPK]
        .astype(jnp.int32)
        .reshape(req_count, TOPK, SIDE, steps, part)
        .transpose(0, 1, 3, 2, 4)
        .reshape(req_count, TOPK, total)
    )
    routes_mine = lax.dynamic_index_in_dim(routes_all, slot, 0, False).T
    beam_mine = mine[width_local + TOPK].astype(jnp.int32)
    inputs = to_all(mine[:width_local], "blk").reshape(width, total)

    output_columns = lax.all_gather(
        output_weight, "blk", axis=1, tiled=True, axis_index_groups=QUAD
    )

    order = lax.dynamic_index_in_dim(page_table, req_index, 0, False)[0]
    pages = prompt[order]
    pages_local = pages.shape[0]
    by_head = (
        pages.reshape(pages_local * PAGE, 2, KEY_VALUE_HEADS, HEAD_WIDTH)
        .transpose(2, 0, 1, 3)
        .reshape(KEY_VALUE_HEADS, pages_local * PAGE, 2 * HEAD_WIDTH)
    )
    key_value_weight, by_head = lax.optimization_barrier((key_value_weight, by_head))
    caches = group_parts(
        lambda d: lax.dynamic_index_in_dim(by_head, x_index ^ d, 0, False), SIDE
    )

    half = key_value_weight.shape[1] // 2
    left, right = key_value_weight[:, :half], key_value_weight[:, half:]
    low_side = blk_index < blk_count // 2
    groups = blk_count // 2
    straight = [(d, 2 * d) for d in range(groups)] + [
        (groups + d, 2 * d + 1) for d in range(groups)
    ]
    crossed = [(d, 2 * d + 1) for d in range(groups)] + [
        (groups + d, 2 * d) for d in range(groups)
    ]
    first = lax.ppermute(jnp.where(low_side, left, right), "blk", straight)
    second = lax.ppermute(jnp.where(low_side, right, left), "blk", crossed)
    key_columns = jnp.where(core == 0, first, second)
    value_columns = jnp.where(core == 0, second, first)
    projection = jnp.concatenate([query_weight, key_columns, value_columns], axis=1)

    normed = norm_rows(inputs, attention_gain[:, None], 0)
    projected = across(projection, normed).astype(bf16)
    length = cache_lengths[req_index]
    frequency = rope_base ** (
        -2.0 * jnp.arange(HEAD_WIDTH // 2, dtype=f32) / HEAD_WIDTH
    )
    position = length + jnp.arange(steps, dtype=jnp.int32)
    angles = position.astype(f32)[:, None] * frequency
    cosine = jnp.tile(jnp.repeat(jnp.cos(angles).T, part, axis=1), (1, SIDE))
    sine = jnp.tile(jnp.repeat(jnp.sin(angles).T, part, axis=1), (1, SIDE))

    line = jnp.arange(total, dtype=jnp.int32)
    parent = jnp.where(
        line // part % steps == 1,
        line // subset * subset + line % part // BEAMS * BEAMS + beam_mine,
        -1,
    )[None]
    parts = attend(
        jnp.stack([length, q_index, x_index]).astype(jnp.int32),
        parent,
        cosine,
        sine,
        group_parts(lambda d: projected, 1),
        caches,
    )
    met = jnp.stack(group_parts(lambda d: parts[d], 1))
    levels = sum(
        met[:, :, span + i * heads_here : span + (i + 1) * heads_here].astype(f32)
        for i in range(3)
    )
    shares = jnp.exp(levels - jnp.max(levels, axis=0, keepdims=True))
    shares = shares / jnp.sum(shares, axis=0, keepdims=True)
    heads = (
        jnp.sum(
            shares[..., None]
            * met[:, :, :span].reshape(SIDE, subset, heads_here, HEAD_WIDTH).astype(f32),
            axis=0,
        )
        .astype(bf16)
        .reshape(subset, span)
    )

    all_heads = jnp.concatenate(
        in_order(group_parts(lambda d: heads, SIDE), x_index), axis=1
    )
    residual = lax.dynamic_slice(
        inputs, (x_index * span, q_index * subset), (span, subset)
    ).T
    attended_part = (residual.astype(f32) + dot(all_heads, output_columns)).astype(bf16)
    gate_here, up_here, down_here, attended_part = lax.optimization_barrier(
        (expert_gate[0], expert_up[0], expert_down[0], attended_part)
    )
    blocks = [gate_here, up_here, down_here]
    expert_blocks = blocks + [lax.ppermute(b, "blk", partners(1)) for b in blocks]
    to_core = jnp.broadcast_to(
        attended_part.reshape(1, steps, part, span), (blk_count // 2, steps, part, span)
    ).reshape(blk_count, part, span)
    attended_pieces = lax.all_to_all(to_core, "blk", 0, 0, tiled=True)

    per_req = E // req_count
    slot_ids = jnp.arange(req_count, dtype=jnp.int32)
    holder = jnp.sum(
        jnp.where(migration[None, :] == slot_ids[:, None], slot_ids[None, :], 0), axis=1
    )
    owned = jnp.arange(per_req, dtype=jnp.int32) + req_index * per_req
    named_all = jnp.any(
        routes_all.reshape(1, req_count, TOPK, steps, rows) == owned[:, None, None, None, None],
        axis=2,
    )
    before = (
        jnp.arange(rows, dtype=jnp.int32)[:, None] < jnp.arange(rows, dtype=jnp.int32)[None, :]
    ).astype(bf16)
    rank_all = dot(named_all.astype(bf16).reshape(-1, rows), before).reshape(named_all.shape)
    codes = (
        jnp.where(
            named_all,
            holder[None, :, None, None] * CAP + rank_all.astype(jnp.int32),
            -1,
        )
        .transpose(0, 2, 1, 3)
        .reshape(per_req * steps, req_count * rows)
    )

    experts = jnp.arange(E, dtype=jnp.int32)
    code = lax.dynamic_index_in_dim(codes, x_index * steps + core, 0, False)
    slot_of = (
        code[None, :] == jnp.arange(req_count * CAP, dtype=jnp.int32)[:, None]
    ).astype(bf16)
    routes_step = lax.dynamic_slice_in_dim(routes_all, core * rows, rows, 2)
    named_rows = (
        jnp.any(routes_step.transpose(0, 2, 1)[..., None] == experts, axis=2)
        .astype(bf16)
        .reshape(req_count * rows, E)
    )
    named_slots = dot(slot_of, named_rows)

    def of_step(a):
        return lax.dynamic_slice_in_dim(a, core * rows, rows, 0)

    def of_expert(a):
        return lax.dynamic_index_in_dim(a.reshape(rows, req_count, per_req), x_index, 2, False).T

    named_step = jnp.any(of_step(routes_mine)[:, :, None] == experts, axis=1)
    rank_step = of_expert(ranks_of(named_step))
    named_here = of_expert(named_step.astype(f32)) > 0.0
    slots = jnp.arange(CAP, dtype=f32)
    dispatch = (
        (named_here[:, None, :] & (rank_step[:, None, :] == slots[None, :, None]))
        .reshape(req_count * CAP, rows)
        .astype(bf16)
    )
    attended, normed_h, sent = spread(attended_pieces, feedforward_gain[None], dispatch)
    arrived = lax.all_to_all(
        sent.reshape(req_count, CAP, width), "req", 0, 0, tiled=True
    ).reshape(req_count * CAP, width)

    other = lax.ppermute(normed_h, "blk", partners(1))
    act = [
        (jax.nn.silu(dot(h, shared_gate)) * dot(h, shared_up)).astype(bf16)
        for h in (normed_h, other)
    ]

    def by_step(here, there):
        return jnp.concatenate(
            [jnp.where(core == 0, here, there), jnp.where(core == 0, there, here)], axis=0
        )

    act = by_step(*act)
    shared_part = lax.dot_general(
        shared_down, act, (((0,), (1,)), ((), ())), preferred_element_type=f32
    ).astype(bf16)
    q_high = q_index // 2
    halves = shared_part.reshape(SIDE, 2, 2, width_local, total)
    pair = (
        lax.dynamic_index_in_dim(halves, core, 2, False).astype(f32)
        + lax.ppermute(
            lax.dynamic_index_in_dim(halves, 1 - core, 2, False), "blk", partners(1)
        ).astype(f32)
    ).astype(bf16)
    over_x = sum(
        p.astype(f32)
        for p in group_parts(
            lambda d: lax.dynamic_index_in_dim(pair, x_index ^ d, 0, False), SIDE
        )
    )
    shared = lax.dynamic_index_in_dim(over_x, q_high, 0, False) + lax.ppermute(
        lax.dynamic_index_in_dim(over_x, 1 - q_high, 0, False).astype(bf16),
        "blk",
        partners(2),
    ).astype(f32)

    def columns_of(b):
        return lax.dynamic_slice_in_dim(attended, b * width_local, width_local, 1)

    own = (
        by_step(
            columns_of(blk_index),
            lax.ppermute(columns_of(blk_index ^ 1), "blk", partners(1)),
        ).T.astype(f32)
        + shared
    )
    arrived, own = lax.optimization_barrier((arrived, own))

    returned = lax.all_to_all(
        expert_rows(
            (req_index * per_req + x_index)[None].astype(jnp.int32),
            arrived,
            router_weight.T,
            named_slots,
            expert_blocks,
        ).reshape(blk_count, width_local, req_count * CAP),
        "blk",
        0,
        0,
        tiled=True,
    )

    outgoing = collect(slot[None], returned, codes, own)
    final = lax.all_to_all(outgoing, "req", 0, 0, tiled=True)
    return (
        jnp.sum(final.astype(f32), axis=0).T.astype(bf16).reshape(steps, rows, width_local)
    )


def solution(mesh):
    in_specs = (
        P(None, "req", "blk"),
        P(),
        P(None, "blk"),
        P(None, "blk"),
        P(None, "blk"),
        P("req", "blk", None, None),
        P(None, "blk", None),
        P(),
        P(),
        P(None, "req"),
        P(None, "req", None),
        P(),
        P(),
        P(("req", "blk"), None, None),
        P(("req", "blk"), None, None),
        P(("req", "blk"), None, None),
        P(None, "blk"),
        P(None, "blk"),
        P("blk", None),
    )
    out_specs = P(None, "req", "blk")
    return jax.shard_map(
        per_device, mesh=mesh, in_specs=in_specs, out_specs=out_specs, check_vma=False
    )
```

```python
import jax
import jax.numpy as jnp
from jax import lax
from jax.experimental import pallas as pl
from jax.experimental.pallas import tpu as pltpu
from jax.sharding import PartitionSpec as P

QUERY_HEADS = 20
KEY_VALUE_HEADS = 4
HEAD_WIDTH = 128
E = 64
TOPK = 6
BEAMS = 8
CAP = 16
PAGE = 128

epsilon = 1e-05
rope_base = 500000.0
masked_floor = -1e30

bf16 = jnp.bfloat16
f32 = jnp.float32

SIDE = 4
QUAD = [[SIDE * i + k for k in range(SIDE)] for i in range(SIDE)]


def dot(a, b):
    return jnp.dot(a, b, preferred_element_type=f32)


def to_all(piece, axis):
    count = lax.axis_size(axis)
    copies = jnp.broadcast_to(piece[None], (count,) + piece.shape)
    return lax.all_to_all(copies, axis, 0, 0, tiled=True)


def partners(distance):
    return [(d, d ^ distance) for d in range(SIDE * SIDE)]


def group_parts(piece_for, stride):
    return [piece_for(0)] + [
        lax.ppermute(piece_for(d), "blk", partners(d * stride)) for d in range(1, SIDE)
    ]


def in_order(parts, index):
    odd = index % 2 == 1
    upper = index // 2 == 1
    a, b, c, d = parts
    a, b = jnp.where(odd, b, a), jnp.where(odd, a, b)
    c, d = jnp.where(odd, d, c), jnp.where(odd, c, d)
    return [
        jnp.where(upper, c, a),
        jnp.where(upper, d, b),
        jnp.where(upper, a, c),
        jnp.where(upper, b, d),
    ]


def norm_rows(rows, gain, axis):
    wide = rows.astype(f32)
    inverse = lax.rsqrt(jnp.mean(wide * wide, axis=axis, keepdims=True) + epsilon)
    return (wide * inverse * gain).astype(bf16)


def three_parts(value):
    high = value.astype(bf16)
    rest = value - high.astype(f32)
    middle = rest.astype(bf16)
    low = (rest - middle.astype(f32)).astype(bf16)
    return high, middle, low


def rotated(vectors, cosine, sine):
    half = vectors.shape[0] // 2
    a = vectors[:half].astype(f32)
    b = vectors[half:].astype(f32)
    return jnp.concatenate([a * cosine - b * sine, b * cosine + a * sine], axis=0)


def across(a, b):
    return lax.dot_general(a, b, (((0,), (0,)), ((), ())), preferred_element_type=f32)


def payload_kernel(x, routes, beams, out, lines):
    total, width = x.shape
    rows = total // 2
    part = rows // SIDE
    main = width // 128 * 128
    ordered = jnp.concatenate(
        [
            x[t * rows + q * part : t * rows + (q + 1) * part, :]
            for q in range(SIDE)
            for t in (0, 1)
        ],
        axis=0,
    ).astype(f32)
    lines[:main, :] = ordered[:, :main].T.astype(bf16)
    rest = jnp.concatenate(
        [ordered[:, main:], jnp.zeros((total, 128 - width + main), f32)], axis=1
    )
    lines[main:width, :] = rest.T[: width - main].astype(bf16)
    none = jnp.zeros((1, rows), jnp.int32)
    by_step = [
        jnp.concatenate([routes[k, t : t + 1, :] for k in range(TOPK)] + [last, none], axis=0)
        for t, last in ((0, none), (1, beams[...]))
    ]
    extra = jnp.concatenate(
        [
            by_step[t][:, q * part : (q + 1) * part]
            for q in range(SIDE)
            for t in (0, 1)
        ],
        axis=1,
    )
    lines[width:, :] = extra.astype(f32).astype(bf16)
    for i in range(out.shape[0]):
        out[i] = lines[...]


def payloads(count, x, routes, beams):
    total, width = x.shape
    vmem = pl.BlockSpec(memory_space=pltpu.VMEM)
    return pl.pallas_call(
        payload_kernel,
        out_shape=jax.ShapeDtypeStruct((count, width + TOPK + 2, total), bf16),
        in_specs=[vmem] * 3,
        out_specs=vmem,
        scratch_shapes=[pltpu.VMEM((width + TOPK + 2, total), bf16)],
        compiler_params=pltpu.CompilerParams(vmem_limit_bytes=4 << 20),
        name="payload",
    )(x, routes, beams)


def project_kernel(core, x, gain, query, first, second, out, normed):
    width = x.shape[0]
    wide = x[...].astype(f32)
    inverse = lax.rsqrt(jnp.sum(wide * wide, axis=0, keepdims=True) / width + epsilon)
    gains = gain[...].T
    for i in range(width // 128):
        rows = slice(i * 128, (i + 1) * 128)
        normed[rows, :] = (
            x[rows, :].astype(f32) * inverse * gains[:, i : i + 1]
        ).astype(bf16)
    share = query.shape[0]
    half = first.shape[0]
    out[:share, :] = dot(query[...], normed[...]).astype(bf16)
    a = dot(first[...], normed[...])
    b = dot(second[...], normed[...])
    even = core[0] == 0
    out[share : share + half, :] = jnp.where(even, a, b).astype(bf16)
    out[share + half :, :] = jnp.where(even, b, a).astype(bf16)


def project(core, x, gain, query, first, second):
    vmem = pl.BlockSpec(memory_space=pltpu.VMEM)
    share = query.shape[0] + 2 * first.shape[0]
    return pl.pallas_call(
        project_kernel,
        out_shape=jax.ShapeDtypeStruct((share, x.shape[1]), bf16),
        in_specs=[pl.BlockSpec(memory_space=pltpu.SMEM)] + [vmem] * 5,
        out_specs=vmem,
        scratch_shapes=[pltpu.VMEM(x.shape, bf16)],
        compiler_params=pltpu.CompilerParams(vmem_limit_bytes=10 << 20),
        name="project",
    )(core, x, gain, query, first, second)


def attention_kernel(
    scalars, parent, cosine, sine, p0, p1, p2, p3, c0, c1, c2, c3,
    o0, o1, o2, o3, query_rows, key_rows, value_rows, bias, scores, stats, joined,
):
    length = scalars[0]
    q_index = scalars[1]
    x_index = scalars[2]
    features, total = p0.shape
    span = query_rows.shape[0]
    share = span // SIDE
    half = HEAD_WIDTH // SIDE
    for d, piece in enumerate((p0, p1, p2, p3)):
        source = q_index ^ d
        query_rows[pl.ds(pl.multiple_of(source * share, half), share), :] = piece[:share, :]
        key_rows[pl.ds(pl.multiple_of(source * half, half), half), :] = piece[
            share : share + half, :
        ]
        value_rows[pl.ds(pl.multiple_of(source * half, half), half), :] = piece[
            share + half :, :
        ]
    cos = cosine[...]
    sin = sine[...]
    new_keys = rotated(key_rows[...], cos, sin).T.astype(bf16)
    new_values = value_rows[...]
    caches = (c0, c1, c2, c3)
    held = c0.shape[0]
    line = lax.broadcasted_iota(jnp.int32, (held, total), 0)
    spread = line + (line // PAGE) * (SIDE * SIDE - 1) * PAGE
    for d in range(SIDE):
        column = (x_index ^ d) * SIDE + q_index
        bias[d * held : (d + 1) * held, :] = jnp.where(
            spread + column * PAGE < length, 0.0, masked_floor
        )
    key_id = lax.broadcasted_iota(jnp.int32, (total, total), 0)
    row_id = lax.broadcasted_iota(jnp.int32, (total, total), 1)
    near = ((key_id == row_id) | (key_id == parent[...])) & (
        key_id // (total // SIDE) == q_index
    )
    bias[SIDE * held :, :] = jnp.where(near, 0.0, masked_floor)
    stats[...] = jnp.zeros(stats.shape, f32)
    scale = HEAD_WIDTH ** (-0.5)
    heads_here = span // HEAD_WIDTH
    for h in range(heads_here):
        query = rotated(
            query_rows[h * HEAD_WIDTH : (h + 1) * HEAD_WIDTH, :], cos, sin
        ).astype(bf16)
        for d, cache in enumerate(caches):
            scores[d * held : (d + 1) * held, :] = (
                dot(cache[:, :HEAD_WIDTH], query) * scale
                + bias[d * held : (d + 1) * held, :]
            )
        scores[SIDE * held :, :] = dot(new_keys, query) * scale + bias[SIDE * held :, :]
        peak = jnp.max(scores[...], axis=0, keepdims=True)
        mass = jnp.zeros((1, total), f32)
        weighted = jnp.zeros((HEAD_WIDTH, total), f32)
        for d, cache in enumerate(caches):
            raised = jnp.exp(scores[d * held : (d + 1) * held, :] - peak)
            mass = mass + jnp.sum(raised, axis=0, keepdims=True)
            weighted = weighted + across(cache[:, HEAD_WIDTH:], raised.astype(bf16))
        raised = jnp.exp(scores[SIDE * held :, :] - peak)
        mass = mass + jnp.sum(raised, axis=0, keepdims=True)
        weighted = weighted + dot(new_values, raised.astype(bf16))
        joined[:, h * HEAD_WIDTH : (h + 1) * HEAD_WIDTH] = (weighted / mass).T.astype(bf16)
        level = jnp.where(peak > 0.5 * masked_floor, peak + jnp.log(mass), masked_floor)
        for i, part in enumerate(three_parts(level)):
            place = i * heads_here + h
            stats[place : place + 1, :] = part.astype(f32)
    joined[:, span:] = stats[...].T.astype(bf16)
    subset = total // SIDE
    for d, out in enumerate((o0, o1, o2, o3)):
        out[...] = joined[pl.ds(pl.multiple_of((q_index ^ d) * subset, subset), subset), :]


def attend(scalars, parent, cosine, sine, pieces, caches):
    total = pieces[0].shape[1]
    subset = total // SIDE
    span = QUERY_HEADS // KEY_VALUE_HEADS * HEAD_WIDTH
    keys = SIDE * caches[0].shape[0] + total
    vmem = pl.BlockSpec(memory_space=pltpu.VMEM)
    return pl.pallas_call(
        attention_kernel,
        out_shape=[jax.ShapeDtypeStruct((subset, span + HEAD_WIDTH), bf16)] * SIDE,
        in_specs=[pl.BlockSpec(memory_space=pltpu.SMEM)] + [vmem] * (3 + 2 * SIDE),
        out_specs=[vmem] * SIDE,
        scratch_shapes=[
            pltpu.VMEM((span, total), bf16),
            pltpu.VMEM((HEAD_WIDTH, total), bf16),
            pltpu.VMEM((HEAD_WIDTH, total), bf16),
            pltpu.VMEM((keys, total), f32),
            pltpu.VMEM((keys, total), f32),
            pltpu.VMEM((HEAD_WIDTH, total), f32),
            pltpu.VMEM((total, span + HEAD_WIDTH), bf16),
        ],
        compiler_params=pltpu.CompilerParams(vmem_limit_bytes=12 << 20),
        name="attention",
    )(scalars, parent, cosine, sine, *pieces, *caches)


def spread_kernel(pieces, gain, dispatch, attended, normed, sent):
    count, part, span = pieces.shape
    for x in range(count // SIDE):
        for q in range(SIDE):
            attended[q * part : (q + 1) * part, x * span : (x + 1) * span] = pieces[
                SIDE * x + q
            ]
    normed[...] = norm_rows(attended[...], gain[...], 1)
    sent[...] = dot(dispatch[...], normed[...]).astype(bf16)


def spread(pieces, gain, dispatch):
    count, part, span = pieces.shape
    width = count // SIDE * span
    vmem = pl.BlockSpec(memory_space=pltpu.VMEM)
    return pl.pallas_call(
        spread_kernel,
        out_shape=[
            jax.ShapeDtypeStruct((SIDE * part, width), bf16),
            jax.ShapeDtypeStruct((SIDE * part, width), bf16),
            jax.ShapeDtypeStruct((dispatch.shape[0], width), bf16),
        ],
        in_specs=[vmem] * 3,
        out_specs=[vmem] * 3,
        name="spread",
    )(pieces, gain, dispatch)


def expert_kernel(
    expert, rows, router, named, g0, u0, d0, g1, u1, d1, out,
    gate_w, up_w, down_w, result, sems, out_sems,
):
    copies = []
    for i, (g, u, d) in enumerate(((g0, u0, d0), (g1, u1, d1))):
        copies.append(
            [
                pltpu.make_async_copy(src, dst.at[i], sems.at[3 * i + k])
                for k, (src, dst) in enumerate(((g, gate_w), (u, up_w), (d, down_w)))
            ]
        )
    order = [(0, 0), (0, 1), (1, 0), (1, 1), (0, 2), (1, 2)]
    for i, k in order:
        copies[i][k].start()
    width = down_w.shape[2]
    logits = lax.dot_general(
        rows[...], router[...], (((1,), (1,)), ((), ())), preferred_element_type=f32
    )
    raised = jnp.where(named[...] > 0.0, jnp.exp(logits), 0.0)
    column = lax.broadcasted_iota(jnp.int32, raised.shape, 1)
    total = jnp.sum(raised, axis=1, keepdims=True)
    picked = jnp.sum(jnp.where(column == expert[0], raised, 0.0), axis=1, keepdims=True)
    weight = picked / jnp.where(total > 0.0, total, 1.0)
    hidden = []
    for i in (0, 1):
        copies[i][0].wait()
        gated = dot(rows[...], gate_w[i])
        copies[i][1].wait()
        lifted = dot(rows[...], up_w[i])
        hidden.append((gated / (1.0 + jnp.exp(-gated)) * lifted).astype(bf16))
    copies[0][2].wait()
    copies[1][2].wait()
    step = width // out_sems.shape[0]
    stores = []
    for n in range(width // step):
        part = dot(hidden[0], down_w[0, :, n * step : (n + 1) * step]) + dot(
            hidden[1], down_w[1, :, n * step : (n + 1) * step]
        )
        span = slice(n * step, (n + 1) * step)
        result[span, :] = (part * weight).T.astype(bf16)
        stores.append(
            pltpu.make_async_copy(result.at[span, :], out.at[span, :], out_sems.at[n])
        )
        stores[-1].start()
    for store in stores:
        store.wait()


def expert_rows(expert, rows, router, named, blocks):
    count, width = rows.shape
    units = blocks[0].shape[1]
    vmem = pl.BlockSpec(memory_space=pltpu.VMEM)
    hbm = pl.BlockSpec(memory_space=pltpu.HBM)
    return pl.pallas_call(
        expert_kernel,
        out_shape=jax.ShapeDtypeStruct((width, count), bf16),
        in_specs=[pl.BlockSpec(memory_space=pltpu.SMEM)] + [vmem] * 3 + [hbm] * 6,
        out_specs=hbm,
        scratch_shapes=[
            pltpu.VMEM((2, width, units), bf16),
            pltpu.VMEM((2, width, units), bf16),
            pltpu.VMEM((2, units, width), bf16),
            pltpu.VMEM((width, count), bf16),
            pltpu.SemaphoreType.DMA((6,)),
            pltpu.SemaphoreType.DMA((5,)),
        ],
        compiler_params=pltpu.CompilerParams(vmem_limit_bytes=28 << 20),
        name="experts",
    )(
        expert,
        rows,
        router,
        named,
        *[pltpu.with_memory_space_constraint(b, pltpu.HBM) for b in blocks],
    )


def collect_kernel(slot, returned, codes, own, out, sums):
    groups, width, count = returned.shape
    slots, _, total = out.shape
    rows = total // 2
    lines = lax.broadcasted_iota(jnp.int32, (count, slots * rows), 0)
    by_step = []
    for c in (0, 1):
        acc = jnp.zeros((2 * width, slots * rows), f32)
        for x in range(SIDE):
            pick = jnp.where(
                lines == codes[2 * x + c : 2 * x + c + 1, :], 1.0, 0.0
            ).astype(bf16)
            pair = jnp.concatenate(
                [returned[SIDE * x + c], returned[SIDE * x + 2 + c]], axis=0
            )
            acc = acc + dot(pair, pick)
        by_step.append(acc[:width] + acc[width:])
    lane = lax.broadcasted_iota(jnp.int32, (width, total), 1)
    for pair in range(slots // 2):
        a = by_step[0][:, pair * total : (pair + 1) * total]
        b = by_step[1][:, pair * total : (pair + 1) * total]
        sums[2 * pair] = jnp.where(lane < rows, a, pltpu.roll(b, rows, 1))
        sums[2 * pair + 1] = jnp.where(lane < rows, pltpu.roll(a, rows, 1), b)
    sums[slot[0]] = sums[slot[0]] + own[...]
    out[...] = sums[...].astype(bf16)


def collect(slot, returned, codes, own):
    groups, width, _ = returned.shape
    shape = (groups, width, own.shape[1])
    vmem = pl.BlockSpec(memory_space=pltpu.VMEM)
    return pl.pallas_call(
        collect_kernel,
        out_shape=jax.ShapeDtypeStruct(shape, bf16),
        in_specs=[pl.BlockSpec(memory_space=pltpu.SMEM)] + [vmem] * 3,
        out_specs=vmem,
        scratch_shapes=[pltpu.VMEM(shape, f32)],
        compiler_params=pltpu.CompilerParams(vmem_limit_bytes=16 << 20),
        name="collect",
    )(slot, returned, codes, own)


def ranks_of(named):
    rows = named.shape[-2]
    lower = (
        jnp.arange(rows, dtype=jnp.int32)[:, None] > jnp.arange(rows, dtype=jnp.int32)[None, :]
    ).astype(bf16)
    return jnp.einsum("ij,...je->...ie", lower, named.astype(bf16), preferred_element_type=f32)


def per_device(
    step_inputs,
    attention_gain,
    query_weight,
    key_value_weight,
    output_weight,
    prompt_cache,
    page_table,
    cache_lengths,
    migration,
    parents,
    routes,
    feedforward_gain,
    router_weight,
    expert_gate,
    expert_up,
    expert_down,
    shared_gate,
    shared_up,
    shared_down,
):
    req_count = lax.axis_size("req")
    blk_count = lax.axis_size("blk")
    req_index = lax.axis_index("req")
    blk_index = lax.axis_index("blk")
    x_index = blk_index // SIDE
    q_index = blk_index % SIDE
    core = blk_index % 2
    steps, rows, width_local = step_inputs.shape
    total = steps * rows
    width = width_local * blk_count
    heads_here = QUERY_HEADS // KEY_VALUE_HEADS
    span = heads_here * HEAD_WIDTH
    subset = total // SIDE

    payload = payloads(
        req_count,
        step_inputs.reshape(total, width_local),
        routes.transpose(2, 0, 1),
        parents,
    )
    prompt, payload = lax.optimization_barrier((prompt_cache[0], payload))
    by_slot = lax.all_to_all(payload, "req", 0, 0, tiled=True)
    slot = migration[req_index]
    mine = lax.dynamic_index_in_dim(by_slot, slot, 0, False)
    part = rows // SIDE
    routes_all = (
        by_slot[:, width_local : width_local + TOPK]
        .astype(jnp.int32)
        .reshape(req_count, TOPK, SIDE, steps, part)
        .transpose(0, 1, 3, 2, 4)
        .reshape(req_count, TOPK, total)
    )
    routes_mine = lax.dynamic_index_in_dim(routes_all, slot, 0, False).T
    beam_mine = mine[width_local + TOPK].astype(jnp.int32)
    inputs = to_all(mine[:width_local], "blk").reshape(width, total)

    output_columns = lax.all_gather(
        output_weight, "blk", axis=1, tiled=True, axis_index_groups=QUAD
    )

    order = lax.dynamic_index_in_dim(page_table, req_index, 0, False)[0]
    pages = prompt[order]
    pages_local = pages.shape[0]
    by_head = (
        pages.reshape(pages_local * PAGE, 2, KEY_VALUE_HEADS, HEAD_WIDTH)
        .transpose(2, 0, 1, 3)
        .reshape(KEY_VALUE_HEADS, pages_local * PAGE, 2 * HEAD_WIDTH)
    )
    key_value_weight, by_head = lax.optimization_barrier((key_value_weight, by_head))
    caches = group_parts(
        lambda d: lax.dynamic_index_in_dim(by_head, x_index ^ d, 0, False), SIDE
    )

    half = key_value_weight.shape[1] // 2
    turned = key_value_weight.T
    left, right = turned[:half], turned[half:]
    low_side = blk_index < blk_count // 2
    groups = blk_count // 2
    straight = [(d, 2 * d) for d in range(groups)] + [
        (groups + d, 2 * d + 1) for d in range(groups)
    ]
    crossed = [(d, 2 * d + 1) for d in range(groups)] + [
        (groups + d, 2 * d) for d in range(groups)
    ]
    first = lax.ppermute(jnp.where(low_side, left, right), "blk", straight)
    second = lax.ppermute(jnp.where(low_side, right, left), "blk", crossed)
    projected = project(
        core[None].astype(jnp.int32),
        inputs,
        attention_gain.reshape(-1, 128),
        query_weight.T,
        first,
        second,
    )
    length = cache_lengths[req_index]
    frequency = rope_base ** (
        -2.0 * jnp.arange(HEAD_WIDTH // 2, dtype=f32) / HEAD_WIDTH
    )
    position = length + jnp.arange(steps, dtype=jnp.int32)
    angles = position.astype(f32)[:, None] * frequency
    cosine = jnp.tile(jnp.repeat(jnp.cos(angles).T, part, axis=1), (1, SIDE))
    sine = jnp.tile(jnp.repeat(jnp.sin(angles).T, part, axis=1), (1, SIDE))

    line = jnp.arange(total, dtype=jnp.int32)
    parent = jnp.where(
        line // part % steps == 1,
        line // subset * subset + line % part // BEAMS * BEAMS + beam_mine,
        -1,
    )[None]
    parts = attend(
        jnp.stack([length, q_index, x_index]).astype(jnp.int32),
        parent,
        cosine,
        sine,
        group_parts(lambda d: projected, 1),
        caches,
    )
    met = jnp.stack(group_parts(lambda d: parts[d], 1))
    levels = sum(
        met[:, :, span + i * heads_here : span + (i + 1) * heads_here].astype(f32)
        for i in range(3)
    )
    shares = jnp.exp(levels - jnp.max(levels, axis=0, keepdims=True))
    shares = shares / jnp.sum(shares, axis=0, keepdims=True)
    heads = (
        jnp.sum(
            shares[..., None]
            * met[:, :, :span].reshape(SIDE, subset, heads_here, HEAD_WIDTH).astype(f32),
            axis=0,
        )
        .astype(bf16)
        .reshape(subset, span)
    )

    all_heads = jnp.concatenate(
        in_order(group_parts(lambda d: heads, SIDE), x_index), axis=1
    )
    residual = lax.dynamic_slice(
        inputs, (x_index * span, q_index * subset), (span, subset)
    ).T
    attended_part = (residual.astype(f32) + dot(all_heads, output_columns)).astype(bf16)
    gate_here, up_here, down_here, attended_part = lax.optimization_barrier(
        (expert_gate[0], expert_up[0], expert_down[0], attended_part)
    )
    blocks = [gate_here, up_here, down_here]
    expert_blocks = blocks + [lax.ppermute(b, "blk", partners(1)) for b in blocks]
    to_core = jnp.broadcast_to(
        attended_part.reshape(1, steps, part, span), (blk_count // 2, steps, part, span)
    ).reshape(blk_count, part, span)
    attended_pieces = lax.all_to_all(to_core, "blk", 0, 0, tiled=True)

    per_req = E // req_count
    slot_ids = jnp.arange(req_count, dtype=jnp.int32)
    holder = jnp.sum(
        jnp.where(migration[None, :] == slot_ids[:, None], slot_ids[None, :], 0), axis=1
    )
    owned = jnp.arange(per_req, dtype=jnp.int32) + req_index * per_req
    named_all = jnp.any(
        routes_all.reshape(1, req_count, TOPK, steps, rows) == owned[:, None, None, None, None],
        axis=2,
    )
    before = (
        jnp.arange(rows, dtype=jnp.int32)[:, None] < jnp.arange(rows, dtype=jnp.int32)[None, :]
    ).astype(bf16)
    rank_all = dot(named_all.astype(bf16).reshape(-1, rows), before).reshape(named_all.shape)
    codes = (
        jnp.where(
            named_all,
            holder[None, :, None, None] * CAP + rank_all.astype(jnp.int32),
            -1,
        )
        .transpose(0, 2, 1, 3)
        .reshape(per_req * steps, req_count * rows)
    )

    experts = jnp.arange(E, dtype=jnp.int32)
    code = lax.dynamic_index_in_dim(codes, x_index * steps + core, 0, False)
    slot_of = (
        code[None, :] == jnp.arange(req_count * CAP, dtype=jnp.int32)[:, None]
    ).astype(bf16)
    routes_step = lax.dynamic_slice_in_dim(routes_all, core * rows, rows, 2)
    named_rows = (
        jnp.any(routes_step.transpose(0, 2, 1)[..., None] == experts, axis=2)
        .astype(bf16)
        .reshape(req_count * rows, E)
    )
    named_slots = dot(slot_of, named_rows)

    def of_step(a):
        return lax.dynamic_slice_in_dim(a, core * rows, rows, 0)

    def of_expert(a):
        return lax.dynamic_index_in_dim(a.reshape(rows, req_count, per_req), x_index, 2, False).T

    named_step = jnp.any(of_step(routes_mine)[:, :, None] == experts, axis=1)
    rank_step = of_expert(ranks_of(named_step))
    named_here = of_expert(named_step.astype(f32)) > 0.0
    slots = jnp.arange(CAP, dtype=f32)
    dispatch = (
        (named_here[:, None, :] & (rank_step[:, None, :] == slots[None, :, None]))
        .reshape(req_count * CAP, rows)
        .astype(bf16)
    )
    attended, normed_h, sent = spread(attended_pieces, feedforward_gain[None], dispatch)
    arrived = lax.all_to_all(
        sent.reshape(req_count, CAP, width), "req", 0, 0, tiled=True
    ).reshape(req_count * CAP, width)

    other = lax.ppermute(normed_h, "blk", partners(1))
    act = [
        (jax.nn.silu(dot(h, shared_gate)) * dot(h, shared_up)).astype(bf16)
        for h in (normed_h, other)
    ]

    def by_step(here, there):
        return jnp.concatenate(
            [jnp.where(core == 0, here, there), jnp.where(core == 0, there, here)], axis=0
        )

    act = by_step(*act)
    shared_part = lax.dot_general(
        shared_down, act, (((0,), (1,)), ((), ())), preferred_element_type=f32
    ).astype(bf16)
    q_high = q_index // 2
    halves = shared_part.reshape(SIDE, 2, 2, width_local, total)
    pair = (
        lax.dynamic_index_in_dim(halves, core, 2, False).astype(f32)
        + lax.ppermute(
            lax.dynamic_index_in_dim(halves, 1 - core, 2, False), "blk", partners(1)
        ).astype(f32)
    ).astype(bf16)
    over_x = sum(
        p.astype(f32)
        for p in group_parts(
            lambda d: lax.dynamic_index_in_dim(pair, x_index ^ d, 0, False), SIDE
        )
    )
    shared = lax.dynamic_index_in_dim(over_x, q_high, 0, False) + lax.ppermute(
        lax.dynamic_index_in_dim(over_x, 1 - q_high, 0, False).astype(bf16),
        "blk",
        partners(2),
    ).astype(f32)

    def columns_of(b):
        return lax.dynamic_slice_in_dim(attended, b * width_local, width_local, 1)

    own = (
        by_step(
            columns_of(blk_index),
            lax.ppermute(columns_of(blk_index ^ 1), "blk", partners(1)),
        ).T.astype(f32)
        + shared
    )
    arrived, own = lax.optimization_barrier((arrived, own))

    returned = lax.all_to_all(
        expert_rows(
            (req_index * per_req + x_index)[None].astype(jnp.int32),
            arrived,
            router_weight.T,
            named_slots,
            expert_blocks,
        ).reshape(blk_count, width_local, req_count * CAP),
        "blk",
        0,
        0,
        tiled=True,
    )

    outgoing = collect(slot[None], returned, codes, own)
    final = lax.all_to_all(outgoing, "req", 0, 0, tiled=True)
    return (
        jnp.sum(final.astype(f32), axis=0).T.astype(bf16).reshape(steps, rows, width_local)
    )


def solution(mesh):
    in_specs = (
        P(None, "req", "blk"),
        P(),
        P(None, "blk"),
        P(None, "blk"),
        P(None, "blk"),
        P("req", "blk", None, None),
        P(None, "blk", None),
        P(),
        P(),
        P(None, "req"),
        P(None, "req", None),
        P(),
        P(),
        P(("req", "blk"), None, None),
        P(("req", "blk"), None, None),
        P(("req", "blk"), None, None),
        P(None, "blk"),
        P(None, "blk"),
        P("blk", None),
    )
    out_specs = P(None, "req", "blk")
    return jax.shard_map(
        per_device, mesh=mesh, in_specs=in_specs, out_specs=out_specs, check_vma=False
    )
```

```python
import jax
import jax.numpy as jnp
from jax import lax
from jax.experimental import pallas as pl
from jax.experimental.pallas import tpu as pltpu
from jax.sharding import PartitionSpec as P

QUERY_HEADS = 20
KEY_VALUE_HEADS = 4
HEAD_WIDTH = 128
E = 64
TOPK = 6
BEAMS = 8
CAP = 16
PAGE = 128

epsilon = 1e-05
rope_base = 500000.0
masked_floor = -1e30

bf16 = jnp.bfloat16
f32 = jnp.float32

SIDE = 4
QUAD = [[SIDE * i + k for k in range(SIDE)] for i in range(SIDE)]


def dot(a, b):
    return jnp.dot(a, b, preferred_element_type=f32)


def to_all(piece, axis):
    count = lax.axis_size(axis)
    copies = jnp.broadcast_to(piece[None], (count,) + piece.shape)
    return lax.all_to_all(copies, axis, 0, 0, tiled=True)


def partners(distance):
    return [(d, d ^ distance) for d in range(SIDE * SIDE)]


def group_parts(piece_for, stride):
    return [piece_for(0)] + [
        lax.ppermute(piece_for(d), "blk", partners(d * stride)) for d in range(1, SIDE)
    ]


def in_order(parts, index):
    odd = index % 2 == 1
    upper = index // 2 == 1
    a, b, c, d = parts
    a, b = jnp.where(odd, b, a), jnp.where(odd, a, b)
    c, d = jnp.where(odd, d, c), jnp.where(odd, c, d)
    return [
        jnp.where(upper, c, a),
        jnp.where(upper, d, b),
        jnp.where(upper, a, c),
        jnp.where(upper, b, d),
    ]


def norm_rows(rows, gain, axis):
    wide = rows.astype(f32)
    inverse = lax.rsqrt(jnp.mean(wide * wide, axis=axis, keepdims=True) + epsilon)
    return (wide * inverse * gain).astype(bf16)


def three_parts(value):
    high = value.astype(bf16)
    rest = value - high.astype(f32)
    middle = rest.astype(bf16)
    low = (rest - middle.astype(f32)).astype(bf16)
    return high, middle, low


def rotated(vectors, cosine, sine):
    half = vectors.shape[0] // 2
    a = vectors[:half].astype(f32)
    b = vectors[half:].astype(f32)
    return jnp.concatenate([a * cosine - b * sine, b * cosine + a * sine], axis=0)


def across(a, b):
    return lax.dot_general(a, b, (((0,), (0,)), ((), ())), preferred_element_type=f32)


def payload_kernel(x, routes, beams, out, lines):
    total, width = x.shape
    rows = total // 2
    part = rows // SIDE
    main = width // 128 * 128
    ordered = jnp.concatenate(
        [
            x[t * rows + q * part : t * rows + (q + 1) * part, :]
            for q in range(SIDE)
            for t in (0, 1)
        ],
        axis=0,
    ).astype(f32)
    lines[:main, :] = ordered[:, :main].T.astype(bf16)
    rest = jnp.concatenate(
        [ordered[:, main:], jnp.zeros((total, 128 - width + main), f32)], axis=1
    )
    lines[main:width, :] = rest.T[: width - main].astype(bf16)
    none = jnp.zeros((1, rows), jnp.int32)
    by_step = [
        jnp.concatenate([routes[k, t : t + 1, :] for k in range(TOPK)] + [last, none], axis=0)
        for t, last in ((0, none), (1, beams[...]))
    ]
    extra = jnp.concatenate(
        [
            by_step[t][:, q * part : (q + 1) * part]
            for q in range(SIDE)
            for t in (0, 1)
        ],
        axis=1,
    )
    lines[width:, :] = extra.astype(f32).astype(bf16)
    for i in range(out.shape[0]):
        out[i] = lines[...]


def payloads(count, x, routes, beams):
    total, width = x.shape
    vmem = pl.BlockSpec(memory_space=pltpu.VMEM)
    return pl.pallas_call(
        payload_kernel,
        out_shape=jax.ShapeDtypeStruct((count, width + TOPK + 2, total), bf16),
        in_specs=[vmem] * 3,
        out_specs=vmem,
        scratch_shapes=[pltpu.VMEM((width + TOPK + 2, total), bf16)],
        name="payload",
    )(x, routes, beams)


def project_kernel(core, x, gain, query, first, second, out, normed):
    width = x.shape[0]
    wide = x[...].astype(f32)
    inverse = lax.rsqrt(jnp.sum(wide * wide, axis=0, keepdims=True) / width + epsilon)
    gains = gain[...].T
    for i in range(width // 128):
        rows = slice(i * 128, (i + 1) * 128)
        normed[rows, :] = (
            x[rows, :].astype(f32) * inverse * gains[:, i : i + 1]
        ).astype(bf16)
    share = query.shape[0]
    half = first.shape[0]
    out[:share, :] = dot(query[...], normed[...]).astype(bf16)
    a = dot(first[...], normed[...])
    b = dot(second[...], normed[...])
    even = core[0] == 0
    out[share : share + half, :] = jnp.where(even, a, b).astype(bf16)
    out[share + half :, :] = jnp.where(even, b, a).astype(bf16)


def project(core, x, gain, query, first, second):
    vmem = pl.BlockSpec(memory_space=pltpu.VMEM)
    share = query.shape[0] + 2 * first.shape[0]
    return pl.pallas_call(
        project_kernel,
        out_shape=jax.ShapeDtypeStruct((share, x.shape[1]), bf16),
        in_specs=[pl.BlockSpec(memory_space=pltpu.SMEM)] + [vmem] * 5,
        out_specs=vmem,
        scratch_shapes=[pltpu.VMEM(x.shape, bf16)],
        compiler_params=pltpu.CompilerParams(vmem_limit_bytes=10 << 20),
        name="project",
    )(core, x, gain, query, first, second)


def attention_kernel(
    scalars, parent, cosine, sine, p0, p1, p2, p3, c0, c1, c2, c3,
    o0, o1, o2, o3, query_rows, key_rows, value_rows, bias, scores, stats, joined,
):
    length = scalars[0]
    q_index = scalars[1]
    x_index = scalars[2]
    features, total = p0.shape
    span = query_rows.shape[0]
    share = span // SIDE
    half = HEAD_WIDTH // SIDE
    for d, piece in enumerate((p0, p1, p2, p3)):
        source = q_index ^ d
        query_rows[pl.ds(pl.multiple_of(source * share, half), share), :] = piece[:share, :]
        key_rows[pl.ds(pl.multiple_of(source * half, half), half), :] = piece[
            share : share + half, :
        ]
        value_rows[pl.ds(pl.multiple_of(source * half, half), half), :] = piece[
            share + half :, :
        ]
    cos = cosine[...]
    sin = sine[...]
    new_keys = rotated(key_rows[...], cos, sin).T.astype(bf16)
    new_values = value_rows[...]
    caches = (c0, c1, c2, c3)
    held = c0.shape[0]
    line = lax.broadcasted_iota(jnp.int32, (held, total), 0)
    spread = line + (line // PAGE) * (SIDE * SIDE - 1) * PAGE
    for d in range(SIDE):
        column = (x_index ^ d) * SIDE + q_index
        bias[d * held : (d + 1) * held, :] = jnp.where(
            spread + column * PAGE < length, 0.0, masked_floor
        )
    key_id = lax.broadcasted_iota(jnp.int32, (total, total), 0)
    row_id = lax.broadcasted_iota(jnp.int32, (total, total), 1)
    near = ((key_id == row_id) | (key_id == parent[...])) & (
        key_id // (total // SIDE) == q_index
    )
    bias[SIDE * held :, :] = jnp.where(near, 0.0, masked_floor)
    stats[...] = jnp.zeros(stats.shape, f32)
    scale = HEAD_WIDTH ** (-0.5)
    heads_here = span // HEAD_WIDTH
    for h in range(heads_here):
        query = rotated(
            query_rows[h * HEAD_WIDTH : (h + 1) * HEAD_WIDTH, :], cos, sin
        ).astype(bf16)
        for d, cache in enumerate(caches):
            scores[d * held : (d + 1) * held, :] = (
                dot(cache[:, :HEAD_WIDTH], query) * scale
                + bias[d * held : (d + 1) * held, :]
            )
        scores[SIDE * held :, :] = dot(new_keys, query) * scale + bias[SIDE * held :, :]
        peak = jnp.max(scores[...], axis=0, keepdims=True)
        mass = jnp.zeros((1, total), f32)
        weighted = jnp.zeros((HEAD_WIDTH, total), f32)
        for d, cache in enumerate(caches):
            raised = jnp.exp(scores[d * held : (d + 1) * held, :] - peak)
            mass = mass + jnp.sum(raised, axis=0, keepdims=True)
            weighted = weighted + across(cache[:, HEAD_WIDTH:], raised.astype(bf16))
        raised = jnp.exp(scores[SIDE * held :, :] - peak)
        mass = mass + jnp.sum(raised, axis=0, keepdims=True)
        weighted = weighted + dot(new_values, raised.astype(bf16))
        joined[:, h * HEAD_WIDTH : (h + 1) * HEAD_WIDTH] = (weighted / mass).T.astype(bf16)
        level = jnp.where(peak > 0.5 * masked_floor, peak + jnp.log(mass), masked_floor)
        for i, part in enumerate(three_parts(level)):
            place = i * heads_here + h
            stats[place : place + 1, :] = part.astype(f32)
    joined[:, span:] = stats[...].T.astype(bf16)
    subset = total // SIDE
    for d, out in enumerate((o0, o1, o2, o3)):
        out[...] = joined[pl.ds(pl.multiple_of((q_index ^ d) * subset, subset), subset), :]


def attend(scalars, parent, cosine, sine, pieces, caches):
    total = pieces[0].shape[1]
    subset = total // SIDE
    span = QUERY_HEADS // KEY_VALUE_HEADS * HEAD_WIDTH
    keys = SIDE * caches[0].shape[0] + total
    vmem = pl.BlockSpec(memory_space=pltpu.VMEM)
    return pl.pallas_call(
        attention_kernel,
        out_shape=[jax.ShapeDtypeStruct((subset, span + HEAD_WIDTH), bf16)] * SIDE,
        in_specs=[pl.BlockSpec(memory_space=pltpu.SMEM)] + [vmem] * (3 + 2 * SIDE),
        out_specs=[vmem] * SIDE,
        scratch_shapes=[
            pltpu.VMEM((span, total), bf16),
            pltpu.VMEM((HEAD_WIDTH, total), bf16),
            pltpu.VMEM((HEAD_WIDTH, total), bf16),
            pltpu.VMEM((keys, total), f32),
            pltpu.VMEM((keys, total), f32),
            pltpu.VMEM((HEAD_WIDTH, total), f32),
            pltpu.VMEM((total, span + HEAD_WIDTH), bf16),
        ],
        compiler_params=pltpu.CompilerParams(vmem_limit_bytes=12 << 20),
        name="attention",
    )(scalars, parent, cosine, sine, *pieces, *caches)


def output_kernel(x_index, h0, h1, h2, h3, weights, residual, out):
    rows, span = h0.shape
    acc = residual[...].astype(f32)
    for d, h in enumerate((h0, h1, h2, h3)):
        place = pl.multiple_of((x_index[0] ^ d) * span, span)
        acc = acc + lax.dot_general(
            h[...],
            weights[:, pl.ds(place, span)],
            (((1,), (1,)), ((), ())),
            preferred_element_type=f32,
        )
    attended = acc.astype(bf16)
    part = rows // 2
    for j in range(out.shape[0]):
        t = j % 2
        out[j] = attended[t * part : (t + 1) * part, :]


def output_rows(x_index, heads, weights, residual, count):
    rows, span = residual.shape
    vmem = pl.BlockSpec(memory_space=pltpu.VMEM)
    return pl.pallas_call(
        output_kernel,
        out_shape=jax.ShapeDtypeStruct((count, rows // 2, span), bf16),
        in_specs=[pl.BlockSpec(memory_space=pltpu.SMEM)] + [vmem] * (SIDE + 2),
        out_specs=vmem,
        compiler_params=pltpu.CompilerParams(vmem_limit_bytes=16 << 20),
        name="output",
    )(x_index, *heads, weights, residual)


def spread_kernel(pieces, gain, dispatch, attended, normed, sent):
    count, part, span = pieces.shape
    for x in range(count // SIDE):
        for q in range(SIDE):
            attended[q * part : (q + 1) * part, x * span : (x + 1) * span] = pieces[
                SIDE * x + q
            ]
    normed[...] = norm_rows(attended[...], gain[...], 1)
    sent[...] = dot(dispatch[...], normed[...]).astype(bf16)


def spread(pieces, gain, dispatch):
    count, part, span = pieces.shape
    width = count // SIDE * span
    vmem = pl.BlockSpec(memory_space=pltpu.VMEM)
    return pl.pallas_call(
        spread_kernel,
        out_shape=[
            jax.ShapeDtypeStruct((SIDE * part, width), bf16),
            jax.ShapeDtypeStruct((SIDE * part, width), bf16),
            jax.ShapeDtypeStruct((dispatch.shape[0], width), bf16),
        ],
        in_specs=[vmem] * 3,
        out_specs=[vmem] * 3,
        name="spread",
    )(pieces, gain, dispatch)


def expert_kernel(
    expert, rows, router, named, g0, u0, d0, g1, u1, d1, out,
    gate_w, up_w, down_w, result, sems, out_sems,
):
    copies = []
    for i, (g, u, d) in enumerate(((g0, u0, d0), (g1, u1, d1))):
        copies.append(
            [
                pltpu.make_async_copy(src, dst.at[i], sems.at[3 * i + k])
                for k, (src, dst) in enumerate(((g, gate_w), (u, up_w), (d, down_w)))
            ]
        )
    order = [(0, 0), (0, 1), (1, 0), (1, 1), (0, 2), (1, 2)]
    for i, k in order:
        copies[i][k].start()
    width = down_w.shape[2]
    logits = lax.dot_general(
        rows[...], router[...], (((1,), (1,)), ((), ())), preferred_element_type=f32
    )
    raised = jnp.where(named[...] > 0.0, jnp.exp(logits), 0.0)
    column = lax.broadcasted_iota(jnp.int32, raised.shape, 1)
    total = jnp.sum(raised, axis=1, keepdims=True)
    picked = jnp.sum(jnp.where(column == expert[0], raised, 0.0), axis=1, keepdims=True)
    weight = picked / jnp.where(total > 0.0, total, 1.0)
    hidden = []
    for i in (0, 1):
        copies[i][0].wait()
        gated = dot(rows[...], gate_w[i])
        copies[i][1].wait()
        lifted = dot(rows[...], up_w[i])
        hidden.append((gated / (1.0 + jnp.exp(-gated)) * lifted).astype(bf16))
    copies[0][2].wait()
    copies[1][2].wait()
    step = width // out_sems.shape[0]
    stores = []
    for n in range(width // step):
        part = dot(hidden[0], down_w[0, :, n * step : (n + 1) * step]) + dot(
            hidden[1], down_w[1, :, n * step : (n + 1) * step]
        )
        span = slice(n * step, (n + 1) * step)
        result[span, :] = (part * weight).T.astype(bf16)
        stores.append(
            pltpu.make_async_copy(result.at[span, :], out.at[span, :], out_sems.at[n])
        )
        stores[-1].start()
    for store in stores:
        store.wait()


def expert_rows(expert, rows, router, named, blocks):
    count, width = rows.shape
    units = blocks[0].shape[1]
    vmem = pl.BlockSpec(memory_space=pltpu.VMEM)
    hbm = pl.BlockSpec(memory_space=pltpu.HBM)
    return pl.pallas_call(
        expert_kernel,
        out_shape=jax.ShapeDtypeStruct((width, count), bf16),
        in_specs=[pl.BlockSpec(memory_space=pltpu.SMEM)] + [vmem] * 3 + [hbm] * 6,
        out_specs=hbm,
        scratch_shapes=[
            pltpu.VMEM((2, width, units), bf16),
            pltpu.VMEM((2, width, units), bf16),
            pltpu.VMEM((2, units, width), bf16),
            pltpu.VMEM((width, count), bf16),
            pltpu.SemaphoreType.DMA((6,)),
            pltpu.SemaphoreType.DMA((5,)),
        ],
        compiler_params=pltpu.CompilerParams(vmem_limit_bytes=28 << 20),
        name="experts",
    )(
        expert,
        rows,
        router,
        named,
        *[pltpu.with_memory_space_constraint(b, pltpu.HBM) for b in blocks],
    )


def collect_kernel(slot, returned, codes, own, out, sums):
    groups, width, count = returned.shape
    slots, _, total = out.shape
    rows = total // 2
    lines = lax.broadcasted_iota(jnp.int32, (count, slots * rows), 0)
    by_step = []
    for c in (0, 1):
        acc = jnp.zeros((2 * width, slots * rows), f32)
        for x in range(SIDE):
            pick = jnp.where(
                lines == codes[2 * x + c : 2 * x + c + 1, :], 1.0, 0.0
            ).astype(bf16)
            pair = jnp.concatenate(
                [returned[SIDE * x + c], returned[SIDE * x + 2 + c]], axis=0
            )
            acc = acc + dot(pair, pick)
        by_step.append(acc[:width] + acc[width:])
    lane = lax.broadcasted_iota(jnp.int32, (width, total), 1)
    for pair in range(slots // 2):
        a = by_step[0][:, pair * total : (pair + 1) * total]
        b = by_step[1][:, pair * total : (pair + 1) * total]
        sums[2 * pair] = jnp.where(lane < rows, a, pltpu.roll(b, rows, 1))
        sums[2 * pair + 1] = jnp.where(lane < rows, pltpu.roll(a, rows, 1), b)
    sums[slot[0]] = sums[slot[0]] + own[...]
    out[...] = sums[...].astype(bf16)


def collect(slot, returned, codes, own):
    groups, width, _ = returned.shape
    shape = (groups, width, own.shape[1])
    vmem = pl.BlockSpec(memory_space=pltpu.VMEM)
    return pl.pallas_call(
        collect_kernel,
        out_shape=jax.ShapeDtypeStruct(shape, bf16),
        in_specs=[pl.BlockSpec(memory_space=pltpu.SMEM)] + [vmem] * 3,
        out_specs=vmem,
        scratch_shapes=[pltpu.VMEM(shape, f32)],
        compiler_params=pltpu.CompilerParams(vmem_limit_bytes=16 << 20),
        name="collect",
    )(slot, returned, codes, own)


def ranks_of(named):
    rows = named.shape[-2]
    lower = (
        jnp.arange(rows, dtype=jnp.int32)[:, None] > jnp.arange(rows, dtype=jnp.int32)[None, :]
    ).astype(bf16)
    return jnp.einsum("ij,...je->...ie", lower, named.astype(bf16), preferred_element_type=f32)


def per_device(
    step_inputs,
    attention_gain,
    query_weight,
    key_value_weight,
    output_weight,
    prompt_cache,
    page_table,
    cache_lengths,
    migration,
    parents,
    routes,
    feedforward_gain,
    router_weight,
    expert_gate,
    expert_up,
    expert_down,
    shared_gate,
    shared_up,
    shared_down,
):
    req_count = lax.axis_size("req")
    blk_count = lax.axis_size("blk")
    req_index = lax.axis_index("req")
    blk_index = lax.axis_index("blk")
    x_index = blk_index // SIDE
    q_index = blk_index % SIDE
    core = blk_index % 2
    steps, rows, width_local = step_inputs.shape
    total = steps * rows
    width = width_local * blk_count
    heads_here = QUERY_HEADS // KEY_VALUE_HEADS
    span = heads_here * HEAD_WIDTH
    subset = total // SIDE

    payload = payloads(
        req_count,
        step_inputs.reshape(total, width_local),
        routes.transpose(2, 0, 1),
        parents,
    )
    prompt, payload = lax.optimization_barrier((prompt_cache[0], payload))
    by_slot = lax.all_to_all(payload, "req", 0, 0, tiled=True)
    slot = migration[req_index]
    mine = lax.dynamic_index_in_dim(by_slot, slot, 0, False)
    part = rows // SIDE
    routes_all = (
        by_slot[:, width_local : width_local + TOPK]
        .astype(jnp.int32)
        .reshape(req_count, TOPK, SIDE, steps, part)
        .transpose(0, 1, 3, 2, 4)
        .reshape(req_count, TOPK, total)
    )
    routes_mine = lax.dynamic_index_in_dim(routes_all, slot, 0, False).T
    beam_mine = mine[width_local + TOPK].astype(jnp.int32)
    inputs = to_all(mine[:width_local], "blk").reshape(width, total)

    output_columns = lax.all_gather(
        output_weight, "blk", axis=1, tiled=True, axis_index_groups=QUAD
    )

    order = lax.dynamic_index_in_dim(page_table, req_index, 0, False)[0]
    pages = prompt[order]
    pages_local = pages.shape[0]
    by_head = (
        pages.reshape(pages_local * PAGE, 2, KEY_VALUE_HEADS, HEAD_WIDTH)
        .transpose(2, 0, 1, 3)
        .reshape(KEY_VALUE_HEADS, pages_local * PAGE, 2 * HEAD_WIDTH)
    )
    key_value_weight, by_head = lax.optimization_barrier((key_value_weight, by_head))
    caches = group_parts(
        lambda d: lax.dynamic_index_in_dim(by_head, x_index ^ d, 0, False), SIDE
    )

    half = key_value_weight.shape[1] // 2
    turned = key_value_weight.T
    left, right = turned[:half], turned[half:]
    low_side = blk_index < blk_count // 2
    groups = blk_count // 2
    straight = [(d, 2 * d) for d in range(groups)] + [
        (groups + d, 2 * d + 1) for d in range(groups)
    ]
    crossed = [(d, 2 * d + 1) for d in range(groups)] + [
        (groups + d, 2 * d) for d in range(groups)
    ]
    first = lax.ppermute(jnp.where(low_side, left, right), "blk", straight)
    second = lax.ppermute(jnp.where(low_side, right, left), "blk", crossed)
    projected = project(
        core[None].astype(jnp.int32),
        inputs,
        attention_gain.reshape(-1, 128),
        query_weight.T,
        first,
        second,
    )
    length = cache_lengths[req_index]
    frequency = rope_base ** (
        -2.0 * jnp.arange(HEAD_WIDTH // 2, dtype=f32) / HEAD_WIDTH
    )
    position = length + jnp.arange(steps, dtype=jnp.int32)
    angles = position.astype(f32)[:, None] * frequency
    cosine = jnp.tile(jnp.repeat(jnp.cos(angles).T, part, axis=1), (1, SIDE))
    sine = jnp.tile(jnp.repeat(jnp.sin(angles).T, part, axis=1), (1, SIDE))

    line = jnp.arange(total, dtype=jnp.int32)
    parent = jnp.where(
        line // part % steps == 1,
        line // subset * subset + line % part // BEAMS * BEAMS + beam_mine,
        -1,
    )[None]
    parts = attend(
        jnp.stack([length, q_index, x_index]).astype(jnp.int32),
        parent,
        cosine,
        sine,
        group_parts(lambda d: projected, 1),
        caches,
    )
    met = jnp.stack(group_parts(lambda d: parts[d], 1))
    levels = sum(
        met[:, :, span + i * heads_here : span + (i + 1) * heads_here].astype(f32)
        for i in range(3)
    )
    shares = jnp.exp(levels - jnp.max(levels, axis=0, keepdims=True))
    shares = shares / jnp.sum(shares, axis=0, keepdims=True)
    heads = (
        jnp.sum(
            shares[..., None]
            * met[:, :, :span].reshape(SIDE, subset, heads_here, HEAD_WIDTH).astype(f32),
            axis=0,
        )
        .astype(bf16)
        .reshape(subset, span)
    )

    residual = lax.dynamic_slice(
        inputs, (x_index * span, q_index * subset), (span, subset)
    ).T
    to_core = output_rows(
        x_index[None].astype(jnp.int32),
        group_parts(lambda d: heads, SIDE),
        output_columns.T,
        residual,
        blk_count,
    )
    gate_here, up_here, down_here, to_core = lax.optimization_barrier(
        (expert_gate[0], expert_up[0], expert_down[0], to_core)
    )
    blocks = [gate_here, up_here, down_here]
    expert_blocks = blocks + [lax.ppermute(b, "blk", partners(1)) for b in blocks]
    attended_pieces = lax.all_to_all(to_core, "blk", 0, 0, tiled=True)

    per_req = E // req_count
    slot_ids = jnp.arange(req_count, dtype=jnp.int32)
    holder = jnp.sum(
        jnp.where(migration[None, :] == slot_ids[:, None], slot_ids[None, :], 0), axis=1
    )
    owned = jnp.arange(per_req, dtype=jnp.int32) + req_index * per_req
    named_all = jnp.any(
        routes_all.reshape(1, req_count, TOPK, steps, rows) == owned[:, None, None, None, None],
        axis=2,
    )
    before = (
        jnp.arange(rows, dtype=jnp.int32)[:, None] < jnp.arange(rows, dtype=jnp.int32)[None, :]
    ).astype(bf16)
    rank_all = dot(named_all.astype(bf16).reshape(-1, rows), before).reshape(named_all.shape)
    codes = (
        jnp.where(
            named_all,
            holder[None, :, None, None] * CAP + rank_all.astype(jnp.int32),
            -1,
        )
        .transpose(0, 2, 1, 3)
        .reshape(per_req * steps, req_count * rows)
    )

    experts = jnp.arange(E, dtype=jnp.int32)
    code = lax.dynamic_index_in_dim(codes, x_index * steps + core, 0, False)
    slot_of = (
        code[None, :] == jnp.arange(req_count * CAP, dtype=jnp.int32)[:, None]
    ).astype(bf16)
    routes_step = lax.dynamic_slice_in_dim(routes_all, core * rows, rows, 2)
    named_rows = (
        jnp.any(routes_step.transpose(0, 2, 1)[..., None] == experts, axis=2)
        .astype(bf16)
        .reshape(req_count * rows, E)
    )
    named_slots = dot(slot_of, named_rows)

    def of_step(a):
        return lax.dynamic_slice_in_dim(a, core * rows, rows, 0)

    def of_expert(a):
        return lax.dynamic_index_in_dim(a.reshape(rows, req_count, per_req), x_index, 2, False).T

    named_step = jnp.any(of_step(routes_mine)[:, :, None] == experts, axis=1)
    rank_step = of_expert(ranks_of(named_step))
    named_here = of_expert(named_step.astype(f32)) > 0.0
    slots = jnp.arange(CAP, dtype=f32)
    dispatch = (
        (named_here[:, None, :] & (rank_step[:, None, :] == slots[None, :, None]))
        .reshape(req_count * CAP, rows)
        .astype(bf16)
    )
    attended, normed_h, sent = spread(attended_pieces, feedforward_gain[None], dispatch)
    arrived = lax.all_to_all(
        sent.reshape(req_count, CAP, width), "req", 0, 0, tiled=True
    ).reshape(req_count * CAP, width)

    other = lax.ppermute(normed_h, "blk", partners(1))
    act = [
        (jax.nn.silu(dot(h, shared_gate)) * dot(h, shared_up)).astype(bf16)
        for h in (normed_h, other)
    ]

    def by_step(here, there):
        return jnp.concatenate(
            [jnp.where(core == 0, here, there), jnp.where(core == 0, there, here)], axis=0
        )

    act = by_step(*act)
    shared_part = lax.dot_general(
        shared_down, act, (((0,), (1,)), ((), ())), preferred_element_type=f32
    ).astype(bf16)
    q_high = q_index // 2
    halves = shared_part.reshape(SIDE, 2, 2, width_local, total)
    pair = (
        lax.dynamic_index_in_dim(halves, core, 2, False).astype(f32)
        + lax.ppermute(
            lax.dynamic_index_in_dim(halves, 1 - core, 2, False), "blk", partners(1)
        ).astype(f32)
    ).astype(bf16)
    over_x = sum(
        p.astype(f32)
        for p in group_parts(
            lambda d: lax.dynamic_index_in_dim(pair, x_index ^ d, 0, False), SIDE
        )
    )
    shared = lax.dynamic_index_in_dim(over_x, q_high, 0, False) + lax.ppermute(
        lax.dynamic_index_in_dim(over_x, 1 - q_high, 0, False).astype(bf16),
        "blk",
        partners(2),
    ).astype(f32)

    def columns_of(b):
        return lax.dynamic_slice_in_dim(attended, b * width_local, width_local, 1)

    own = (
        by_step(
            columns_of(blk_index),
            lax.ppermute(columns_of(blk_index ^ 1), "blk", partners(1)),
        ).T.astype(f32)
        + shared
    )
    arrived, own = lax.optimization_barrier((arrived, own))

    returned = lax.all_to_all(
        expert_rows(
            (req_index * per_req + x_index)[None].astype(jnp.int32),
            arrived,
            router_weight.T,
            named_slots,
            expert_blocks,
        ).reshape(blk_count, width_local, req_count * CAP),
        "blk",
        0,
        0,
        tiled=True,
    )

    outgoing = collect(slot[None], returned, codes, own)
    final = lax.all_to_all(outgoing, "req", 0, 0, tiled=True)
    return (
        jnp.sum(final.astype(f32), axis=0).T.astype(bf16).reshape(steps, rows, width_local)
    )


def solution(mesh):
    in_specs = (
        P(None, "req", "blk"),
        P(),
        P(None, "blk"),
        P(None, "blk"),
        P(None, "blk"),
        P("req", "blk", None, None),
        P(None, "blk", None),
        P(),
        P(),
        P(None, "req"),
        P(None, "req", None),
        P(),
        P(),
        P(("req", "blk"), None, None),
        P(("req", "blk"), None, None),
        P(("req", "blk"), None, None),
        P(None, "blk"),
        P(None, "blk"),
        P("blk", None),
    )
    out_specs = P(None, "req", "blk")
    return jax.shard_map(
        per_device, mesh=mesh, in_specs=in_specs, out_specs=out_specs, check_vma=False
    )
```

```python
import jax
import jax.numpy as jnp
from jax import lax
from jax.experimental import pallas as pl
from jax.experimental.pallas import tpu as pltpu
from jax.sharding import PartitionSpec as P

QUERY_HEADS = 20
KEY_VALUE_HEADS = 4
HEAD_WIDTH = 128
E = 64
TOPK = 6
BEAMS = 8
CAP = 16
PAGE = 128

epsilon = 1e-05
rope_base = 500000.0
masked_floor = -1e30

bf16 = jnp.bfloat16
f32 = jnp.float32

SIDE = 4
QUAD = [[SIDE * i + k for k in range(SIDE)] for i in range(SIDE)]


def dot(a, b):
    return jnp.dot(a, b, preferred_element_type=f32)


def to_all(piece, axis):
    count = lax.axis_size(axis)
    copies = jnp.broadcast_to(piece[None], (count,) + piece.shape)
    return lax.all_to_all(copies, axis, 0, 0, tiled=True)


def partners(distance):
    return [(d, d ^ distance) for d in range(SIDE * SIDE)]


def group_parts(piece_for, stride):
    return [piece_for(0)] + [
        lax.ppermute(piece_for(d), "blk", partners(d * stride)) for d in range(1, SIDE)
    ]


def in_order(parts, index):
    odd = index % 2 == 1
    upper = index // 2 == 1
    a, b, c, d = parts
    a, b = jnp.where(odd, b, a), jnp.where(odd, a, b)
    c, d = jnp.where(odd, d, c), jnp.where(odd, c, d)
    return [
        jnp.where(upper, c, a),
        jnp.where(upper, d, b),
        jnp.where(upper, a, c),
        jnp.where(upper, b, d),
    ]


def norm_rows(rows, gain, axis):
    wide = rows.astype(f32)
    inverse = lax.rsqrt(jnp.mean(wide * wide, axis=axis, keepdims=True) + epsilon)
    return (wide * inverse * gain).astype(bf16)


def three_parts(value):
    high = value.astype(bf16)
    rest = value - high.astype(f32)
    middle = rest.astype(bf16)
    low = (rest - middle.astype(f32)).astype(bf16)
    return high, middle, low


def rotated(vectors, cosine, sine):
    half = vectors.shape[0] // 2
    a = vectors[:half].astype(f32)
    b = vectors[half:].astype(f32)
    return jnp.concatenate([a * cosine - b * sine, b * cosine + a * sine], axis=0)


def across(a, b):
    return lax.dot_general(a, b, (((0,), (0,)), ((), ())), preferred_element_type=f32)


def payload_kernel(x, routes, beams, out, lines):
    total, width = x.shape
    rows = total // 2
    part = rows // SIDE
    main = width // 128 * 128
    ordered = jnp.concatenate(
        [
            x[t * rows + q * part : t * rows + (q + 1) * part, :]
            for q in range(SIDE)
            for t in (0, 1)
        ],
        axis=0,
    ).astype(f32)
    lines[:main, :] = ordered[:, :main].T.astype(bf16)
    rest = jnp.concatenate(
        [ordered[:, main:], jnp.zeros((total, 128 - width + main), f32)], axis=1
    )
    lines[main:width, :] = rest.T[: width - main].astype(bf16)
    none = jnp.zeros((1, rows), jnp.int32)
    by_step = [
        jnp.concatenate([routes[k, t : t + 1, :] for k in range(TOPK)] + [last, none], axis=0)
        for t, last in ((0, none), (1, beams[...]))
    ]
    extra = jnp.concatenate(
        [
            by_step[t][:, q * part : (q + 1) * part]
            for q in range(SIDE)
            for t in (0, 1)
        ],
        axis=1,
    )
    lines[width:, :] = extra.astype(f32).astype(bf16)
    for i in range(out.shape[0]):
        out[i] = lines[...]


def payloads(count, x, routes, beams):
    total, width = x.shape
    vmem = pl.BlockSpec(memory_space=pltpu.VMEM)
    return pl.pallas_call(
        payload_kernel,
        out_shape=jax.ShapeDtypeStruct((count, width + TOPK + 2, total), bf16),
        in_specs=[vmem] * 3,
        out_specs=vmem,
        scratch_shapes=[pltpu.VMEM((width + TOPK + 2, total), bf16)],
        name="payload",
    )(x, routes, beams)


def project_kernel(core, x, gain, query, first, second, out, normed):
    width = x.shape[0]
    wide = x[...].astype(f32)
    inverse = lax.rsqrt(jnp.sum(wide * wide, axis=0, keepdims=True) / width + epsilon)
    gains = gain[...].T
    for i in range(width // 128):
        rows = slice(i * 128, (i + 1) * 128)
        normed[rows, :] = (
            x[rows, :].astype(f32) * inverse * gains[:, i : i + 1]
        ).astype(bf16)
    share = query.shape[0]
    half = first.shape[0]
    out[:share, :] = dot(query[...], normed[...]).astype(bf16)
    a = dot(first[...], normed[...])
    b = dot(second[...], normed[...])
    even = core[0] == 0
    out[share : share + half, :] = jnp.where(even, a, b).astype(bf16)
    out[share + half :, :] = jnp.where(even, b, a).astype(bf16)


def project(core, x, gain, query, first, second):
    vmem = pl.BlockSpec(memory_space=pltpu.VMEM)
    share = query.shape[0] + 2 * first.shape[0]
    return pl.pallas_call(
        project_kernel,
        out_shape=jax.ShapeDtypeStruct((share, x.shape[1]), bf16),
        in_specs=[pl.BlockSpec(memory_space=pltpu.SMEM)] + [vmem] * 5,
        out_specs=vmem,
        scratch_shapes=[pltpu.VMEM(x.shape, bf16)],
        compiler_params=pltpu.CompilerParams(vmem_limit_bytes=10 << 20),
        name="project",
    )(core, x, gain, query, first, second)


def attention_kernel(
    scalars, parent, cosine, sine, p0, p1, p2, p3, c0, c1, c2, c3,
    o0, o1, o2, o3, query_rows, key_rows, value_rows, bias, scores, stats, joined,
):
    length = scalars[0]
    q_index = scalars[1]
    x_index = scalars[2]
    features, total = p0.shape
    span = query_rows.shape[0]
    share = span // SIDE
    half = HEAD_WIDTH // SIDE
    for d, piece in enumerate((p0, p1, p2, p3)):
        source = q_index ^ d
        query_rows[pl.ds(pl.multiple_of(source * share, half), share), :] = piece[:share, :]
        key_rows[pl.ds(pl.multiple_of(source * half, half), half), :] = piece[
            share : share + half, :
        ]
        value_rows[pl.ds(pl.multiple_of(source * half, half), half), :] = piece[
            share + half :, :
        ]
    cos = cosine[...]
    sin = sine[...]
    new_keys = rotated(key_rows[...], cos, sin).T.astype(bf16)
    new_values = value_rows[...]
    caches = (c0, c1, c2, c3)
    held = c0.shape[0]
    line = lax.broadcasted_iota(jnp.int32, (held, total), 0)
    spread = line + (line // PAGE) * (SIDE * SIDE - 1) * PAGE
    for d in range(SIDE):
        column = (x_index ^ d) * SIDE + q_index
        bias[d * held : (d + 1) * held, :] = jnp.where(
            spread + column * PAGE < length, 0.0, masked_floor
        )
    key_id = lax.broadcasted_iota(jnp.int32, (total, total), 0)
    row_id = lax.broadcasted_iota(jnp.int32, (total, total), 1)
    near = ((key_id == row_id) | (key_id == parent[...])) & (
        key_id // (total // SIDE) == q_index
    )
    bias[SIDE * held :, :] = jnp.where(near, 0.0, masked_floor)
    stats[...] = jnp.zeros(stats.shape, f32)
    scale = HEAD_WIDTH ** (-0.5)
    heads_here = span // HEAD_WIDTH
    for h in range(heads_here):
        query = rotated(
            query_rows[h * HEAD_WIDTH : (h + 1) * HEAD_WIDTH, :], cos, sin
        ).astype(bf16)
        for d, cache in enumerate(caches):
            scores[d * held : (d + 1) * held, :] = (
                dot(cache[:, :HEAD_WIDTH], query) * scale
                + bias[d * held : (d + 1) * held, :]
            )
        scores[SIDE * held :, :] = dot(new_keys, query) * scale + bias[SIDE * held :, :]
        peak = jnp.max(scores[...], axis=0, keepdims=True)
        mass = jnp.zeros((1, total), f32)
        weighted = jnp.zeros((HEAD_WIDTH, total), f32)
        for d, cache in enumerate(caches):
            raised = jnp.exp(scores[d * held : (d + 1) * held, :] - peak)
            mass = mass + jnp.sum(raised, axis=0, keepdims=True)
            weighted = weighted + across(cache[:, HEAD_WIDTH:], raised.astype(bf16))
        raised = jnp.exp(scores[SIDE * held :, :] - peak)
        mass = mass + jnp.sum(raised, axis=0, keepdims=True)
        weighted = weighted + dot(new_values, raised.astype(bf16))
        joined[:, h * HEAD_WIDTH : (h + 1) * HEAD_WIDTH] = (weighted / mass).T.astype(bf16)
        level = jnp.where(peak > 0.5 * masked_floor, peak + jnp.log(mass), masked_floor)
        for i, part in enumerate(three_parts(level)):
            place = i * heads_here + h
            stats[place : place + 1, :] = part.astype(f32)
    joined[:, span:] = stats[...].T.astype(bf16)
    subset = total // SIDE
    for d, out in enumerate((o0, o1, o2, o3)):
        out[...] = joined[pl.ds(pl.multiple_of((q_index ^ d) * subset, subset), subset), :]


def attend(scalars, parent, cosine, sine, pieces, caches):
    total = pieces[0].shape[1]
    subset = total // SIDE
    span = QUERY_HEADS // KEY_VALUE_HEADS * HEAD_WIDTH
    keys = SIDE * caches[0].shape[0] + total
    vmem = pl.BlockSpec(memory_space=pltpu.VMEM)
    return pl.pallas_call(
        attention_kernel,
        out_shape=[jax.ShapeDtypeStruct((subset, span + HEAD_WIDTH), bf16)] * SIDE,
        in_specs=[pl.BlockSpec(memory_space=pltpu.SMEM)] + [vmem] * (3 + 2 * SIDE),
        out_specs=[vmem] * SIDE,
        scratch_shapes=[
            pltpu.VMEM((span, total), bf16),
            pltpu.VMEM((HEAD_WIDTH, total), bf16),
            pltpu.VMEM((HEAD_WIDTH, total), bf16),
            pltpu.VMEM((keys, total), f32),
            pltpu.VMEM((keys, total), f32),
            pltpu.VMEM((HEAD_WIDTH, total), f32),
            pltpu.VMEM((total, span + HEAD_WIDTH), bf16),
        ],
        compiler_params=pltpu.CompilerParams(vmem_limit_bytes=12 << 20),
        name="attention",
    )(scalars, parent, cosine, sine, *pieces, *caches)


def output_kernel(x_index, h0, h1, h2, h3, weights, residual, out, blocks, sems):
    rows, span = h0.shape
    copies = []
    for d in range(SIDE):
        place = pl.multiple_of((x_index[0] ^ d) * span, span)
        copies.append(
            pltpu.make_async_copy(
                weights.at[:, pl.ds(place, span)], blocks.at[d], sems.at[d]
            )
        )
        copies[-1].start()
    acc = residual[...].astype(f32)
    for d, h in enumerate((h0, h1, h2, h3)):
        copies[d].wait()
        acc = acc + lax.dot_general(
            h[...],
            blocks[d],
            (((1,), (1,)), ((), ())),
            preferred_element_type=f32,
        )
    attended = acc.astype(bf16)
    part = rows // 2
    for j in range(out.shape[0]):
        t = j % 2
        out[j] = attended[t * part : (t + 1) * part, :]


def output_rows(x_index, heads, weights, residual, count):
    rows, span = residual.shape
    vmem = pl.BlockSpec(memory_space=pltpu.VMEM)
    return pl.pallas_call(
        output_kernel,
        out_shape=jax.ShapeDtypeStruct((count, rows // 2, span), bf16),
        in_specs=[pl.BlockSpec(memory_space=pltpu.SMEM)]
        + [vmem] * SIDE
        + [pl.BlockSpec(memory_space=pltpu.HBM), vmem],
        out_specs=vmem,
        scratch_shapes=[
            pltpu.VMEM((SIDE, span, span), bf16),
            pltpu.SemaphoreType.DMA((SIDE,)),
        ],
        compiler_params=pltpu.CompilerParams(vmem_limit_bytes=16 << 20),
        name="output",
    )(
        x_index, *heads, pltpu.with_memory_space_constraint(weights, pltpu.HBM), residual
    )


def spread_kernel(pieces, gain, dispatch, attended, normed, sent):
    count, part, span = pieces.shape
    for x in range(count // SIDE):
        for q in range(SIDE):
            attended[q * part : (q + 1) * part, x * span : (x + 1) * span] = pieces[
                SIDE * x + q
            ]
    normed[...] = norm_rows(attended[...], gain[...], 1)
    sent[...] = dot(dispatch[...], normed[...]).astype(bf16)


def spread(pieces, gain, dispatch):
    count, part, span = pieces.shape
    width = count // SIDE * span
    vmem = pl.BlockSpec(memory_space=pltpu.VMEM)
    return pl.pallas_call(
        spread_kernel,
        out_shape=[
            jax.ShapeDtypeStruct((SIDE * part, width), bf16),
            jax.ShapeDtypeStruct((SIDE * part, width), bf16),
            jax.ShapeDtypeStruct((dispatch.shape[0], width), bf16),
        ],
        in_specs=[vmem] * 3,
        out_specs=[vmem] * 3,
        name="spread",
    )(pieces, gain, dispatch)


def expert_kernel(
    expert, rows, router, named, g0, u0, d0, g1, u1, d1, out,
    gate_w, up_w, down_w, result, sems, out_sems,
):
    copies = []
    for i, (g, u, d) in enumerate(((g0, u0, d0), (g1, u1, d1))):
        copies.append(
            [
                pltpu.make_async_copy(src, dst.at[i], sems.at[3 * i + k])
                for k, (src, dst) in enumerate(((g, gate_w), (u, up_w), (d, down_w)))
            ]
        )
    order = [(0, 0), (0, 1), (1, 0), (1, 1), (0, 2), (1, 2)]
    for i, k in order:
        copies[i][k].start()
    width = down_w.shape[2]
    logits = lax.dot_general(
        rows[...], router[...], (((1,), (1,)), ((), ())), preferred_element_type=f32
    )
    raised = jnp.where(named[...] > 0.0, jnp.exp(logits), 0.0)
    column = lax.broadcasted_iota(jnp.int32, raised.shape, 1)
    total = jnp.sum(raised, axis=1, keepdims=True)
    picked = jnp.sum(jnp.where(column == expert[0], raised, 0.0), axis=1, keepdims=True)
    weight = picked / jnp.where(total > 0.0, total, 1.0)
    hidden = []
    for i in (0, 1):
        copies[i][0].wait()
        gated = dot(rows[...], gate_w[i])
        copies[i][1].wait()
        lifted = dot(rows[...], up_w[i])
        hidden.append((gated / (1.0 + jnp.exp(-gated)) * lifted).astype(bf16))
    copies[0][2].wait()
    copies[1][2].wait()
    step = width // out_sems.shape[0]
    stores = []
    for n in range(width // step):
        part = dot(hidden[0], down_w[0, :, n * step : (n + 1) * step]) + dot(
            hidden[1], down_w[1, :, n * step : (n + 1) * step]
        )
        span = slice(n * step, (n + 1) * step)
        result[span, :] = (part * weight).T.astype(bf16)
        stores.append(
            pltpu.make_async_copy(result.at[span, :], out.at[span, :], out_sems.at[n])
        )
        stores[-1].start()
    for store in stores:
        store.wait()


def expert_rows(expert, rows, router, named, blocks):
    count, width = rows.shape
    units = blocks[0].shape[1]
    vmem = pl.BlockSpec(memory_space=pltpu.VMEM)
    hbm = pl.BlockSpec(memory_space=pltpu.HBM)
    return pl.pallas_call(
        expert_kernel,
        out_shape=jax.ShapeDtypeStruct((width, count), bf16),
        in_specs=[pl.BlockSpec(memory_space=pltpu.SMEM)] + [vmem] * 3 + [hbm] * 6,
        out_specs=hbm,
        scratch_shapes=[
            pltpu.VMEM((2, width, units), bf16),
            pltpu.VMEM((2, width, units), bf16),
            pltpu.VMEM((2, units, width), bf16),
            pltpu.VMEM((width, count), bf16),
            pltpu.SemaphoreType.DMA((6,)),
            pltpu.SemaphoreType.DMA((5,)),
        ],
        compiler_params=pltpu.CompilerParams(vmem_limit_bytes=28 << 20),
        name="experts",
    )(
        expert,
        rows,
        router,
        named,
        *[pltpu.with_memory_space_constraint(b, pltpu.HBM) for b in blocks],
    )


def collect_kernel(slot, returned, codes, own, out, sums):
    groups, width, count = returned.shape
    slots, _, total = out.shape
    rows = total // 2
    lines = lax.broadcasted_iota(jnp.int32, (count, slots * rows), 0)
    by_step = []
    for c in (0, 1):
        acc = jnp.zeros((2 * width, slots * rows), f32)
        for x in range(SIDE):
            pick = jnp.where(
                lines == codes[2 * x + c : 2 * x + c + 1, :], 1.0, 0.0
            ).astype(bf16)
            pair = jnp.concatenate(
                [returned[SIDE * x + c], returned[SIDE * x + 2 + c]], axis=0
            )
            acc = acc + dot(pair, pick)
        by_step.append(acc[:width] + acc[width:])
    lane = lax.broadcasted_iota(jnp.int32, (width, total), 1)
    for pair in range(slots // 2):
        a = by_step[0][:, pair * total : (pair + 1) * total]
        b = by_step[1][:, pair * total : (pair + 1) * total]
        sums[2 * pair] = jnp.where(lane < rows, a, pltpu.roll(b, rows, 1))
        sums[2 * pair + 1] = jnp.where(lane < rows, pltpu.roll(a, rows, 1), b)
    sums[slot[0]] = sums[slot[0]] + own[...]
    out[...] = sums[...].astype(bf16)


def collect(slot, returned, codes, own):
    groups, width, _ = returned.shape
    shape = (groups, width, own.shape[1])
    vmem = pl.BlockSpec(memory_space=pltpu.VMEM)
    return pl.pallas_call(
        collect_kernel,
        out_shape=jax.ShapeDtypeStruct(shape, bf16),
        in_specs=[pl.BlockSpec(memory_space=pltpu.SMEM)] + [vmem] * 3,
        out_specs=vmem,
        scratch_shapes=[pltpu.VMEM(shape, f32)],
        compiler_params=pltpu.CompilerParams(vmem_limit_bytes=16 << 20),
        name="collect",
    )(slot, returned, codes, own)


def ranks_of(named):
    rows = named.shape[-2]
    lower = (
        jnp.arange(rows, dtype=jnp.int32)[:, None] > jnp.arange(rows, dtype=jnp.int32)[None, :]
    ).astype(bf16)
    return jnp.einsum("ij,...je->...ie", lower, named.astype(bf16), preferred_element_type=f32)


def per_device(
    step_inputs,
    attention_gain,
    query_weight,
    key_value_weight,
    output_weight,
    prompt_cache,
    page_table,
    cache_lengths,
    migration,
    parents,
    routes,
    feedforward_gain,
    router_weight,
    expert_gate,
    expert_up,
    expert_down,
    shared_gate,
    shared_up,
    shared_down,
):
    req_count = lax.axis_size("req")
    blk_count = lax.axis_size("blk")
    req_index = lax.axis_index("req")
    blk_index = lax.axis_index("blk")
    x_index = blk_index // SIDE
    q_index = blk_index % SIDE
    core = blk_index % 2
    steps, rows, width_local = step_inputs.shape
    total = steps * rows
    width = width_local * blk_count
    heads_here = QUERY_HEADS // KEY_VALUE_HEADS
    span = heads_here * HEAD_WIDTH
    subset = total // SIDE

    payload = payloads(
        req_count,
        step_inputs.reshape(total, width_local),
        routes.transpose(2, 0, 1),
        parents,
    )
    prompt, payload = lax.optimization_barrier((prompt_cache[0], payload))
    by_slot = lax.all_to_all(payload, "req", 0, 0, tiled=True)
    slot = migration[req_index]
    mine = lax.dynamic_index_in_dim(by_slot, slot, 0, False)
    part = rows // SIDE
    routes_all = (
        by_slot[:, width_local : width_local + TOPK]
        .astype(jnp.int32)
        .reshape(req_count, TOPK, SIDE, steps, part)
        .transpose(0, 1, 3, 2, 4)
        .reshape(req_count, TOPK, total)
    )
    routes_mine = lax.dynamic_index_in_dim(routes_all, slot, 0, False).T
    beam_mine = mine[width_local + TOPK].astype(jnp.int32)
    inputs = to_all(mine[:width_local], "blk").reshape(width, total)

    output_columns = lax.all_gather(
        output_weight, "blk", axis=1, tiled=True, axis_index_groups=QUAD
    )

    order = lax.dynamic_index_in_dim(page_table, req_index, 0, False)[0]
    pages = prompt[order]
    pages_local = pages.shape[0]
    by_head = (
        pages.reshape(pages_local * PAGE, 2, KEY_VALUE_HEADS, HEAD_WIDTH)
        .transpose(2, 0, 1, 3)
        .reshape(KEY_VALUE_HEADS, pages_local * PAGE, 2 * HEAD_WIDTH)
    )
    key_value_weight, by_head = lax.optimization_barrier((key_value_weight, by_head))
    caches = group_parts(
        lambda d: lax.dynamic_index_in_dim(by_head, x_index ^ d, 0, False), SIDE
    )

    half = key_value_weight.shape[1] // 2
    turned = key_value_weight.T
    left, right = turned[:half], turned[half:]
    low_side = blk_index < blk_count // 2
    groups = blk_count // 2
    straight = [(d, 2 * d) for d in range(groups)] + [
        (groups + d, 2 * d + 1) for d in range(groups)
    ]
    crossed = [(d, 2 * d + 1) for d in range(groups)] + [
        (groups + d, 2 * d) for d in range(groups)
    ]
    first = lax.ppermute(jnp.where(low_side, left, right), "blk", straight)
    second = lax.ppermute(jnp.where(low_side, right, left), "blk", crossed)
    projected = project(
        core[None].astype(jnp.int32),
        inputs,
        attention_gain.reshape(-1, 128),
        query_weight.T,
        first,
        second,
    )
    length = cache_lengths[req_index]
    frequency = rope_base ** (
        -2.0 * jnp.arange(HEAD_WIDTH // 2, dtype=f32) / HEAD_WIDTH
    )
    position = length + jnp.arange(steps, dtype=jnp.int32)
    angles = position.astype(f32)[:, None] * frequency
    cosine = jnp.tile(jnp.repeat(jnp.cos(angles).T, part, axis=1), (1, SIDE))
    sine = jnp.tile(jnp.repeat(jnp.sin(angles).T, part, axis=1), (1, SIDE))

    line = jnp.arange(total, dtype=jnp.int32)
    parent = jnp.where(
        line // part % steps == 1,
        line // subset * subset + line % part // BEAMS * BEAMS + beam_mine,
        -1,
    )[None]
    parts = attend(
        jnp.stack([length, q_index, x_index]).astype(jnp.int32),
        parent,
        cosine,
        sine,
        group_parts(lambda d: projected, 1),
        caches,
    )
    met = jnp.stack(group_parts(lambda d: parts[d], 1))
    levels = sum(
        met[:, :, span + i * heads_here : span + (i + 1) * heads_here].astype(f32)
        for i in range(3)
    )
    shares = jnp.exp(levels - jnp.max(levels, axis=0, keepdims=True))
    shares = shares / jnp.sum(shares, axis=0, keepdims=True)
    heads = (
        jnp.sum(
            shares[..., None]
            * met[:, :, :span].reshape(SIDE, subset, heads_here, HEAD_WIDTH).astype(f32),
            axis=0,
        )
        .astype(bf16)
        .reshape(subset, span)
    )

    residual = lax.dynamic_slice(
        inputs, (x_index * span, q_index * subset), (span, subset)
    ).T
    to_core = output_rows(
        x_index[None].astype(jnp.int32),
        group_parts(lambda d: heads, SIDE),
        output_columns.T,
        residual,
        blk_count,
    )
    gate_here, up_here, down_here, to_core = lax.optimization_barrier(
        (expert_gate[0], expert_up[0], expert_down[0], to_core)
    )
    blocks = [gate_here, up_here, down_here]
    expert_blocks = blocks + [lax.ppermute(b, "blk", partners(1)) for b in blocks]
    attended_pieces = lax.all_to_all(to_core, "blk", 0, 0, tiled=True)

    per_req = E // req_count
    slot_ids = jnp.arange(req_count, dtype=jnp.int32)
    holder = jnp.sum(
        jnp.where(migration[None, :] == slot_ids[:, None], slot_ids[None, :], 0), axis=1
    )
    owned = jnp.arange(per_req, dtype=jnp.int32) + req_index * per_req
    named_all = jnp.any(
        routes_all.reshape(1, req_count, TOPK, steps, rows) == owned[:, None, None, None, None],
        axis=2,
    )
    before = (
        jnp.arange(rows, dtype=jnp.int32)[:, None] < jnp.arange(rows, dtype=jnp.int32)[None, :]
    ).astype(bf16)
    rank_all = dot(named_all.astype(bf16).reshape(-1, rows), before).reshape(named_all.shape)
    codes = (
        jnp.where(
            named_all,
            holder[None, :, None, None] * CAP + rank_all.astype(jnp.int32),
            -1,
        )
        .transpose(0, 2, 1, 3)
        .reshape(per_req * steps, req_count * rows)
    )

    experts = jnp.arange(E, dtype=jnp.int32)
    code = lax.dynamic_index_in_dim(codes, x_index * steps + core, 0, False)
    slot_of = (
        code[None, :] == jnp.arange(req_count * CAP, dtype=jnp.int32)[:, None]
    ).astype(bf16)
    routes_step = lax.dynamic_slice_in_dim(routes_all, core * rows, rows, 2)
    named_rows = (
        jnp.any(routes_step.transpose(0, 2, 1)[..., None] == experts, axis=2)
        .astype(bf16)
        .reshape(req_count * rows, E)
    )
    named_slots = dot(slot_of, named_rows)

    def of_step(a):
        return lax.dynamic_slice_in_dim(a, core * rows, rows, 0)

    def of_expert(a):
        return lax.dynamic_index_in_dim(a.reshape(rows, req_count, per_req), x_index, 2, False).T

    named_step = jnp.any(of_step(routes_mine)[:, :, None] == experts, axis=1)
    rank_step = of_expert(ranks_of(named_step))
    named_here = of_expert(named_step.astype(f32)) > 0.0
    slots = jnp.arange(CAP, dtype=f32)
    dispatch = (
        (named_here[:, None, :] & (rank_step[:, None, :] == slots[None, :, None]))
        .reshape(req_count * CAP, rows)
        .astype(bf16)
    )
    attended, normed_h, sent = spread(attended_pieces, feedforward_gain[None], dispatch)
    arrived = lax.all_to_all(
        sent.reshape(req_count, CAP, width), "req", 0, 0, tiled=True
    ).reshape(req_count * CAP, width)

    other = lax.ppermute(normed_h, "blk", partners(1))
    act = [
        (jax.nn.silu(dot(h, shared_gate)) * dot(h, shared_up)).astype(bf16)
        for h in (normed_h, other)
    ]

    def by_step(here, there):
        return jnp.concatenate(
            [jnp.where(core == 0, here, there), jnp.where(core == 0, there, here)], axis=0
        )

    act = by_step(*act)
    shared_part = lax.dot_general(
        shared_down, act, (((0,), (1,)), ((), ())), preferred_element_type=f32
    ).astype(bf16)
    q_high = q_index // 2
    halves = shared_part.reshape(SIDE, 2, 2, width_local, total)
    pair = (
        lax.dynamic_index_in_dim(halves, core, 2, False).astype(f32)
        + lax.ppermute(
            lax.dynamic_index_in_dim(halves, 1 - core, 2, False), "blk", partners(1)
        ).astype(f32)
    ).astype(bf16)
    over_x = sum(
        p.astype(f32)
        for p in group_parts(
            lambda d: lax.dynamic_index_in_dim(pair, x_index ^ d, 0, False), SIDE
        )
    )
    shared = lax.dynamic_index_in_dim(over_x, q_high, 0, False) + lax.ppermute(
        lax.dynamic_index_in_dim(over_x, 1 - q_high, 0, False).astype(bf16),
        "blk",
        partners(2),
    ).astype(f32)

    def columns_of(b):
        return lax.dynamic_slice_in_dim(attended, b * width_local, width_local, 1)

    own = (
        by_step(
            columns_of(blk_index),
            lax.ppermute(columns_of(blk_index ^ 1), "blk", partners(1)),
        ).T.astype(f32)
        + shared
    )
    arrived, _ = lax.optimization_barrier((arrived, over_x))

    returned = lax.all_to_all(
        expert_rows(
            (req_index * per_req + x_index)[None].astype(jnp.int32),
            arrived,
            router_weight.T,
            named_slots,
            expert_blocks,
        ).reshape(blk_count, width_local, req_count * CAP),
        "blk",
        0,
        0,
        tiled=True,
    )

    outgoing = collect(slot[None], returned, codes, own)
    final = lax.all_to_all(outgoing, "req", 0, 0, tiled=True)
    return (
        jnp.sum(final.astype(f32), axis=0).T.astype(bf16).reshape(steps, rows, width_local)
    )


def solution(mesh):
    in_specs = (
        P(None, "req", "blk"),
        P(),
        P(None, "blk"),
        P(None, "blk"),
        P(None, "blk"),
        P("req", "blk", None, None),
        P(None, "blk", None),
        P(),
        P(),
        P(None, "req"),
        P(None, "req", None),
        P(),
        P(),
        P(("req", "blk"), None, None),
        P(("req", "blk"), None, None),
        P(("req", "blk"), None, None),
        P(None, "blk"),
        P(None, "blk"),
        P("blk", None),
    )
    out_specs = P(None, "req", "blk")
    return jax.shard_map(
        per_device, mesh=mesh, in_specs=in_specs, out_specs=out_specs, check_vma=False
    )
```

```python
import jax
import jax.numpy as jnp
from jax import lax
from jax.experimental import pallas as pl
from jax.experimental.pallas import tpu as pltpu
from jax.sharding import PartitionSpec as P

QUERY_HEADS = 20
KEY_VALUE_HEADS = 4
HEAD_WIDTH = 128
E = 64
TOPK = 6
BEAMS = 8
CAP = 16
PAGE = 128

epsilon = 1e-05
rope_base = 500000.0
masked_floor = -1e30

bf16 = jnp.bfloat16
f32 = jnp.float32

SIDE = 4
QUAD = [[SIDE * i + k for k in range(SIDE)] for i in range(SIDE)]


def dot(a, b):
    return jnp.dot(a, b, preferred_element_type=f32)


def to_all(piece, axis):
    count = lax.axis_size(axis)
    copies = jnp.broadcast_to(piece[None], (count,) + piece.shape)
    return lax.all_to_all(copies, axis, 0, 0, tiled=True)


def partners(distance):
    return [(d, d ^ distance) for d in range(SIDE * SIDE)]


def group_parts(piece_for, stride):
    return [piece_for(0)] + [
        lax.ppermute(piece_for(d), "blk", partners(d * stride)) for d in range(1, SIDE)
    ]


def in_order(parts, index):
    odd = index % 2 == 1
    upper = index // 2 == 1
    a, b, c, d = parts
    a, b = jnp.where(odd, b, a), jnp.where(odd, a, b)
    c, d = jnp.where(odd, d, c), jnp.where(odd, c, d)
    return [
        jnp.where(upper, c, a),
        jnp.where(upper, d, b),
        jnp.where(upper, a, c),
        jnp.where(upper, b, d),
    ]


def norm_rows(rows, gain, axis):
    wide = rows.astype(f32)
    inverse = lax.rsqrt(jnp.mean(wide * wide, axis=axis, keepdims=True) + epsilon)
    return (wide * inverse * gain).astype(bf16)


def three_parts(value):
    high = value.astype(bf16)
    rest = value - high.astype(f32)
    middle = rest.astype(bf16)
    low = (rest - middle.astype(f32)).astype(bf16)
    return high, middle, low


def rotated(vectors, cosine, sine):
    half = vectors.shape[0] // 2
    a = vectors[:half].astype(f32)
    b = vectors[half:].astype(f32)
    return jnp.concatenate([a * cosine - b * sine, b * cosine + a * sine], axis=0)


def across(a, b):
    return lax.dot_general(a, b, (((0,), (0,)), ((), ())), preferred_element_type=f32)


def payload_kernel(x, routes, beams, out, lines):
    total, width = x.shape
    rows = total // 2
    part = rows // SIDE
    main = width // 128 * 128
    ordered = jnp.concatenate(
        [
            x[t * rows + q * part : t * rows + (q + 1) * part, :]
            for q in range(SIDE)
            for t in (0, 1)
        ],
        axis=0,
    ).astype(f32)
    lines[:main, :] = ordered[:, :main].T.astype(bf16)
    rest = jnp.concatenate(
        [ordered[:, main:], jnp.zeros((total, 128 - width + main), f32)], axis=1
    )
    lines[main:width, :] = rest.T[: width - main].astype(bf16)
    none = jnp.zeros((1, rows), jnp.int32)
    by_step = [
        jnp.concatenate([routes[k, t : t + 1, :] for k in range(TOPK)] + [last, none], axis=0)
        for t, last in ((0, none), (1, beams[...]))
    ]
    extra = jnp.concatenate(
        [
            by_step[t][:, q * part : (q + 1) * part]
            for q in range(SIDE)
            for t in (0, 1)
        ],
        axis=1,
    )
    lines[width:, :] = extra.astype(f32).astype(bf16)
    for i in range(out.shape[0]):
        out[i] = lines[...]


def payloads(count, x, routes, beams):
    total, width = x.shape
    vmem = pl.BlockSpec(memory_space=pltpu.VMEM)
    return pl.pallas_call(
        payload_kernel,
        out_shape=jax.ShapeDtypeStruct((count, width + TOPK + 2, total), bf16),
        in_specs=[vmem] * 3,
        out_specs=vmem,
        scratch_shapes=[pltpu.VMEM((width + TOPK + 2, total), bf16)],
        name="payload",
    )(x, routes, beams)


def project_kernel(core, x, gain, query, first, second, out, normed):
    width = x.shape[0]
    wide = x[...].astype(f32)
    inverse = lax.rsqrt(jnp.sum(wide * wide, axis=0, keepdims=True) / width + epsilon)
    gains = gain[...].T
    for i in range(width // 128):
        rows = slice(i * 128, (i + 1) * 128)
        normed[rows, :] = (
            x[rows, :].astype(f32) * inverse * gains[:, i : i + 1]
        ).astype(bf16)
    share = query.shape[0]
    half = first.shape[0]
    out[:share, :] = dot(query[...], normed[...]).astype(bf16)
    a = dot(first[...], normed[...])
    b = dot(second[...], normed[...])
    even = core[0] == 0
    out[share : share + half, :] = jnp.where(even, a, b).astype(bf16)
    out[share + half :, :] = jnp.where(even, b, a).astype(bf16)


def project(core, x, gain, query, first, second):
    vmem = pl.BlockSpec(memory_space=pltpu.VMEM)
    share = query.shape[0] + 2 * first.shape[0]
    return pl.pallas_call(
        project_kernel,
        out_shape=jax.ShapeDtypeStruct((share, x.shape[1]), bf16),
        in_specs=[pl.BlockSpec(memory_space=pltpu.SMEM)] + [vmem] * 5,
        out_specs=vmem,
        scratch_shapes=[pltpu.VMEM(x.shape, bf16)],
        compiler_params=pltpu.CompilerParams(vmem_limit_bytes=10 << 20),
        name="project",
    )(core, x, gain, query, first, second)


def attention_kernel(
    scalars, parent, cosine, sine, p0, p1, p2, p3, c0, c1, c2, c3,
    o0, o1, o2, o3, query_rows, key_rows, value_rows, bias, scores, stats, joined,
):
    length = scalars[0]
    q_index = scalars[1]
    x_index = scalars[2]
    features, total = p0.shape
    span = query_rows.shape[0]
    share = span // SIDE
    half = HEAD_WIDTH // SIDE
    for d, piece in enumerate((p0, p1, p2, p3)):
        source = q_index ^ d
        query_rows[pl.ds(pl.multiple_of(source * share, half), share), :] = piece[:share, :]
        key_rows[pl.ds(pl.multiple_of(source * half, half), half), :] = piece[
            share : share + half, :
        ]
        value_rows[pl.ds(pl.multiple_of(source * half, half), half), :] = piece[
            share + half :, :
        ]
    cos = cosine[...]
    sin = sine[...]
    new_keys = rotated(key_rows[...], cos, sin).T.astype(bf16)
    new_values = value_rows[...]
    caches = (c0, c1, c2, c3)
    held = c0.shape[0]
    line = lax.broadcasted_iota(jnp.int32, (held, total), 0)
    spread = line + (line // PAGE) * (SIDE * SIDE - 1) * PAGE
    for d in range(SIDE):
        column = (x_index ^ d) * SIDE + q_index
        bias[d * held : (d + 1) * held, :] = jnp.where(
            spread + column * PAGE < length, 0.0, masked_floor
        )
    key_id = lax.broadcasted_iota(jnp.int32, (total, total), 0)
    row_id = lax.broadcasted_iota(jnp.int32, (total, total), 1)
    near = ((key_id == row_id) | (key_id == parent[...])) & (
        key_id // (total // SIDE) == q_index
    )
    bias[SIDE * held :, :] = jnp.where(near, 0.0, masked_floor)
    stats[...] = jnp.zeros(stats.shape, f32)
    scale = HEAD_WIDTH ** (-0.5)
    heads_here = span // HEAD_WIDTH
    for h in range(heads_here):
        query = rotated(
            query_rows[h * HEAD_WIDTH : (h + 1) * HEAD_WIDTH, :], cos, sin
        ).astype(bf16)
        for d, cache in enumerate(caches):
            scores[d * held : (d + 1) * held, :] = (
                dot(cache[:, :HEAD_WIDTH], query) * scale
                + bias[d * held : (d + 1) * held, :]
            )
        scores[SIDE * held :, :] = dot(new_keys, query) * scale + bias[SIDE * held :, :]
        peak = jnp.max(scores[...], axis=0, keepdims=True)
        mass = jnp.zeros((1, total), f32)
        weighted = jnp.zeros((HEAD_WIDTH, total), f32)
        for d, cache in enumerate(caches):
            raised = jnp.exp(scores[d * held : (d + 1) * held, :] - peak)
            mass = mass + jnp.sum(raised, axis=0, keepdims=True)
            weighted = weighted + across(cache[:, HEAD_WIDTH:], raised.astype(bf16))
        raised = jnp.exp(scores[SIDE * held :, :] - peak)
        mass = mass + jnp.sum(raised, axis=0, keepdims=True)
        weighted = weighted + dot(new_values, raised.astype(bf16))
        joined[:, h * HEAD_WIDTH : (h + 1) * HEAD_WIDTH] = (weighted / mass).T.astype(bf16)
        level = jnp.where(peak > 0.5 * masked_floor, peak + jnp.log(mass), masked_floor)
        for i, part in enumerate(three_parts(level)):
            place = i * heads_here + h
            stats[place : place + 1, :] = part.astype(f32)
    joined[:, span:] = stats[...].T.astype(bf16)
    subset = total // SIDE
    for d, out in enumerate((o0, o1, o2, o3)):
        out[...] = joined[pl.ds(pl.multiple_of((q_index ^ d) * subset, subset), subset), :]


def attend(scalars, parent, cosine, sine, pieces, caches):
    total = pieces[0].shape[1]
    subset = total // SIDE
    span = QUERY_HEADS // KEY_VALUE_HEADS * HEAD_WIDTH
    keys = SIDE * caches[0].shape[0] + total
    vmem = pl.BlockSpec(memory_space=pltpu.VMEM)
    return pl.pallas_call(
        attention_kernel,
        out_shape=[jax.ShapeDtypeStruct((subset, span + HEAD_WIDTH), bf16)] * SIDE,
        in_specs=[pl.BlockSpec(memory_space=pltpu.SMEM)] + [vmem] * (3 + 2 * SIDE),
        out_specs=[vmem] * SIDE,
        scratch_shapes=[
            pltpu.VMEM((span, total), bf16),
            pltpu.VMEM((HEAD_WIDTH, total), bf16),
            pltpu.VMEM((HEAD_WIDTH, total), bf16),
            pltpu.VMEM((keys, total), f32),
            pltpu.VMEM((keys, total), f32),
            pltpu.VMEM((HEAD_WIDTH, total), f32),
            pltpu.VMEM((total, span + HEAD_WIDTH), bf16),
        ],
        compiler_params=pltpu.CompilerParams(vmem_limit_bytes=12 << 20),
        name="attention",
    )(scalars, parent, cosine, sine, *pieces, *caches)


def output_kernel(x_index, h0, h1, h2, h3, weights, residual, out, blocks, sems):
    rows, span = h0.shape
    copies = []
    for d in range(SIDE):
        place = pl.multiple_of((x_index[0] ^ d) * span, span)
        copies.append(
            pltpu.make_async_copy(
                weights.at[:, pl.ds(place, span)], blocks.at[d], sems.at[d]
            )
        )
        copies[-1].start()
    acc = residual[...].astype(f32)
    for d, h in enumerate((h0, h1, h2, h3)):
        copies[d].wait()
        acc = acc + lax.dot_general(
            h[...],
            blocks[d],
            (((1,), (1,)), ((), ())),
            preferred_element_type=f32,
        )
    attended = acc.astype(bf16)
    part = rows // 2
    for j in range(out.shape[0]):
        t = j % 2
        out[j] = attended[t * part : (t + 1) * part, :]


def output_rows(x_index, heads, weights, residual, count):
    rows, span = residual.shape
    vmem = pl.BlockSpec(memory_space=pltpu.VMEM)
    return pl.pallas_call(
        output_kernel,
        out_shape=jax.ShapeDtypeStruct((count, rows // 2, span), bf16),
        in_specs=[pl.BlockSpec(memory_space=pltpu.SMEM)]
        + [vmem] * SIDE
        + [pl.BlockSpec(memory_space=pltpu.HBM), vmem],
        out_specs=vmem,
        scratch_shapes=[
            pltpu.VMEM((SIDE, span, span), bf16),
            pltpu.SemaphoreType.DMA((SIDE,)),
        ],
        compiler_params=pltpu.CompilerParams(vmem_limit_bytes=16 << 20),
        name="output",
    )(
        x_index, *heads, pltpu.with_memory_space_constraint(weights, pltpu.HBM), residual
    )


def spread_kernel(pieces, gain, dispatch, attended, normed, sent):
    count, part, span = pieces.shape
    for x in range(count // SIDE):
        for q in range(SIDE):
            attended[q * part : (q + 1) * part, x * span : (x + 1) * span] = pieces[
                SIDE * x + q
            ]
    normed[...] = norm_rows(attended[...], gain[...], 1)
    sent[...] = dot(dispatch[...], normed[...]).astype(bf16)


def spread(pieces, gain, dispatch):
    count, part, span = pieces.shape
    width = count // SIDE * span
    vmem = pl.BlockSpec(memory_space=pltpu.VMEM)
    return pl.pallas_call(
        spread_kernel,
        out_shape=[
            jax.ShapeDtypeStruct((SIDE * part, width), bf16),
            jax.ShapeDtypeStruct((SIDE * part, width), bf16),
            jax.ShapeDtypeStruct((dispatch.shape[0], width), bf16),
        ],
        in_specs=[vmem] * 3,
        out_specs=[vmem] * 3,
        name="spread",
    )(pieces, gain, dispatch)


def expert_kernel(
    expert, rows, router, named, g0, u0, d0, g1, u1, d1, out,
    gate_w, up_w, down_w, result, sems, out_sems,
):
    copies = []
    for i, (g, u, d) in enumerate(((g0, u0, d0), (g1, u1, d1))):
        copies.append(
            [
                pltpu.make_async_copy(src, dst.at[i], sems.at[3 * i + k])
                for k, (src, dst) in enumerate(((g, gate_w), (u, up_w), (d, down_w)))
            ]
        )
    order = [(0, 0), (0, 1), (1, 0), (1, 1), (0, 2), (1, 2)]
    for i, k in order:
        copies[i][k].start()
    width = down_w.shape[2]
    logits = lax.dot_general(
        rows[...], router[...], (((1,), (1,)), ((), ())), preferred_element_type=f32
    )
    raised = jnp.where(named[...] > 0.0, jnp.exp(logits), 0.0)
    column = lax.broadcasted_iota(jnp.int32, raised.shape, 1)
    total = jnp.sum(raised, axis=1, keepdims=True)
    picked = jnp.sum(jnp.where(column == expert[0], raised, 0.0), axis=1, keepdims=True)
    weight = picked / jnp.where(total > 0.0, total, 1.0)
    hidden = []
    for i in (0, 1):
        copies[i][0].wait()
        gated = dot(rows[...], gate_w[i])
        copies[i][1].wait()
        lifted = dot(rows[...], up_w[i])
        hidden.append((gated / (1.0 + jnp.exp(-gated)) * lifted).astype(bf16))
    copies[0][2].wait()
    copies[1][2].wait()
    step = width // out_sems.shape[0]
    stores = []
    for n in range(width // step):
        part = dot(hidden[0], down_w[0, :, n * step : (n + 1) * step]) + dot(
            hidden[1], down_w[1, :, n * step : (n + 1) * step]
        )
        span = slice(n * step, (n + 1) * step)
        result[span, :] = (part * weight).T.astype(bf16)
        stores.append(
            pltpu.make_async_copy(result.at[span, :], out.at[span, :], out_sems.at[n])
        )
        stores[-1].start()
    for store in stores:
        store.wait()


def expert_rows(expert, rows, router, named, blocks):
    count, width = rows.shape
    units = blocks[0].shape[1]
    vmem = pl.BlockSpec(memory_space=pltpu.VMEM)
    hbm = pl.BlockSpec(memory_space=pltpu.HBM)
    return pl.pallas_call(
        expert_kernel,
        out_shape=jax.ShapeDtypeStruct((width, count), bf16),
        in_specs=[pl.BlockSpec(memory_space=pltpu.SMEM)] + [vmem] * 3 + [hbm] * 6,
        out_specs=hbm,
        scratch_shapes=[
            pltpu.VMEM((2, width, units), bf16),
            pltpu.VMEM((2, width, units), bf16),
            pltpu.VMEM((2, units, width), bf16),
            pltpu.VMEM((width, count), bf16),
            pltpu.SemaphoreType.DMA((6,)),
            pltpu.SemaphoreType.DMA((5,)),
        ],
        compiler_params=pltpu.CompilerParams(vmem_limit_bytes=28 << 20),
        name="experts",
    )(
        expert,
        rows,
        router,
        named,
        *[pltpu.with_memory_space_constraint(b, pltpu.HBM) for b in blocks],
    )


def collect_kernel(slot, returned, codes, own, out, sums):
    groups, width, count = returned.shape
    slots, _, total = out.shape
    rows = total // 2
    lines = lax.broadcasted_iota(jnp.int32, (count, slots * rows), 0)
    by_step = []
    for c in (0, 1):
        acc = jnp.zeros((2 * width, slots * rows), f32)
        for x in range(SIDE):
            pick = jnp.where(
                lines == codes[2 * x + c : 2 * x + c + 1, :], 1.0, 0.0
            ).astype(bf16)
            pair = jnp.concatenate(
                [returned[SIDE * x + c], returned[SIDE * x + 2 + c]], axis=0
            )
            acc = acc + dot(pair, pick)
        by_step.append(acc[:width] + acc[width:])
    lane = lax.broadcasted_iota(jnp.int32, (width, total), 1)
    for pair in range(slots // 2):
        a = by_step[0][:, pair * total : (pair + 1) * total]
        b = by_step[1][:, pair * total : (pair + 1) * total]
        sums[2 * pair] = jnp.where(lane < rows, a, pltpu.roll(b, rows, 1))
        sums[2 * pair + 1] = jnp.where(lane < rows, pltpu.roll(a, rows, 1), b)
    sums[slot[0]] = sums[slot[0]] + own[...]
    out[...] = sums[...].astype(bf16)


def collect(slot, returned, codes, own):
    groups, width, _ = returned.shape
    shape = (groups, width, own.shape[1])
    vmem = pl.BlockSpec(memory_space=pltpu.VMEM)
    return pl.pallas_call(
        collect_kernel,
        out_shape=jax.ShapeDtypeStruct(shape, bf16),
        in_specs=[pl.BlockSpec(memory_space=pltpu.SMEM)] + [vmem] * 3,
        out_specs=vmem,
        scratch_shapes=[pltpu.VMEM(shape, f32)],
        compiler_params=pltpu.CompilerParams(vmem_limit_bytes=16 << 20),
        name="collect",
    )(slot, returned, codes, own)


def ranks_of(named):
    rows = named.shape[-2]
    lower = (
        jnp.arange(rows, dtype=jnp.int32)[:, None] > jnp.arange(rows, dtype=jnp.int32)[None, :]
    ).astype(bf16)
    return jnp.einsum("ij,...je->...ie", lower, named.astype(bf16), preferred_element_type=f32)


def per_device(
    step_inputs,
    attention_gain,
    query_weight,
    key_value_weight,
    output_weight,
    prompt_cache,
    page_table,
    cache_lengths,
    migration,
    parents,
    routes,
    feedforward_gain,
    router_weight,
    expert_gate,
    expert_up,
    expert_down,
    shared_gate,
    shared_up,
    shared_down,
):
    req_count = lax.axis_size("req")
    blk_count = lax.axis_size("blk")
    req_index = lax.axis_index("req")
    blk_index = lax.axis_index("blk")
    x_index = blk_index // SIDE
    q_index = blk_index % SIDE
    core = blk_index % 2
    steps, rows, width_local = step_inputs.shape
    total = steps * rows
    width = width_local * blk_count
    heads_here = QUERY_HEADS // KEY_VALUE_HEADS
    span = heads_here * HEAD_WIDTH
    subset = total // SIDE

    payload = payloads(
        req_count,
        step_inputs.reshape(total, width_local),
        routes.transpose(2, 0, 1),
        parents,
    )
    prompt, payload = lax.optimization_barrier((prompt_cache[0], payload))
    by_slot = lax.all_to_all(payload, "req", 0, 0, tiled=True)
    slot = migration[req_index]
    mine = lax.dynamic_index_in_dim(by_slot, slot, 0, False)
    part = rows // SIDE
    routes_all = (
        by_slot[:, width_local : width_local + TOPK]
        .astype(jnp.int32)
        .reshape(req_count, TOPK, SIDE, steps, part)
        .transpose(0, 1, 3, 2, 4)
        .reshape(req_count, TOPK, total)
    )
    routes_mine = lax.dynamic_index_in_dim(routes_all, slot, 0, False).T
    beam_mine = mine[width_local + TOPK].astype(jnp.int32)
    inputs = to_all(mine[:width_local], "blk").reshape(width, total)

    output_columns = lax.all_gather(
        output_weight, "blk", axis=1, tiled=True, axis_index_groups=QUAD
    )

    order = lax.dynamic_index_in_dim(page_table, req_index, 0, False)[0]
    pages = prompt[order]
    pages_local = pages.shape[0]
    by_head = (
        pages.reshape(pages_local * PAGE, 2, KEY_VALUE_HEADS, HEAD_WIDTH)
        .transpose(2, 0, 1, 3)
        .reshape(KEY_VALUE_HEADS, pages_local * PAGE, 2 * HEAD_WIDTH)
    )
    key_value_weight, by_head = lax.optimization_barrier((key_value_weight, by_head))
    caches = group_parts(
        lambda d: lax.dynamic_index_in_dim(by_head, x_index ^ d, 0, False), SIDE
    )

    half = key_value_weight.shape[1] // 2
    turned = key_value_weight.T
    left, right = turned[:half], turned[half:]
    low_side = blk_index < blk_count // 2
    groups = blk_count // 2
    straight = [(d, 2 * d) for d in range(groups)] + [
        (groups + d, 2 * d + 1) for d in range(groups)
    ]
    crossed = [(d, 2 * d + 1) for d in range(groups)] + [
        (groups + d, 2 * d) for d in range(groups)
    ]
    first = lax.ppermute(jnp.where(low_side, left, right), "blk", straight)
    second = lax.ppermute(jnp.where(low_side, right, left), "blk", crossed)
    projected = project(
        core[None].astype(jnp.int32),
        inputs,
        attention_gain.reshape(-1, 128),
        query_weight.T,
        first,
        second,
    )
    lengths, _ = lax.optimization_barrier((cache_lengths, by_slot))
    length = lengths[req_index]
    frequency = rope_base ** (
        -2.0 * jnp.arange(HEAD_WIDTH // 2, dtype=f32) / HEAD_WIDTH
    )
    position = length + jnp.arange(steps, dtype=jnp.int32)
    angles = position.astype(f32)[:, None] * frequency
    cosine = jnp.tile(jnp.repeat(jnp.cos(angles).T, part, axis=1), (1, SIDE))
    sine = jnp.tile(jnp.repeat(jnp.sin(angles).T, part, axis=1), (1, SIDE))

    line = jnp.arange(total, dtype=jnp.int32)
    parent = jnp.where(
        line // part % steps == 1,
        line // subset * subset + line % part // BEAMS * BEAMS + beam_mine,
        -1,
    )[None]
    parts = attend(
        jnp.stack([length, q_index, x_index]).astype(jnp.int32),
        parent,
        cosine,
        sine,
        group_parts(lambda d: projected, 1),
        caches,
    )
    migration_late, _ = lax.optimization_barrier((migration, parts[0]))
    met = jnp.stack(group_parts(lambda d: parts[d], 1))
    levels = sum(
        met[:, :, span + i * heads_here : span + (i + 1) * heads_here].astype(f32)
        for i in range(3)
    )
    shares = jnp.exp(levels - jnp.max(levels, axis=0, keepdims=True))
    shares = shares / jnp.sum(shares, axis=0, keepdims=True)
    heads = (
        jnp.sum(
            shares[..., None]
            * met[:, :, :span].reshape(SIDE, subset, heads_here, HEAD_WIDTH).astype(f32),
            axis=0,
        )
        .astype(bf16)
        .reshape(subset, span)
    )

    residual = lax.dynamic_slice(
        inputs, (x_index * span, q_index * subset), (span, subset)
    ).T
    to_core = output_rows(
        x_index[None].astype(jnp.int32),
        group_parts(lambda d: heads, SIDE),
        output_columns.T,
        residual,
        blk_count,
    )
    gate_here, up_here, down_here, to_core = lax.optimization_barrier(
        (expert_gate[0], expert_up[0], expert_down[0], to_core)
    )
    blocks = [gate_here, up_here, down_here]
    expert_blocks = blocks + [lax.ppermute(b, "blk", partners(1)) for b in blocks]
    attended_pieces = lax.all_to_all(to_core, "blk", 0, 0, tiled=True)

    per_req = E // req_count
    slot_ids = jnp.arange(req_count, dtype=jnp.int32)
    holder = jnp.sum(
        jnp.where(migration_late[None, :] == slot_ids[:, None], slot_ids[None, :], 0), axis=1
    )
    owned = jnp.arange(per_req, dtype=jnp.int32) + req_index * per_req
    named_all = jnp.any(
        routes_all.reshape(1, req_count, TOPK, steps, rows) == owned[:, None, None, None, None],
        axis=2,
    )
    before = (
        jnp.arange(rows, dtype=jnp.int32)[:, None] < jnp.arange(rows, dtype=jnp.int32)[None, :]
    ).astype(bf16)
    rank_all = dot(named_all.astype(bf16).reshape(-1, rows), before).reshape(named_all.shape)
    codes = (
        jnp.where(
            named_all,
            holder[None, :, None, None] * CAP + rank_all.astype(jnp.int32),
            -1,
        )
        .transpose(0, 2, 1, 3)
        .reshape(per_req * steps, req_count * rows)
    )

    experts = jnp.arange(E, dtype=jnp.int32)
    code = lax.dynamic_index_in_dim(codes, x_index * steps + core, 0, False)
    slot_of = (
        code[None, :] == jnp.arange(req_count * CAP, dtype=jnp.int32)[:, None]
    ).astype(bf16)
    routes_step = lax.dynamic_slice_in_dim(routes_all, core * rows, rows, 2)
    named_rows = (
        jnp.any(routes_step.transpose(0, 2, 1)[..., None] == experts, axis=2)
        .astype(bf16)
        .reshape(req_count * rows, E)
    )
    named_slots = dot(slot_of, named_rows)

    def of_step(a):
        return lax.dynamic_slice_in_dim(a, core * rows, rows, 0)

    def of_expert(a):
        return lax.dynamic_index_in_dim(a.reshape(rows, req_count, per_req), x_index, 2, False).T

    named_step = jnp.any(of_step(routes_mine)[:, :, None] == experts, axis=1)
    rank_step = of_expert(ranks_of(named_step))
    named_here = of_expert(named_step.astype(f32)) > 0.0
    slots = jnp.arange(CAP, dtype=f32)
    dispatch = (
        (named_here[:, None, :] & (rank_step[:, None, :] == slots[None, :, None]))
        .reshape(req_count * CAP, rows)
        .astype(bf16)
    )
    attended, normed_h, sent = spread(attended_pieces, feedforward_gain[None], dispatch)
    arrived = lax.all_to_all(
        sent.reshape(req_count, CAP, width), "req", 0, 0, tiled=True
    ).reshape(req_count * CAP, width)

    other = lax.ppermute(normed_h, "blk", partners(1))
    act = [
        (jax.nn.silu(dot(h, shared_gate)) * dot(h, shared_up)).astype(bf16)
        for h in (normed_h, other)
    ]

    def by_step(here, there):
        return jnp.concatenate(
            [jnp.where(core == 0, here, there), jnp.where(core == 0, there, here)], axis=0
        )

    act = by_step(*act)
    shared_part = lax.dot_general(
        shared_down, act, (((0,), (1,)), ((), ())), preferred_element_type=f32
    ).astype(bf16)
    q_high = q_index // 2
    halves = shared_part.reshape(SIDE, 2, 2, width_local, total)
    pair = (
        lax.dynamic_index_in_dim(halves, core, 2, False).astype(f32)
        + lax.ppermute(
            lax.dynamic_index_in_dim(halves, 1 - core, 2, False), "blk", partners(1)
        ).astype(f32)
    ).astype(bf16)
    over_x = sum(
        p.astype(f32)
        for p in group_parts(
            lambda d: lax.dynamic_index_in_dim(pair, x_index ^ d, 0, False), SIDE
        )
    )
    shared = lax.dynamic_index_in_dim(over_x, q_high, 0, False) + lax.ppermute(
        lax.dynamic_index_in_dim(over_x, 1 - q_high, 0, False).astype(bf16),
        "blk",
        partners(2),
    ).astype(f32)

    def columns_of(b):
        return lax.dynamic_slice_in_dim(attended, b * width_local, width_local, 1)

    own = (
        by_step(
            columns_of(blk_index),
            lax.ppermute(columns_of(blk_index ^ 1), "blk", partners(1)),
        ).T.astype(f32)
        + shared
    )
    arrived, _ = lax.optimization_barrier((arrived, over_x))

    returned = lax.all_to_all(
        expert_rows(
            (req_index * per_req + x_index)[None].astype(jnp.int32),
            arrived,
            router_weight.T,
            named_slots,
            expert_blocks,
        ).reshape(blk_count, width_local, req_count * CAP),
        "blk",
        0,
        0,
        tiled=True,
    )

    outgoing = collect(slot[None], returned, codes, own)
    final = lax.all_to_all(outgoing, "req", 0, 0, tiled=True)
    return (
        jnp.sum(final.astype(f32), axis=0).T.astype(bf16).reshape(steps, rows, width_local)
    )


def solution(mesh):
    in_specs = (
        P(None, "req", "blk"),
        P(),
        P(None, "blk"),
        P(None, "blk"),
        P(None, "blk"),
        P("req", "blk", None, None),
        P(None, "blk", None),
        P(),
        P(),
        P(None, "req"),
        P(None, "req", None),
        P(),
        P(),
        P(("req", "blk"), None, None),
        P(("req", "blk"), None, None),
        P(("req", "blk"), None, None),
        P(None, "blk"),
        P(None, "blk"),
        P("blk", None),
    )
    out_specs = P(None, "req", "blk")
    return jax.shard_map(
        per_device, mesh=mesh, in_specs=in_specs, out_specs=out_specs, check_vma=False
    )
```
